128 devices in a mesh: run: 2 (over core), row: 8 (over z_lo, x), col: 8 (over y, z_hi).
Axes of the slice: x: 4, y: 4, z: 4 (z_hi: 2, z_lo: 2; z = z_hi * 2 + z_lo), core: 2. Of those that a mesh axis runs over, the one named last changes fastest.
Arguments:
- init_field: float32 [96, 512, 1024], P('run', 'row', 'col'), may hold values from -6 to 6
- conduct: float32 [512, 1024], P('row', 'col'), may hold values from 0.5 to 2
- nonlin: float32 [96], P('run'), may hold values from 0.1 to 1
- counts: int32 [96], P('run'), may hold values from 1 to 8
- descriptors: bfloat16 [96, 256], replicated, may hold values from -6 to 6
- time_code: bfloat16 [8, 256], replicated, may hold values from -6 to 6
- w_in: bfloat16 [256, 512], replicated, may hold values from -0.375 to 0.375
- bias_in: float32 [512], replicated, may hold values from -6 to 6
- w_out: bfloat16 [512, 512], replicated, may hold values from -0.25 to 0.25
- decoder: bfloat16 [512, 512, 1024], P(None, ('row', 'col')), may hold values from -0.22 to 0.22
Outputs:
- final_field: float32 [96, 512, 1024], P('run', 'row', 'col')
- new_w_in: float32 [256, 512], replicated
- new_bias: float32 [512], replicated
- new_w_out: float32 [512, 512], replicated
- mean_loss: float32 [], replicated
The draws below stay inside these ranges and needn't reach their ends.
All inputs are finite; a program needn't handle non-finite values.
Results may differ from the reference program's by a relative error of at most 0.0017.
Values may be sent and summed in bfloat16 or wider, within the bound.
A program may use at most 128 MiB of HBM per device.

```python
import math
import jax
import jax.numpy as jnp
from jax import lax

P_SIZE = 256
H = 512
STEPS = 8
RUNS = 96
GRID_ROWS = 512
GRID_COLS = 1024


pattern_count = 8


def smooth_patterns(key):
    freq_key = jax.random.fold_in(key, 3)
    phase_key = jax.random.fold_in(key, 5)
    frequency = jax.random.randint(freq_key, (pattern_count, 2), 1, 4).astype(jnp.float32)
    phase_draw = jax.random.uniform(phase_key, (pattern_count, 2), jnp.float32, 0.0, 2.0 * math.pi)
    row_place = jnp.arange(GRID_ROWS, dtype=jnp.float32) / GRID_ROWS
    col_place = jnp.arange(GRID_COLS, dtype=jnp.float32) / GRID_COLS
    along_rows = jnp.cos(2.0 * math.pi * frequency[:, 0:1] * row_place[None, :] + phase_draw[:, 0:1])
    along_cols = jnp.cos(2.0 * math.pi * frequency[:, 1:2] * col_place[None, :] + phase_draw[:, 1:2])
    return 2.0 * along_rows[:, :, None] * along_cols[:, None, :]


def draw_init_field(key, part):
    shapes = smooth_patterns(jax.random.fold_in(key, 7))
    coef_key = jax.random.fold_in(key, 11)
    rough_key = jax.random.fold_in(key, 13)
    weights_mix = 0.5 * jax.random.normal(coef_key, (RUNS, pattern_count), jnp.float32)
    rough = jax.random.normal(rough_key, (RUNS, GRID_ROWS, GRID_COLS), jnp.float32)
    smooth = jnp.einsum('rk,kij->rij', weights_mix, shapes)
    return jnp.clip(smooth + rough, -6.0, 6.0)


def draw_decoder(key, part):
    shapes = smooth_patterns(jax.random.fold_in(key, 7))
    mix_key = jax.random.fold_in(key, 17)
    noise_key = jax.random.fold_in(key, 19)
    noise = jax.random.normal(noise_key, (H, GRID_ROWS, GRID_COLS), jnp.float32)
    blend = 0.002
    mixing = jax.random.normal(mix_key, (H, pattern_count), jnp.float32)
    smooth = jnp.einsum('hk,kij->hij', mixing, shapes)
    return jnp.clip(noise * H ** (-0.5) + blend * smooth, -0.22, 0.22).astype(jnp.bfloat16)


def set_ends(values, rng, least, largest):
    longest = values.shape.index(max(values.shape))
    spots = []
    for shift in (0, 1):
        where = [jax.random.randint(jax.random.fold_in(rng, axis), (), 0, length) for axis, length in enumerate(values.shape)]
        where[longest] = (where[longest] + shift) % values.shape[longest]
        spots.append(tuple(where))
    return values.at[spots[0]].set(least).at[spots[1]].set(largest)


def block_levels(rng, extent, shards, smallest, high):
    def one(position, shards_of):
        draws = jax.random.uniform(jax.random.fold_in(jax.random.fold_in(rng, 6), position), (shards_of,), jnp.float32, smallest / len(shards), high / len(shards))
        return jnp.repeat(jnp.exp(draws), extent[position] // shards_of).reshape((-1,) + (1,) * (len(extent) - position - 1))

    loudness = one(*shards[0])
    for cut in shards[1:]:
        loudness = loudness * one(*cut)
    return loudness


def centred(rng, dims, scale, reach, kind=jnp.bfloat16):
    return jnp.clip(scale * jax.random.normal(rng, dims, jnp.float32), -reach, reach).astype(kind)


def setup_inputs(seed: int = 0) -> dict:
    key_list = jax.random.split(jax.random.key(seed), 11)
    init_field = draw_init_field(jax.random.fold_in(key_list[10], 71), 0)
    conduct = jnp.clip(jnp.exp(math.log(2.0) - 1.3862944 * jax.random.uniform(key_list[1], (GRID_ROWS, GRID_COLS), jnp.float32) ** block_levels(key_list[1], (GRID_ROWS, GRID_COLS), ((0, 8), (1, 8)), -0.2, 0.2)), 0.5, 2.0)
    nonlin = jnp.clip(jnp.exp(math.log(1.0) - 2.3025851 * jax.random.uniform(key_list[2], (RUNS,), jnp.float32) ** block_levels(key_list[2], (RUNS,), ((0, 2),), -0.2, 0.2)), 0.1, 1.0)
    counts = set_ends(jax.random.randint(key_list[3], (RUNS,), 1, STEPS + 1), jax.random.fold_in(key_list[3], 1), 1, STEPS).astype(jnp.int32)
    descriptors = centred(key_list[4], (RUNS, P_SIZE), 1.0, 6.0)
    time_code = centred(key_list[5], (STEPS, P_SIZE), 1.0, 6.0)
    w_in = centred(key_list[6], (P_SIZE, H), P_SIZE ** -0.5, 0.375)
    bias_in = centred(key_list[7], (H,), 1.0, 6.0, jnp.float32)
    w_out = centred(key_list[8], (H, H), H ** -0.5, 0.25)
    decoder = draw_decoder(jax.random.fold_in(key_list[10], 71), 0)
    return {"init_field": init_field, "conduct": conduct, "nonlin": nonlin, "counts": counts, "descriptors": descriptors, "time_code": time_code, "w_in": w_in, "bias_in": bias_in, "w_out": w_out, "decoder": decoder}


time_step = 0.12
learn_rate = 0.5

def advance(padded, cond_pad, nonlin, active, inside):
    kappa = cond_pad[None] / (1.0 + nonlin[:, None, None] * padded * padded)
    centre = padded[:, 1:-1, 1:-1]
    middle = kappa[:, 1:-1, 1:-1]
    flux = jnp.zeros_like(centre)
    places = ((slice(2, None), slice(1, -1)), (slice(0, -2), slice(1, -1)), (slice(1, -1), slice(2, None)), (slice(1, -1), slice(0, -2)))
    for rows_at, cols_at in places:
        flux = flux + 0.5 * (middle + kappa[:, rows_at, cols_at]) * (padded[:, rows_at, cols_at] - centre)
    moved = jnp.where(inside[None, 1:-1, 1:-1], centre + time_step * flux, jnp.zeros_like(centre))
    return jnp.where(active[:, None, None], moved, centre)

def trunk(rows_in, w_in, bias_in, w_out):
    pre = jnp.dot(rows_in, w_in, preferred_element_type=jnp.float32) + bias_in
    act = jax.nn.gelu(pre).astype(jnp.bfloat16)
    hidden = jnp.dot(act, w_out, preferred_element_type=jnp.float32).astype(jnp.bfloat16)
    return (pre, act, hidden)

def trunk_grads(rows_in, pre, act, w_out, dhidden):
    grad_b = dhidden.astype(jnp.bfloat16)
    grad_out = lax.dot_general(act, grad_b, (((0,), (0,)), ((), ())), preferred_element_type=jnp.float32)
    back = lax.dot_general(grad_b, w_out, (((1,), (1,)), ((), ())), preferred_element_type=jnp.float32)
    _, pull = jax.vjp(jax.nn.gelu, pre)
    grad_pre = pull(back)[0]
    grad_in = lax.dot_general(rows_in, grad_pre.astype(jnp.bfloat16), (((0,), (0,)), ((), ())), preferred_element_type=jnp.float32)
    return (grad_in, lax.optimization_barrier(jnp.sum(grad_pre, axis=0)), grad_out)

def reference(init_field, conduct, nonlin, counts, descriptors, time_code, w_in, bias_in, w_out, decoder):
    inside = jnp.pad(jnp.ones_like(conduct), 1) > 0.5
    cond_pad = jnp.pad(conduct, 1)
    field = init_field
    shots = []
    for step in range(STEPS):
        padded = jnp.pad(field, ((0, 0), (1, 1), (1, 1)))
        field = advance(padded, cond_pad, nonlin, step < counts, inside)
        shots.append(field.astype(jnp.bfloat16))
    snapshots = jnp.stack(shots, axis=1)
    rows_in = (descriptors.astype(jnp.float32)[:, None, :] + time_code.astype(jnp.float32)[None]).astype(jnp.bfloat16).reshape(RUNS * STEPS, P_SIZE)
    pre, act, hidden = trunk(rows_in, w_in, bias_in, w_out)
    cells = GRID_ROWS * GRID_COLS
    weights = decoder.reshape(H, cells)
    scale = 1.0 / (RUNS * STEPS)
    hid_blocks = hidden.reshape(RUNS // 8, 8 * STEPS, H)
    shot_blocks = snapshots.reshape(RUNS // 8, 8 * STEPS, cells)

    def one_block(pair):
        hid, shot = pair
        pred = jnp.dot(hid, weights, preferred_element_type=jnp.float32)
        err = pred - shot.astype(jnp.float32)
        grad_pred = (err * scale).astype(jnp.bfloat16)
        back = lax.dot_general(grad_pred, weights, (((1,), (1,)), ((), ())), preferred_element_type=jnp.float32)
        return (back, jnp.sum(err * err))
    backs, losses = lax.map(one_block, (hid_blocks, shot_blocks))
    dhidden = backs.reshape(RUNS * STEPS, H)
    grad_in, grad_bias, grad_out = trunk_grads(rows_in, pre, act, w_out, dhidden)
    new_w_in = w_in.astype(jnp.float32) - learn_rate * grad_in
    new_bias = bias_in - learn_rate * grad_bias
    new_w_out = w_out.astype(jnp.float32) - learn_rate * grad_out
    mean_loss = jnp.sum(losses) / (RUNS * STEPS * cells)
    return (field, new_w_in, new_bias, new_w_out, mean_loss)
```

```python
import jax
import jax.numpy as jnp
from jax import lax
from jax.experimental import pallas as pl
from jax.experimental.pallas import tpu as pltpu
from jax.sharding import PartitionSpec as P

MESH = pl.DeviceIdType.MESH
f32, bf16 = jnp.float32, jnp.bfloat16
STEP, RATE = 0.12, 0.5
ROWS = 96
GROUPS = ROWS // 4
OFFSETS = ((2, 1), (1, 1), (3, 1), (2, 0), (0, 1), (1, 0), (3, 0))
VMEM_ALL = 64 << 20


def signal_all(peers):
    barrier = pltpu.get_barrier_semaphore()
    for peer in peers:
        pl.semaphore_signal(barrier, inc=1, device_id=peer, device_id_type=MESH)
    pl.semaphore_wait(barrier, len(peers))


def remote(src, dst, send, recv, peer):
    return pltpu.make_async_remote_copy(
        src_ref=src, dst_ref=dst, send_sem=send, recv_sem=recv, device_id=peer, device_id_type=MESH
    )


def main_kernel(
    field, conduct, nl, cnt, decoder, hid,
    final, part, loss,
    fs, cd, u, cb, xs, xr, fx, snap, tr, dl, raw, tf, gram, acc,
    loc_sem, raw_sem, row_send, row_recv, col_send, col_recv, dec_send, dec_recv, own_sem, fwd_send, fwd_recv,
):
    core, row, col = (lax.axis_index(n) for n in ("run", "row", "col"))
    y, zh = col // 2, col % 2
    sibling = (1 - core, row, col)
    down, up = (core, (row + 1) % 8, col), (core, (row + 7) % 8, col)
    right, left = (core, row, (col + 1) % 8), (core, row, (col + 7) % 8)
    targets = [((y + dy) % 4) * 2 + (zh + dz) % 2 for dy, dz in OFFSETS]
    signal_all([(core, row, t) for t in targets] + [up, down, sibling])

    fs3 = fs.reshape(48, 80, 128)
    row_copies = [
        remote(field.at[:, pl.ds(56, 8), :], fs3.at[:, pl.ds(0, 8), :], row_send.at[0], row_recv.at[0], down),
        remote(field.at[:, pl.ds(0, 8), :], fs3.at[:, pl.ds(72, 8), :], row_send.at[1], row_recv.at[1], up),
        remote(conduct.at[pl.ds(56, 8), :], cd.at[pl.ds(0, 8), :], row_send.at[2], row_recv.at[2], down),
        remote(conduct.at[pl.ds(0, 8), :], cd.at[pl.ds(72, 8), :], row_send.at[3], row_recv.at[3], up),
    ]
    loc_copies = [
        pltpu.make_async_copy(field, fs3.at[:, pl.ds(8, 64), :], loc_sem.at[0]),
        pltpu.make_async_copy(conduct, cd.at[pl.ds(8, 64), :], loc_sem.at[1]),
    ]

    def raw_copy(part_at, slot):
        start = pl.multiple_of(part_at * 1024, 1024)
        return pltpu.make_async_copy(decoder.at[pl.ds(start, 1024), :], raw.at[slot], raw_sem.at[slot])

    mine, other = 2 * core, 2 * (1 - core)

    def turn(quarter, slot):
        def piece(hb, carry):
            at = pl.multiple_of(hb * 256, 256)
            to = pl.multiple_of(quarter * 128 + hb * 32, 32)
            for t in range(8):
                tf[t] = raw[slot, pl.ds(at, 256), t * 128 : (t + 1) * 128].astype(f32)
            for t in range(8):
                for i in range(8):
                    tr[t, i, pl.ds(to, 32), :] = tf[t, pl.ds(i, 32, stride=8), :].astype(bf16)
            return carry

        lax.fori_loop(0, 4, piece, 0)

    def dec_copies(hh, kk):
        h0 = pl.multiple_of((mine + hh) * 128, 128)
        rnd = hh * 4 + kk
        out = []
        for j, t in enumerate(targets):
            out.append(
                remote(
                    tr.at[t, pl.ds(2 * kk, 2), pl.ds(h0, 128), :],
                    dl.at[kk, pl.ds(2 * col, 2), pl.ds(h0, 128), :],
                    dec_send.at[rnd, j], dec_recv.at[rnd, j], (core, row, t),
                )
            )
        return out

    def own_copy(hh, kk):
        h0 = pl.multiple_of((mine + hh) * 128, 128)
        return pltpu.make_async_copy(
            tr.at[col, pl.ds(2 * kk, 2), pl.ds(h0, 128), :],
            dl.at[kk, pl.ds(2 * col, 2), pl.ds(h0, 128), :],
            own_sem.at[hh * 4 + kk],
        )

    def fwd_copy(hh, kk):
        h0 = pl.multiple_of((mine + hh) * 128, 128)
        block = dl.at[kk, :, pl.ds(h0, 128), :]
        return remote(block, block, fwd_send.at[hh * 4 + kk], fwd_recv.at[hh * 4 + kk], sibling)

    def send_round(hh, kk):
        for c in dec_copies(hh, kk):
            c.start()
        own_copy(hh, kk).start()

    def pass_round(hh, kk):
        for c in dec_copies(hh, kk):
            c.wait_recv()
        own_copy(hh, kk).wait()
        fwd_copy(hh, kk).start()

    for c in row_copies + loc_copies:
        c.start()
    raw_copy(mine, 0).start()
    raw_copy(mine + 1, 1).start()
    raw_copy(mine, 0).wait()
    turn(mine, 0)
    raw_copy(other, 0).start()
    send_round(0, 0)

    for c in loc_copies:
        c.wait()
    for c in row_copies:
        c.wait_recv()
    for b in range(3):
        u[b, 0:8] = jnp.zeros((8, 2, 8, 128), f32)
        u[b, 88:96] = jnp.zeros((8, 2, 8, 128), f32)

    def fill(i, carry):
        for b in range(3):
            u[b, i + 8] = fs[pl.ds(b * 1280 + i, 16, stride=80), :].reshape(2, 8, 128)
        cb[0, i + 8] = jnp.broadcast_to(cd[pl.ds(i, 1), :] * (0.5 * STEP), (8, 128))
        return carry

    lax.fori_loop(0, 80, fill, 0)
    for s in (0, 1):
        cb[s, 0:8] = jnp.zeros((8, 8, 128), f32)
        cb[s, 88:96] = jnp.zeros((8, 8, 128), f32)

    def clear(b):
        @pl.when(row == 0)
        def _():
            u[b, 8:16] = jnp.zeros((8, 2, 8, 128), f32)

        @pl.when(row == 7)
        def _():
            u[b, 80:88] = jnp.zeros((8, 2, 8, 128), f32)

    for b in range(3):
        clear(b)

    @pl.when(row == 0)
    def _():
        cb[0, 8:16] = jnp.zeros((8, 8, 128), f32)

    @pl.when(row == 7)
    def _():
        cb[0, 80:88] = jnp.zeros((8, 8, 128), f32)

    lane = lax.broadcasted_iota(jnp.int32, (2, 8, 128), 2)
    in32 = lane % 32

    def gather_edges(i):
        out = None
        for b in range(4):
            v = u[b, i] if b < 3 else jnp.broadcast_to(cb[0, i][None], (2, 8, 128))
            ends = pltpu.roll(v, (32 * b + 8) % 128, 2)
            starts = pltpu.roll(v, (32 * b + 24) % 128, 2)
            both = jnp.where(in32 < 8, ends, starts)
            out = both if b == 0 else jnp.where(lane // 32 == b, both, out)
        return out

    def pack(g, carry):
        to_right = to_left = None
        for q in range(4):
            o = gather_edges(4 * g + q)
            u[3, 4 * g + q] = o
            r = pltpu.roll(o, 8 * q, 2) if q else o
            l = pltpu.roll(o, (8 * q + 8) % 32 + 96 if q < 3 else 0, 2) if q < 3 else pltpu.roll(o, 0, 2)
            here = in32 // 8 == q
            to_right = r if q == 0 else jnp.where(here, r, to_right)
            to_left = l if q == 0 else jnp.where(here, l, to_left)
        xs[0, g] = to_right
        xs[1, g] = to_left
        return carry

    lax.fori_loop(2, GROUPS - 2, pack, 0)
    col_copies = [
        remote(xs.at[0], xr.at[0], col_send.at[0], col_recv.at[0], right),
        remote(xs.at[1], xr.at[1], col_send.at[1], col_recv.at[1], left),
    ]
    for c in col_copies:
        c.start()
    for kk in range(1, 4):
        send_round(0, kk)
    raw_copy(mine + 1, 1).wait()
    turn(mine + 1, 1)
    raw_copy(other + 1, 1).start()
    for kk in range(4):
        send_round(1, kk)

    raw_copy(other, 0).wait()
    turn(other, 0)
    for c in col_copies:
        c.wait_recv()

    u[3, 0:8] = jnp.zeros((8, 2, 8, 128), f32)
    u[3, 88:96] = jnp.zeros((8, 2, 8, 128), f32)
    from_left = (in32 >= 16) & (in32 < 24)
    from_right = (in32 >= 8) & (in32 < 16)
    left_ok = (jnp.zeros((2, 8, 128), jnp.int32) + col) > 0
    right_ok = (jnp.zeros((2, 8, 128), jnp.int32) + col) < 7

    def unpack(g, carry):
        gl = xr[0, g]
        gr = xr[1, g]
        for q in range(4):
            o = u[3, 4 * g + q]
            a = pltpu.roll(gl, (16 - 8 * q) % 128, 2)
            c = pltpu.roll(gr, (8 - 8 * q) % 128, 2)
            o = jnp.where(from_left, jnp.where(left_ok, a, 0.0), o)
            o = jnp.where(from_right, jnp.where(right_ok, c, 0.0), o)
            u[3, 4 * g + q] = o
            k = o[0]
            for b in range(3):
                k = jnp.where(lane[0] // 32 == b, pltpu.roll(o[0], 32 * (b + 1), 1), k)
            cb[1, 4 * g + q] = jnp.where(lane[0] < 96, k, 0.0)
        return carry

    lax.fori_loop(2, GROUPS - 2, unpack, 0)
    clear(3)

    @pl.when(row == 0)
    def _():
        cb[1, 8:16] = jnp.zeros((8, 8, 128), f32)

    @pl.when(row == 7)
    def _():
        cb[1, 80:88] = jnp.zeros((8, 8, 128), f32)

    first, last = lane == 0, lane == 127

    def solve(b):
        side = 1 if b == 3 else 0
        coef = nl[b]
        limit = cnt[b]

        def kappa(v, i):
            return cb[side, i][None] / (1.0 + coef * v * v)

        def one_step(s, carry):
            active = jnp.where(limit > s, 1.0, 0.0).astype(f32)
            begin = (9 + s) // 4
            r0 = 4 * begin
            before = u[b, r0 - 1]
            v0 = u[b, r0]
            k0 = kappa(v0, r0)
            flow0 = (k0 + kappa(before, r0 - 1)) * (v0 - before)

            def group(g, state):
                v, k, flow = state
                for q in range(4):
                    i = 4 * g + q
                    vn = u[b, i + 1]
                    kn = kappa(vn, i + 1)
                    flow_n = (k + kn) * (vn - v)
                    vr = pltpu.roll(v, 127, 2)
                    kr = pltpu.roll(k, 127, 2)
                    across = (k + kr) * (vr - v)
                    if b == 3:
                        fx[s, i] = jnp.where(in32 == 8, pltpu.roll(across, 128 - 15, 2), across)
                        came = pltpu.roll(across, 1, 2)
                    else:
                        e = pltpu.roll(fx[s, i], (120 - 32 * b) % 128, 2)
                        across = jnp.where(last, e, across)
                        came = jnp.where(first, e, pltpu.roll(across, 1, 2))
                    new = v + active * ((flow_n - flow) + (across - came))
                    u[b, i] = new
                    if b < 3:
                        snap[2 * (g % 2) + q // 2, 2 * (g // 2) - 2 + q % 2, s, 16 * b : 16 * b + 16, :] = (
                            new.reshape(16, 128).astype(bf16)
                        )
                    v, k, flow = vn, kn, flow_n
                return v, k, flow

            lax.fori_loop(begin, GROUPS - begin, group, (v0, k0, flow0))
            clear(b)
            return carry

        lax.fori_loop(0, 8, one_step, 0)

    solve(3)
    raw_copy(other + 1, 1).wait()
    turn(other + 1, 1)
    pass_round(0, 0)
    solve(0)
    pass_round(0, 1)
    pass_round(0, 2)
    solve(1)
    pass_round(0, 3)
    pass_round(1, 0)
    solve(2)

    def give_back(i, carry):
        for b in range(3):
            fs[pl.ds(b * 1280 + i, 16, stride=80), :] = u[b, i + 8].reshape(16, 128)
        return carry

    lax.fori_loop(8, 72, give_back, 0)
    out_copy = pltpu.make_async_copy(fs3.at[:, pl.ds(8, 64), :], final, loc_sem.at[2])
    out_copy.start()

    gram[...] = jnp.zeros((512, 512), f32)
    nt = (((1,), (1,)), ((), ()))

    def add_gram(t, carry):
        for h in range(2):
            x = jnp.concatenate([tr[t, 4 * h + i] for i in range(4)], axis=1)
            gram[...] += lax.dot_general(x, x, nt, preferred_element_type=f32)
        return carry

    lax.fori_loop(0, 8, add_gram, 0)
    big = gram[...].astype(bf16)
    small = (gram[...] - big.astype(f32)).astype(bf16)
    part[...] = jnp.dot(hid[...], big, preferred_element_type=f32) + jnp.dot(
        hid[...], small, preferred_element_type=f32
    )

    def square(n, total):
        x = snap[n // 16, 2 + n % 16].astype(f32).reshape(48, 8, 128)
        return total + jnp.sum(x * x, axis=0)

    squares = lax.fori_loop(0, 64, square, jnp.zeros((8, 128), f32))

    acc[...] = jnp.zeros((2, 384, 256), f32)
    for hh in range(2):
        for kk in range(4):
            if hh == 0 and kk == 0:
                pass_round(1, 1)
            if hh == 0 and kk == 2:
                pass_round(1, 2)
            if hh == 1 and kk == 0:
                pass_round(1, 3)
            fwd_copy(hh, kk).wait_recv()

            def multiply(n, carry):
                lhs = jnp.concatenate(
                    [snap[kk, 2 + 4 * n + i].reshape(384, 128) for i in range(4)], axis=1
                )
                rhs = jnp.concatenate(
                    [
                        jnp.concatenate(
                            [
                                dl[kk, 4 * n + i, 128 * hh : 128 * hh + 128, :],
                                dl[kk, 4 * n + i, 256 + 128 * hh : 384 + 128 * hh, :],
                            ],
                            axis=0,
                        )
                        for i in range(4)
                    ],
                    axis=1,
                )
                acc[hh] += lax.dot_general(lhs, rhs, nt, preferred_element_type=f32)
                return carry

            lax.fori_loop(0, 4, multiply, 0)

    total = squares
    for hh in range(2):
        for half in range(2):
            at = slice(256 * half + 128 * hh, 256 * half + 128 * hh + 128)
            a = part[:, at]
            c = acc[hh, :, 128 * half : 128 * half + 128]
            part[:, at] = a - c
            total = total + jnp.sum((hid[:, at].astype(f32) * (a - 2.0 * c)).reshape(48, 8, 128), axis=0)
    loss[...] = total

    out_copy.wait()
    for c in row_copies + col_copies:
        c.wait_send()
    for hh in range(2):
        for kk in range(4):
            for c in dec_copies(hh, kk):
                c.wait_send()
            fwd_copy(hh, kk).wait_send()


def reduce_kernel(part, loss_in, grad, loss_out, r1, q1, r2, q2, l1, l2, l3, g_stage, sem_s, sem_r):
    core, row, col = (lax.axis_index(n) for n in ("run", "row", "col"))
    x, zl = row % 4, row // 4
    y, zh = col // 2, col % 2
    spot = y * 4 + zh * 2 + zl

    def at_x(v):
        return (core, zl * 4 + v, col)

    def at_spot(p):
        return (core, (p % 2) * 4 + x, (p // 4) * 2 + (p // 2) % 2)

    xs = [(x + j) % 4 for j in range(1, 4)]
    spots = [(spot + j) % 16 for j in range(1, 16)]
    sibling = (1 - core, row, col)
    signal_all([at_x(v) for v in xs] + [at_spot(p) for p in spots] + [sibling])
    done = []

    def go(copies):
        for c in copies:
            c.start()
        done.extend(copies)

    first = [
        remote(part.at[pl.ds(pl.multiple_of(96 * v, 8), 96), :], r1.at[j], sem_s.at[j], sem_r.at[j], at_x(v))
        for j, v in enumerate(xs)
    ]
    lfirst = [
        remote(loss_in, l1.at[x], sem_s.at[3 + j], sem_r.at[3 + j], at_x(v)) for j, v in enumerate(xs)
    ]
    go(first + lfirst)
    l1[x] = loss_in[...]
    for c in first + lfirst:
        c.wait_recv()
    total = part[pl.ds(pl.multiple_of(96 * x, 8), 96), :]
    for j in range(3):
        total = total + r1[j]
    for b in range(4):
        q1[b] = total[:, 128 * b : 128 * b + 128]
    l2[spot] = (l1[0] + l1[1]) + (l1[2] + l1[3])

    def tile(ref, p):
        return ref.at[p % 4, pl.ds(pl.multiple_of(24 * (p // 4), 8), 24), :]

    second = [
        remote(tile(q1, p), r2.at[j], sem_s.at[6 + j], sem_r.at[6 + j], at_spot(p)) for j, p in enumerate(spots)
    ]
    lsecond = [
        remote(l2.at[spot], l2.at[spot], sem_s.at[21 + j], sem_r.at[21 + j], at_spot(p))
        for j, p in enumerate(spots)
    ]
    go(second + lsecond)
    for c in second + lsecond:
        c.wait_recv()
    mine = q1[spot % 4, pl.ds(pl.multiple_of(24 * (spot // 4), 8), 24), :]
    for j in range(15):
        mine = mine + r2[j]
    q2[spot % 4, pl.ds(pl.multiple_of(24 * (spot // 4), 8), 24), :] = mine * (1.0 / 768.0)
    lsum = l2[0]
    for p in range(1, 16):
        lsum = lsum + l2[p]
    l3[core] = lsum

    third = [
        remote(tile(q2, spot), tile(q2, spot), sem_s.at[36 + j], sem_r.at[36 + j], at_spot(p))
        for j, p in enumerate(spots)
    ]
    lthird = [remote(l3.at[core], l3.at[core], sem_s.at[51], sem_r.at[51], sibling)]
    go(third + lthird)
    for c in third:
        c.wait_recv()
    for b in range(4):
        g_stage[core, x, :, 128 * b : 128 * b + 128] = q2[b].astype(bf16)

    def block(c, v):
        return g_stage.at[c, v]

    fourth = [
        remote(block(core, x), block(core, x), sem_s.at[52 + j], sem_r.at[52 + j], at_x(v)) for j, v in enumerate(xs)
    ]
    cross = [
        remote(block(core, v), block(core, v), sem_s.at[55 + j], sem_r.at[55 + j], sibling)
        for j, v in enumerate([x] + [(x + 4 - j) % 4 for j in range(1, 4)])
    ]
    go(fourth + cross[:1])
    for j in range(3):
        fourth[j].wait_recv()
        go([cross[1 + j]])
    for c in cross + lthird:
        c.wait_recv()
    grad[...] = g_stage[...].reshape(768, 512)
    loss_out[...] = l3[0] + l3[1]
    for c in done:
        c.wait_send()


def spread(values):
    three = values.reshape(3, 16)
    wide = jnp.broadcast_to(three[:, :, None], (3, 16, 128))
    edge = jnp.concatenate(
        [jnp.broadcast_to(three[b][:, None], (16, 32)) for b in range(3)] + [jnp.zeros((16, 32), values.dtype)],
        axis=1,
    )
    return jnp.concatenate([wide, edge[None]], axis=0).reshape(4, 2, 8, 128)


def per_device(
    init_field, conduct, nonlin, counts, descriptors, time_code, w_in, bias_in, w_out, decoder
):
    core = lax.axis_index("run")
    col = lax.axis_index("col")
    wide = descriptors.astype(f32).reshape(2, 1, 48, 256) + time_code.astype(f32).reshape(1, 8, 1, 256)
    rows_in = wide.astype(bf16).reshape(768, 256)
    pre = jnp.dot(rows_in, w_in, preferred_element_type=f32) + bias_in
    act = jax.nn.gelu(pre).astype(bf16)
    hidden = jnp.dot(act, w_out, preferred_element_type=f32).astype(bf16)
    hid = lax.dynamic_slice_in_dim(hidden, core * 384, 384, 0)

    lanes = jnp.arange(128) % 32
    outside = ((lanes >= 16) & (lanes < 24) & (col == 0)) | ((lanes >= 8) & (lanes < 16) & (col == 7))
    cnt = spread(counts)
    cnt = cnt.at[3].set(jnp.where(outside[None, None, :], 0, cnt[3]))
    vmem = pl.BlockSpec(memory_space=pltpu.VMEM)
    hbm = pl.BlockSpec(memory_space=pl.ANY)
    dma = pltpu.SemaphoreType.DMA
    final, part, loss = pl.pallas_call(
        main_kernel,
        name="solve_and_learn",
        out_shape=(
            jax.ShapeDtypeStruct((48, 64, 128), f32),
            jax.ShapeDtypeStruct((384, 512), f32),
            jax.ShapeDtypeStruct((8, 128), f32),
        ),
        in_specs=[hbm, hbm, vmem, vmem, hbm, vmem],
        out_specs=(hbm, vmem, vmem),
        scratch_shapes=[
            pltpu.VMEM((3840, 128), f32),
            pltpu.VMEM((80, 128), f32),
            pltpu.VMEM((4, ROWS, 2, 8, 128), f32),
            pltpu.VMEM((2, ROWS, 8, 128), f32),
            pltpu.VMEM((2, GROUPS, 2, 8, 128), f32),
            pltpu.VMEM((2, GROUPS, 2, 8, 128), f32),
            pltpu.VMEM((8, ROWS, 2, 8, 128), f32),
            pltpu.VMEM((4, 20, 8, 48, 128), bf16),
            pltpu.VMEM((8, 8, 512, 128), bf16),
            pltpu.VMEM((4, 16, 512, 128), bf16),
            pltpu.VMEM((2, 1024, 1024), bf16),
            pltpu.VMEM((8, 256, 128), f32),
            pltpu.VMEM((512, 512), f32),
            pltpu.VMEM((2, 384, 256), f32),
            dma((3,)), dma((2,)), dma((4,)), dma((4,)), dma((2,)), dma((2,)),
            dma((8, 7)), dma((8, 7)), dma((8,)), dma((8,)), dma((8,)),
        ],
        compiler_params=pltpu.CompilerParams(
            collective_id=0, has_side_effects=True, vmem_limit_bytes=VMEM_ALL - (1 << 16)
        ),
    )(init_field, conduct, spread(nonlin), cnt, decoder.reshape(4096, 1024), hid)

    grad, loss_sum = pl.pallas_call(
        reduce_kernel,
        name="reduce_grad",
        out_shape=(jax.ShapeDtypeStruct((768, 512), bf16), jax.ShapeDtypeStruct((8, 128), f32)),
        in_specs=[vmem, vmem],
        out_specs=(vmem, vmem),
        scratch_shapes=[
            pltpu.VMEM((3, 96, 512), f32),
            pltpu.VMEM((4, 96, 128), f32),
            pltpu.VMEM((15, 24, 128), f32),
            pltpu.VMEM((4, 96, 128), f32),
            pltpu.VMEM((4, 8, 128), f32),
            pltpu.VMEM((16, 8, 128), f32),
            pltpu.VMEM((2, 8, 128), f32),
            pltpu.VMEM((2, 4, 96, 512), bf16),
            dma((60,)), dma((60,)),
        ],
        compiler_params=pltpu.CompilerParams(collective_id=1, has_side_effects=True),
    )(part, loss)

    grad_out = lax.dot_general(act, grad, (((0,), (0,)), ((), ())), preferred_element_type=f32)
    back = lax.dot_general(grad, w_out, (((1,), (1,)), ((), ())), preferred_element_type=f32)
    _, pull = jax.vjp(jax.nn.gelu, pre)
    grad_pre = pull(back)[0]
    grad_in = lax.dot_general(
        rows_in, grad_pre.astype(bf16), (((0,), (0,)), ((), ())), preferred_element_type=f32
    )
    new_w_in = w_in.astype(f32) - RATE * grad_in
    new_bias = bias_in - RATE * jnp.sum(grad_pre, axis=0)
    new_w_out = w_out.astype(f32) - RATE * grad_out
    mean_loss = jnp.sum(loss_sum) / (768 * 512 * 1024)
    return final, new_w_in, new_bias, new_w_out, mean_loss


def solution(mesh):
    in_specs = (
        P("run", "row", "col"), P("row", "col"), P("run"), P("run"), P(), P(), P(), P(), P(),
        P(None, ("row", "col"), None),
    )
    out_specs = (P("run", "row", "col"), P(), P(), P(), P())
    return jax.shard_map(
        per_device, mesh=mesh, in_specs=in_specs, out_specs=out_specs, check_vma=False
    )
```

```python
import jax
import jax.numpy as jnp
from jax import lax
from jax.experimental import pallas as pl
from jax.experimental.pallas import tpu as pltpu
from jax.sharding import PartitionSpec as P

MESH = pl.DeviceIdType.MESH
f32, bf16 = jnp.float32, jnp.bfloat16
STEP, RATE = 0.12, 0.5
ROWS = 96
GROUPS = ROWS // 4
OFFSETS = ((2, 1), (1, 1), (3, 1), (2, 0), (0, 1), (1, 0), (3, 0))
VMEM_ALL = 64 << 20


def signal_all(peers):
    barrier = pltpu.get_barrier_semaphore()
    for peer in peers:
        pl.semaphore_signal(barrier, inc=1, device_id=peer, device_id_type=MESH)
    pl.semaphore_wait(barrier, len(peers))


def remote(src, dst, send, recv, peer):
    return pltpu.make_async_remote_copy(
        src_ref=src, dst_ref=dst, send_sem=send, recv_sem=recv, device_id=peer, device_id_type=MESH
    )


def main_kernel(
    field, conduct, nl, cnt, decoder, hid,
    final, part, loss,
    fs, cd, u, cb, xs, xr, fx, ks, ac, snap, tr, dl, raw, tf, gram, acc,
    loc_sem, raw_sem, row_send, row_recv, col_send, col_recv, dec_send, dec_recv, own_sem, fwd_send, fwd_recv,
):
    core, row, col = (lax.axis_index(n) for n in ("run", "row", "col"))
    y, zh = col // 2, col % 2
    sibling = (1 - core, row, col)
    down, up = (core, (row + 1) % 8, col), (core, (row + 7) % 8, col)
    right, left = (core, row, (col + 1) % 8), (core, row, (col + 7) % 8)
    targets = [((y + dy) % 4) * 2 + (zh + dz) % 2 for dy, dz in OFFSETS]
    signal_all([(core, row, t) for t in targets] + [up, down, sibling])

    fs3 = fs.reshape(48, 80, 128)
    row_copies = [
        remote(field.at[:, pl.ds(56, 8), :], fs3.at[:, pl.ds(0, 8), :], row_send.at[0], row_recv.at[0], down),
        remote(field.at[:, pl.ds(0, 8), :], fs3.at[:, pl.ds(72, 8), :], row_send.at[1], row_recv.at[1], up),
        remote(conduct.at[pl.ds(56, 8), :], cd.at[pl.ds(0, 8), :], row_send.at[2], row_recv.at[2], down),
        remote(conduct.at[pl.ds(0, 8), :], cd.at[pl.ds(72, 8), :], row_send.at[3], row_recv.at[3], up),
    ]
    loc_copies = [
        pltpu.make_async_copy(field, fs3.at[:, pl.ds(8, 64), :], loc_sem.at[0]),
        pltpu.make_async_copy(conduct, cd.at[pl.ds(8, 64), :], loc_sem.at[1]),
    ]

    def raw_copy(part_at, slot):
        start = pl.multiple_of(part_at * 1024, 1024)
        return pltpu.make_async_copy(decoder.at[pl.ds(start, 1024), :], raw.at[slot], raw_sem.at[slot])

    mine, other = 2 * core, 2 * (1 - core)

    def turn(quarter, slot):
        def piece(hb, carry):
            at = pl.multiple_of(hb * 256, 256)
            to = pl.multiple_of(quarter * 128 + hb * 32, 32)
            for t in range(8):
                tf[t] = raw[slot, pl.ds(at, 256), t * 128 : (t + 1) * 128].astype(f32)
            for t in range(8):
                for i in range(8):
                    tr[t, i, pl.ds(to, 32), :] = tf[t, pl.ds(i, 32, stride=8), :].astype(bf16)
            return carry

        lax.fori_loop(0, 4, piece, 0)

    def dec_copies(hh, kk):
        h0 = pl.multiple_of((mine + hh) * 128, 128)
        rnd = hh * 4 + kk
        out = []
        for j, t in enumerate(targets):
            out.append(
                remote(
                    tr.at[t, pl.ds(2 * kk, 2), pl.ds(h0, 128), :],
                    dl.at[kk, pl.ds(2 * col, 2), pl.ds(h0, 128), :],
                    dec_send.at[rnd, j], dec_recv.at[rnd, j], (core, row, t),
                )
            )
        return out

    def own_copy(hh, kk):
        h0 = pl.multiple_of((mine + hh) * 128, 128)
        return pltpu.make_async_copy(
            tr.at[col, pl.ds(2 * kk, 2), pl.ds(h0, 128), :],
            dl.at[kk, pl.ds(2 * col, 2), pl.ds(h0, 128), :],
            own_sem.at[hh * 4 + kk],
        )

    def fwd_copy(hh, kk):
        h0 = pl.multiple_of((mine + hh) * 128, 128)
        block = dl.at[kk, :, pl.ds(h0, 128), :]
        return remote(block, block, fwd_send.at[hh * 4 + kk], fwd_recv.at[hh * 4 + kk], sibling)

    def send_round(hh, kk):
        for c in dec_copies(hh, kk):
            c.start()
        own_copy(hh, kk).start()

    def pass_round(hh, kk):
        for c in dec_copies(hh, kk):
            c.wait_recv()
        own_copy(hh, kk).wait()
        fwd_copy(hh, kk).start()

    for c in row_copies + loc_copies:
        c.start()
    raw_copy(mine, 0).start()
    raw_copy(mine + 1, 1).start()
    raw_copy(mine, 0).wait()
    turn(mine, 0)
    raw_copy(other, 0).start()
    send_round(0, 0)

    for c in loc_copies:
        c.wait()
    for c in row_copies:
        c.wait_recv()
    for b in range(3):
        u[b, 0:8] = jnp.zeros((8, 2, 8, 128), f32)
        u[b, 88:96] = jnp.zeros((8, 2, 8, 128), f32)

    def fill(i, carry):
        for b in range(3):
            u[b, i + 8] = fs[pl.ds(b * 1280 + i, 16, stride=80), :].reshape(2, 8, 128)
        cb[0, i + 8] = jnp.broadcast_to(cd[pl.ds(i, 1), :] * (0.5 * STEP), (8, 128))
        return carry

    lax.fori_loop(0, 80, fill, 0)
    for s in range(4):
        cb[s, 0:8] = jnp.zeros((8, 8, 128), f32)
        cb[s, 88:96] = jnp.zeros((8, 8, 128), f32)

    def clear(b):
        @pl.when(row == 0)
        def _():
            u[b, 8:16] = jnp.zeros((8, 2, 8, 128), f32)

        @pl.when(row == 7)
        def _():
            u[b, 80:88] = jnp.zeros((8, 2, 8, 128), f32)

    for b in range(3):
        clear(b)

    @pl.when(row == 0)
    def _():
        cb[0, 8:16] = jnp.zeros((8, 8, 128), f32)

    @pl.when(row == 7)
    def _():
        cb[0, 80:88] = jnp.zeros((8, 8, 128), f32)

    lane = lax.broadcasted_iota(jnp.int32, (2, 8, 128), 2)
    in32 = lane % 32

    def gather_edges(i):
        out = None
        for b in range(4):
            v = u[b, i] if b < 3 else jnp.broadcast_to(cb[0, i][None], (2, 8, 128))
            ends = pltpu.roll(v, (32 * b + 8) % 128, 2)
            starts = pltpu.roll(v, (32 * b + 24) % 128, 2)
            both = jnp.where(in32 < 8, ends, starts)
            out = both if b == 0 else jnp.where(lane // 32 == b, both, out)
        return out

    def pack(g, carry):
        to_right = to_left = None
        for q in range(4):
            o = gather_edges(4 * g + q)
            u[3, 4 * g + q] = o
            r = pltpu.roll(o, 8 * q, 2) if q else o
            l = pltpu.roll(o, (8 * q + 8) % 32 + 96 if q < 3 else 0, 2) if q < 3 else pltpu.roll(o, 0, 2)
            here = in32 // 8 == q
            to_right = r if q == 0 else jnp.where(here, r, to_right)
            to_left = l if q == 0 else jnp.where(here, l, to_left)
        xs[0, g] = to_right
        xs[1, g] = to_left
        return carry

    lax.fori_loop(2, GROUPS - 2, pack, 0)
    col_copies = [
        remote(xs.at[0], xr.at[0], col_send.at[0], col_recv.at[0], right),
        remote(xs.at[1], xr.at[1], col_send.at[1], col_recv.at[1], left),
    ]
    for c in col_copies:
        c.start()
    for kk in range(1, 4):
        send_round(0, kk)
    raw_copy(mine + 1, 1).wait()
    turn(mine + 1, 1)
    raw_copy(other + 1, 1).start()
    for kk in range(4):
        send_round(1, kk)

    raw_copy(other, 0).wait()
    turn(other, 0)
    for c in col_copies:
        c.wait_recv()

    u[3, 0:8] = jnp.zeros((8, 2, 8, 128), f32)
    u[3, 88:96] = jnp.zeros((8, 2, 8, 128), f32)
    from_left = (in32 >= 16) & (in32 < 24)
    from_right = (in32 >= 8) & (in32 < 16)
    left_ok = (jnp.zeros((2, 8, 128), jnp.int32) + col) > 0
    right_ok = (jnp.zeros((2, 8, 128), jnp.int32) + col) < 7

    def unpack(g, carry):
        gl = xr[0, g]
        gr = xr[1, g]
        for q in range(4):
            o = u[3, 4 * g + q]
            a = pltpu.roll(gl, (16 - 8 * q) % 128, 2)
            c = pltpu.roll(gr, (8 - 8 * q) % 128, 2)
            o = jnp.where(from_left, jnp.where(left_ok, a, 0.0), o)
            o = jnp.where(from_right, jnp.where(right_ok, c, 0.0), o)
            u[3, 4 * g + q] = o
            k = o[0]
            for b in range(3):
                k = jnp.where(lane[0] // 32 == b, pltpu.roll(o[0], 32 * (b + 1), 1), k)
            cb[2, 4 * g + q] = jnp.where(lane[0] < 96, k, 0.0)
        return carry

    lax.fori_loop(2, GROUPS - 2, unpack, 0)
    clear(3)

    @pl.when(row == 0)
    def _():
        cb[2, 8:16] = jnp.zeros((8, 8, 128), f32)

    @pl.when(row == 7)
    def _():
        cb[2, 80:88] = jnp.zeros((8, 8, 128), f32)

    def shift_conduct(g, carry):
        for q in range(4):
            for side in (0, 2):
                cb[side + 1, 4 * g + q] = pltpu.roll(cb[side, 4 * g + q], 127, 1)
        return carry

    lax.fori_loop(2, GROUPS - 2, shift_conduct, 0)
    first, last = lane == 0, lane == 127

    def solve(blocks, size, after_step=None):
        edge = blocks == (3,)
        side = 2 if edge else 0
        per = 8 // size
        coef = [nl[b] for b in blocks]

        def kappa(v, i, n, shifted=0):
            return cb[side + shifted, i][None] / (1.0 + coef[n] * v * v)

        def one_step(s, carry):
            active = [jnp.where(cnt[b] > s, 1.0, 0.0).astype(f32) for b in blocks]
            begin = (9 + s) // size
            r0 = size * begin

            def ahead(i, vs):
                out = []
                for n, b in enumerate(blocks):
                    v = vs[n]
                    k = kappa(v, i, n)
                    vr = pltpu.roll(v, 127, 2)
                    across = (k + kappa(vr, i, n, 1)) * (vr - v)
                    if not edge:
                        across = jnp.where(last, fx[b, s, i], across)
                    out.append((k, across))
                return out

            def keep(g, q, made):
                for n, (k, across) in enumerate(made):
                    ks[n, (g % 2) * size + q] = k
                    ac[n, (g % 2) * size + q] = across

            flows = []
            for q in range(size):
                vs = [u[b, r0 + q] for b in blocks]
                made = ahead(r0 + q, vs)
                keep(begin, q, made)
                if q == 0:
                    for n, b in enumerate(blocks):
                        before = u[b, r0 - 1]
                        flows.append((made[n][0] + kappa(before, r0 - 1, n)) * (vs[n] - before))

            def group(g, flow):
                flow = list(flow)
                base, now = size * g, (g % 2) * size
                count = range(len(blocks))
                v = [[u[b, base + q] for b in blocks] for q in range(size)]
                k = [[ks[n, now + q] for n in count] for q in range(size)]
                a = [[ac[n, now + q] for n in count] for q in range(size)]
                v_next = [[u[b, base + size + q] for b in blocks] for q in range(size)]
                made = [ahead(base + size + q, v_next[q]) for q in range(size)]
                for q in range(size):
                    for n, b in enumerate(blocks):
                        vn = v[q + 1][n] if q + 1 < size else v_next[0][n]
                        kn = k[q + 1][n] if q + 1 < size else made[0][n][0]
                        flow_n = (k[q][n] + kn) * (vn - v[q][n])
                        came = pltpu.roll(a[q][n], 1, 2)
                        if edge:
                            f = jnp.where(in32 == 8, pltpu.roll(a[q][n], 113, 2), a[q][n])
                            for to in range(3):
                                fx[to, s, base + q] = pltpu.roll(f, 120 - 32 * to, 2)
                        else:
                            came = jnp.where(first, fx[b, s, base + q], came)
                        new = v[q][n] + active[n] * ((flow_n - flow[n]) + (a[q][n] - came))
                        u[b, base + q] = new
                        if not edge:
                            snap[
                                size * (g % per) // 2 + q // 2, 2 * (g // per) - 2 + q % 2, s, 16 * b : 16 * b + 16, :
                            ] = new.reshape(16, 128).astype(bf16)
                        flow[n] = flow_n
                for q in range(size):
                    keep(g + 1, q, made[q])
                return tuple(flow)

            lax.fori_loop(begin, ROWS // size - begin, group, tuple(flows))
            for b in blocks:
                clear(b)
            if after_step is not None:
                after_step(s)
            return carry

        lax.fori_loop(0, 8, one_step, 0)

    solve((3,), 8)
    raw_copy(other + 1, 1).wait()
    turn(other + 1, 1)
    pass_round(0, 0)
    pass_round(0, 1)
    pass_round(0, 2)

    def pass_at(s):
        for at, hh, kk in ((2, 0, 3), (4, 1, 0), (6, 1, 1)):

            @pl.when(s == at)
            def _():
                pass_round(hh, kk)

    solve((0, 1, 2), 4, pass_at)
    pass_round(1, 2)

    def give_back(i, carry):
        for b in range(3):
            fs[pl.ds(b * 1280 + i, 16, stride=80), :] = u[b, i + 8].reshape(16, 128)
        return carry

    lax.fori_loop(8, 72, give_back, 0)
    out_copy = pltpu.make_async_copy(fs3.at[:, pl.ds(8, 64), :], final, loc_sem.at[2])
    out_copy.start()

    gram[...] = jnp.zeros((512, 512), f32)
    nt = (((1,), (1,)), ((), ()))

    def add_gram(t, carry):
        x = jnp.concatenate([tr[t, i] for i in range(8)], axis=1)
        gram[0:256] += lax.dot_general(x[0:256], x, nt, preferred_element_type=f32)
        gram[256:512, 256:512] += lax.dot_general(x[256:512], x[256:512], nt, preferred_element_type=f32)
        return carry

    lax.fori_loop(0, 8, add_gram, 0)
    pass_round(1, 3)
    gram[256:512, 0:256] = gram[0:256, 256:512].T
    big = gram[...].astype(bf16)
    small = (gram[...] - big.astype(f32)).astype(bf16)
    part[...] = jnp.dot(hid[...], big, preferred_element_type=f32) + jnp.dot(
        hid[...], small, preferred_element_type=f32
    )

    def square(n, total):
        x = snap[n // 16, 2 + n % 16].astype(f32).reshape(48, 8, 128)
        return total + jnp.sum(x * x, axis=0)

    squares = lax.fori_loop(0, 64, square, jnp.zeros((8, 128), f32))

    for hh in range(2):
        for kk in range(4):
            fwd_copy(hh, kk).wait_recv()

            lhs = jnp.concatenate([snap[kk, 2 + i].reshape(384, 128) for i in range(16)], axis=1)
            rhs = jnp.concatenate(
                [
                    jnp.concatenate(
                        [
                            dl[kk, i, 128 * hh : 128 * hh + 128, :],
                            dl[kk, i, 256 + 128 * hh : 384 + 128 * hh, :],
                        ],
                        axis=0,
                    )
                    for i in range(16)
                ],
                axis=1,
            )
            got = lax.dot_general(lhs, rhs, nt, preferred_element_type=f32)
            acc[hh] = got if kk == 0 else acc[hh] + got

    total = squares
    for hh in range(2):
        for half in range(2):
            at = slice(256 * half + 128 * hh, 256 * half + 128 * hh + 128)
            a = part[:, at]
            c = acc[hh, :, 128 * half : 128 * half + 128]
            part[:, at] = a - c
            total = total + jnp.sum((hid[:, at].astype(f32) * (a - 2.0 * c)).reshape(48, 8, 128), axis=0)
    loss[...] = total

    out_copy.wait()
    for c in row_copies + col_copies:
        c.wait_send()
    for hh in range(2):
        for kk in range(4):
            for c in dec_copies(hh, kk):
                c.wait_send()
            fwd_copy(hh, kk).wait_send()


def reduce_kernel(part, loss_in, grad, loss_out, r1, q1, r2, q2, l1, l2, l3, g_stage, sem_s, sem_r):
    core, row, col = (lax.axis_index(n) for n in ("run", "row", "col"))
    x, zl = row % 4, row // 4
    y, zh = col // 2, col % 2
    spot = y * 4 + zh * 2 + zl

    def at_x(v):
        return (core, zl * 4 + v, col)

    def at_spot(p):
        return (core, (p % 2) * 4 + x, (p // 4) * 2 + (p // 2) % 2)

    xs = [(x + j) % 4 for j in range(1, 4)]
    spots = [(spot + j) % 16 for j in range(1, 16)]
    sibling = (1 - core, row, col)
    signal_all([at_x(v) for v in xs] + [at_spot(p) for p in spots] + [sibling])
    done = []

    def go(copies):
        for c in copies:
            c.start()
        done.extend(copies)

    first = [
        remote(part.at[pl.ds(pl.multiple_of(96 * v, 8), 96), :], r1.at[j], sem_s.at[j], sem_r.at[j], at_x(v))
        for j, v in enumerate(xs)
    ]
    lfirst = [
        remote(loss_in, l1.at[x], sem_s.at[3 + j], sem_r.at[3 + j], at_x(v)) for j, v in enumerate(xs)
    ]
    go(first + lfirst)
    l1[x] = loss_in[...]
    for c in first + lfirst:
        c.wait_recv()
    total = part[pl.ds(pl.multiple_of(96 * x, 8), 96), :]
    for j in range(3):
        total = total + r1[j]
    for b in range(4):
        q1[b] = total[:, 128 * b : 128 * b + 128]
    l2[spot] = (l1[0] + l1[1]) + (l1[2] + l1[3])

    def tile(ref, p):
        return ref.at[p % 4, pl.ds(pl.multiple_of(24 * (p // 4), 8), 24), :]

    second = [
        remote(tile(q1, p), r2.at[j], sem_s.at[6 + j], sem_r.at[6 + j], at_spot(p)) for j, p in enumerate(spots)
    ]
    lsecond = [
        remote(l2.at[spot], l2.at[spot], sem_s.at[21 + j], sem_r.at[21 + j], at_spot(p))
        for j, p in enumerate(spots)
    ]
    go(second + lsecond)
    for c in second + lsecond:
        c.wait_recv()
    mine = q1[spot % 4, pl.ds(pl.multiple_of(24 * (spot // 4), 8), 24), :]
    for j in range(15):
        mine = mine + r2[j]
    q2[spot % 4, pl.ds(pl.multiple_of(24 * (spot // 4), 8), 24), :] = mine * (1.0 / 768.0)
    lsum = l2[0]
    for p in range(1, 16):
        lsum = lsum + l2[p]
    l3[core] = lsum

    third = [
        remote(tile(q2, spot), tile(q2, spot), sem_s.at[36 + j], sem_r.at[36 + j], at_spot(p))
        for j, p in enumerate(spots)
    ]
    lthird = [remote(l3.at[core], l3.at[core], sem_s.at[51], sem_r.at[51], sibling)]
    go(third + lthird)
    for c in third:
        c.wait_recv()
    for b in range(4):
        g_stage[core, x, :, 128 * b : 128 * b + 128] = q2[b].astype(bf16)

    def block(c, v):
        return g_stage.at[c, v]

    fourth = [
        remote(block(core, x), block(core, x), sem_s.at[52 + j], sem_r.at[52 + j], at_x(v)) for j, v in enumerate(xs)
    ]
    cross = [
        remote(block(core, v), block(core, v), sem_s.at[55 + j], sem_r.at[55 + j], sibling)
        for j, v in enumerate([x] + [(x + 4 - j) % 4 for j in range(1, 4)])
    ]
    go(fourth + cross[:1])
    for j in range(3):
        fourth[j].wait_recv()
        go([cross[1 + j]])
    for c in cross + lthird:
        c.wait_recv()
    grad[...] = g_stage[...].reshape(768, 512)
    loss_out[...] = l3[0] + l3[1]
    for c in done:
        c.wait_send()


def spread(values):
    three = values.reshape(3, 16)
    wide = jnp.broadcast_to(three[:, :, None], (3, 16, 128))
    edge = jnp.concatenate(
        [jnp.broadcast_to(three[b][:, None], (16, 32)) for b in range(3)] + [jnp.zeros((16, 32), values.dtype)],
        axis=1,
    )
    return jnp.concatenate([wide, edge[None]], axis=0).reshape(4, 2, 8, 128)


def per_device(
    init_field, conduct, nonlin, counts, descriptors, time_code, w_in, bias_in, w_out, decoder
):
    core = lax.axis_index("run")
    col = lax.axis_index("col")
    wide = descriptors.astype(f32).reshape(2, 1, 48, 256) + time_code.astype(f32).reshape(1, 8, 1, 256)
    rows_in = wide.astype(bf16).reshape(768, 256)
    pre = jnp.dot(rows_in, w_in, preferred_element_type=f32) + bias_in
    act = jax.nn.gelu(pre).astype(bf16)
    hidden = jnp.dot(act, w_out, preferred_element_type=f32).astype(bf16)
    hid = lax.dynamic_slice_in_dim(hidden, core * 384, 384, 0)

    lanes = jnp.arange(128) % 32
    outside = ((lanes >= 16) & (lanes < 24) & (col == 0)) | ((lanes >= 8) & (lanes < 16) & (col == 7))
    cnt = spread(counts)
    cnt = cnt.at[3].set(jnp.where(outside[None, None, :], 0, cnt[3]))
    vmem = pl.BlockSpec(memory_space=pltpu.VMEM)
    hbm = pl.BlockSpec(memory_space=pl.ANY)
    dma = pltpu.SemaphoreType.DMA
    final, part, loss = pl.pallas_call(
        main_kernel,
        name="solve_and_learn",
        out_shape=(
            jax.ShapeDtypeStruct((48, 64, 128), f32),
            jax.ShapeDtypeStruct((384, 512), f32),
            jax.ShapeDtypeStruct((8, 128), f32),
        ),
        in_specs=[hbm, hbm, vmem, vmem, hbm, vmem],
        out_specs=(hbm, vmem, vmem),
        scratch_shapes=[
            pltpu.VMEM((3840, 128), f32),
            pltpu.VMEM((80, 128), f32),
            pltpu.VMEM((4, ROWS, 2, 8, 128), f32),
            pltpu.VMEM((4, ROWS, 8, 128), f32),
            pltpu.VMEM((2, GROUPS, 2, 8, 128), f32),
            pltpu.VMEM((2, GROUPS, 2, 8, 128), f32),
            pltpu.VMEM((3, 8, ROWS, 2, 8, 128), f32),
            pltpu.VMEM((3, 16, 2, 8, 128), f32),
            pltpu.VMEM((3, 16, 2, 8, 128), f32),
            pltpu.VMEM((4, 20, 8, 48, 128), bf16),
            pltpu.VMEM((8, 8, 512, 128), bf16),
            pltpu.VMEM((4, 16, 512, 128), bf16),
            pltpu.VMEM((2, 1024, 1024), bf16),
            pltpu.VMEM((8, 256, 128), f32),
            pltpu.VMEM((512, 512), f32),
            pltpu.VMEM((2, 384, 256), f32),
            dma((3,)), dma((2,)), dma((4,)), dma((4,)), dma((2,)), dma((2,)),
            dma((8, 7)), dma((8, 7)), dma((8,)), dma((8,)), dma((8,)),
        ],
        compiler_params=pltpu.CompilerParams(
            collective_id=0, has_side_effects=True, vmem_limit_bytes=VMEM_ALL - (1 << 16)
        ),
    )(init_field, conduct, spread(nonlin), cnt, decoder.reshape(4096, 1024), hid)

    grad, loss_sum = pl.pallas_call(
        reduce_kernel,
        name="reduce_grad",
        out_shape=(jax.ShapeDtypeStruct((768, 512), bf16), jax.ShapeDtypeStruct((8, 128), f32)),
        in_specs=[vmem, vmem],
        out_specs=(vmem, vmem),
        scratch_shapes=[
            pltpu.VMEM((3, 96, 512), f32),
            pltpu.VMEM((4, 96, 128), f32),
            pltpu.VMEM((15, 24, 128), f32),
            pltpu.VMEM((4, 96, 128), f32),
            pltpu.VMEM((4, 8, 128), f32),
            pltpu.VMEM((16, 8, 128), f32),
            pltpu.VMEM((2, 8, 128), f32),
            pltpu.VMEM((2, 4, 96, 512), bf16),
            dma((60,)), dma((60,)),
        ],
        compiler_params=pltpu.CompilerParams(collective_id=1, has_side_effects=True),
    )(part, loss)

    grad_out = lax.dot_general(act, grad, (((0,), (0,)), ((), ())), preferred_element_type=f32)
    back = lax.dot_general(grad, w_out, (((1,), (1,)), ((), ())), preferred_element_type=f32)
    _, pull = jax.vjp(jax.nn.gelu, pre)
    grad_pre = pull(back)[0]
    grad_in = lax.dot_general(
        rows_in, grad_pre.astype(bf16), (((0,), (0,)), ((), ())), preferred_element_type=f32
    )
    new_w_in = w_in.astype(f32) - RATE * grad_in
    new_bias = bias_in - RATE * jnp.sum(grad_pre, axis=0)
    new_w_out = w_out.astype(f32) - RATE * grad_out
    mean_loss = jnp.sum(loss_sum) / (768 * 512 * 1024)
    return final, new_w_in, new_bias, new_w_out, mean_loss


def solution(mesh):
    in_specs = (
        P("run", "row", "col"), P("row", "col"), P("run"), P("run"), P(), P(), P(), P(), P(),
        P(None, ("row", "col"), None),
    )
    out_specs = (P("run", "row", "col"), P(), P(), P(), P())
    return jax.shard_map(
        per_device, mesh=mesh, in_specs=in_specs, out_specs=out_specs, check_vma=False
    )
```

```python
import jax
import jax.numpy as jnp
from jax import lax
from jax.experimental import pallas as pl
from jax.experimental.pallas import tpu as pltpu
from jax.sharding import PartitionSpec as P

MESH = pl.DeviceIdType.MESH
f32, bf16 = jnp.float32, jnp.bfloat16
STEP, RATE = 0.12, 0.5
ROWS = 96
GROUPS = ROWS // 4
OFFSETS = ((2, 1), (1, 1), (3, 1), (2, 0), (0, 1), (1, 0), (3, 0))
VMEM_ALL = 64 << 20


def signal_all(peers):
    barrier = pltpu.get_barrier_semaphore()
    for peer in peers:
        pl.semaphore_signal(barrier, inc=1, device_id=peer, device_id_type=MESH)
    pl.semaphore_wait(barrier, len(peers))


def remote(src, dst, send, recv, peer):
    return pltpu.make_async_remote_copy(
        src_ref=src, dst_ref=dst, send_sem=send, recv_sem=recv, device_id=peer, device_id_type=MESH
    )


def main_kernel(
    field, conduct, nl, cnt, decoder, hid,
    final, part, loss,
    fs, cd, u, cb, rs, rr, xs, xr, fx, ks, ac, snap, tr, dl, raw, tf, gram, acc,
    loc_sem, raw_sem, row_send, row_recv, col_send, col_recv, dec_send, dec_recv, own_sem, fwd_send, fwd_recv,
):
    core, row, col = (lax.axis_index(n) for n in ("run", "row", "col"))
    y, zh = col // 2, col % 2
    sibling = (1 - core, row, col)
    down, up = (core, (row + 1) % 8, col), (core, (row + 7) % 8, col)
    right, left = (core, row, (col + 1) % 8), (core, row, (col + 7) % 8)
    targets = [((y + dy) % 4) * 2 + (zh + dz) % 2 for dy, dz in OFFSETS]
    signal_all([(core, row, t) for t in targets] + [up, down, sibling])

    fs3 = fs.reshape(48, 64, 128)
    row_copies = [
        remote(rs.at[0], rr.at[0], row_send.at[0], row_recv.at[0], down),
        remote(rs.at[1], rr.at[1], row_send.at[1], row_recv.at[1], up),
    ]
    edge_copies = [
        remote(conduct.at[pl.ds(56, 8), :], cd.at[pl.ds(0, 8), :], row_send.at[2], row_recv.at[2], down),
        remote(conduct.at[pl.ds(0, 8), :], cd.at[pl.ds(72, 8), :], row_send.at[3], row_recv.at[3], up),
    ]
    loc_copies = [
        pltpu.make_async_copy(field, fs3, loc_sem.at[0]),
        pltpu.make_async_copy(conduct, cd.at[pl.ds(8, 64), :], loc_sem.at[1]),
    ]

    def raw_copy(part_at, slot):
        start = pl.multiple_of(part_at * 1024, 1024)
        return pltpu.make_async_copy(decoder.at[pl.ds(start, 1024), :], raw.at[slot], raw_sem.at[slot])

    mine, other = 2 * core, 2 * (1 - core)

    def turn(quarter, slot):
        def piece(hb, carry):
            at = pl.multiple_of(hb * 256, 256)
            to = pl.multiple_of(quarter * 128 + hb * 32, 32)
            for t in range(8):
                tf[t] = raw[slot, pl.ds(at, 256), t * 128 : (t + 1) * 128].astype(f32)
            for t in range(8):
                for i in range(8):
                    tr[t, i, pl.ds(to, 32), :] = tf[t, pl.ds(i, 32, stride=8), :].astype(bf16)
            return carry

        lax.fori_loop(0, 4, piece, 0)

    def dec_copies(hh, kk):
        h0 = pl.multiple_of((mine + hh) * 128, 128)
        rnd = hh * 4 + kk
        out = []
        for j, t in enumerate(targets):
            out.append(
                remote(
                    tr.at[t, pl.ds(2 * kk, 2), pl.ds(h0, 128), :],
                    dl.at[kk, pl.ds(2 * col, 2), pl.ds(h0, 128), :],
                    dec_send.at[rnd, j], dec_recv.at[rnd, j], (core, row, t),
                )
            )
        return out

    def own_copy(hh, kk):
        h0 = pl.multiple_of((mine + hh) * 128, 128)
        return pltpu.make_async_copy(
            tr.at[col, pl.ds(2 * kk, 2), pl.ds(h0, 128), :],
            dl.at[kk, pl.ds(2 * col, 2), pl.ds(h0, 128), :],
            own_sem.at[hh * 4 + kk],
        )

    def fwd_copy(hh, kk):
        h0 = pl.multiple_of((mine + hh) * 128, 128)
        block = dl.at[kk, :, pl.ds(h0, 128), :]
        return remote(block, block, fwd_send.at[hh * 4 + kk], fwd_recv.at[hh * 4 + kk], sibling)

    def send_round(hh, kk):
        for c in dec_copies(hh, kk):
            c.start()
        own_copy(hh, kk).start()

    def pass_round(hh, kk):
        for c in dec_copies(hh, kk):
            c.wait_recv()
        own_copy(hh, kk).wait()
        fwd_copy(hh, kk).start()

    for c in loc_copies + edge_copies:
        c.start()
    raw_copy(mine, 0).start()
    raw_copy(mine + 1, 1).start()
    raw_copy(mine, 0).wait()
    turn(mine, 0)
    raw_copy(other, 0).start()
    send_round(0, 0)

    for c in loc_copies:
        c.wait()
    for b in range(3):
        u[b, 0:8] = jnp.zeros((8, 2, 8, 128), f32)
        u[b, 88:96] = jnp.zeros((8, 2, 8, 128), f32)

    def fill(n, carry):
        for q in range(4):
            i = 4 * n + q
            for b in range(3):
                u[b, i + 16] = fs[pl.ds(b * 1024 + i, 16, stride=64), :].reshape(2, 8, 128)
        return carry

    lax.fori_loop(0, 16, fill, 0)

    def pack_rows(i, carry):
        for b in range(3):
            rs[0, i, b] = u[b, i + 72].reshape(16, 128).astype(bf16)
            rs[1, i, b] = u[b, i + 16].reshape(16, 128).astype(bf16)
        return carry

    lax.fori_loop(0, 8, pack_rows, 0)
    for c in row_copies:
        c.start()
    send_round(0, 1)
    raw_copy(mine + 1, 1).wait()
    turn(mine + 1, 1)
    raw_copy(other + 1, 1).start()
    for c in edge_copies + row_copies:
        c.wait_recv()

    def unpack_rows(i, carry):
        for b in range(3):
            u[b, i + 8] = rr[0, i, b].astype(f32).reshape(2, 8, 128)
            u[b, i + 80] = rr[1, i, b].astype(f32).reshape(2, 8, 128)
        return carry

    lax.fori_loop(0, 8, unpack_rows, 0)

    def fill_conduct(n, carry):
        for q in range(4):
            i = 4 * n + q
            cb[0, i + 8] = jnp.broadcast_to(cd[pl.ds(i, 1), :] * (0.5 * STEP), (8, 128))
        return carry

    lax.fori_loop(0, 20, fill_conduct, 0)
    for s in range(4):
        cb[s, 0:8] = jnp.zeros((8, 8, 128), f32)
        cb[s, 88:96] = jnp.zeros((8, 8, 128), f32)

    def clear(b):
        @pl.when(row == 0)
        def _():
            u[b, 8:16] = jnp.zeros((8, 2, 8, 128), f32)

        @pl.when(row == 7)
        def _():
            u[b, 80:88] = jnp.zeros((8, 2, 8, 128), f32)

    for b in range(3):
        clear(b)

    @pl.when(row == 0)
    def _():
        cb[0, 8:16] = jnp.zeros((8, 8, 128), f32)

    @pl.when(row == 7)
    def _():
        cb[0, 80:88] = jnp.zeros((8, 8, 128), f32)

    lane = lax.broadcasted_iota(jnp.int32, (2, 8, 128), 2)
    in32 = lane % 32

    def gather_edges(i):
        out = None
        for b in range(4):
            v = u[b, i] if b < 3 else jnp.broadcast_to(cb[0, i][None], (2, 8, 128))
            ends = pltpu.roll(v, (32 * b + 8) % 128, 2)
            starts = pltpu.roll(v, (32 * b + 24) % 128, 2)
            both = jnp.where(in32 < 8, ends, starts)
            out = both if b == 0 else jnp.where(lane // 32 == b, both, out)
        return out

    def pack(g, carry):
        to_right = to_left = None
        for q in range(4):
            o = gather_edges(4 * g + q)
            u[3, 4 * g + q] = o
            r = pltpu.roll(o, 8 * q, 2) if q else o
            l = pltpu.roll(o, (8 * q + 8) % 32 + 96 if q < 3 else 0, 2) if q < 3 else pltpu.roll(o, 0, 2)
            here = in32 // 8 == q
            to_right = r if q == 0 else jnp.where(here, r, to_right)
            to_left = l if q == 0 else jnp.where(here, l, to_left)
        xs[0, g] = to_right.reshape(16, 128).astype(bf16)
        xs[1, g] = to_left.reshape(16, 128).astype(bf16)
        return carry

    lax.fori_loop(2, GROUPS - 2, pack, 0)
    col_copies = [
        remote(xs.at[0], xr.at[0], col_send.at[0], col_recv.at[0], right),
        remote(xs.at[1], xr.at[1], col_send.at[1], col_recv.at[1], left),
    ]
    for c in col_copies:
        c.start()
    for rnd in range(2, 8):
        send_round(rnd // 4, rnd % 4)

    raw_copy(other, 0).wait()
    turn(other, 0)
    raw_copy(other + 1, 1).wait()
    turn(other + 1, 1)

    gram[...] = jnp.zeros((512, 512), f32)
    nt = (((1,), (1,)), ((), ()))

    def add_gram(t, carry):
        x = jnp.concatenate([tr[t, i] for i in range(8)], axis=1)
        gram[0:256] += lax.dot_general(x[0:256], x, nt, preferred_element_type=f32)
        gram[256:512, 256:512] += lax.dot_general(x[256:512], x[256:512], nt, preferred_element_type=f32)
        return carry

    lax.fori_loop(0, 8, add_gram, 0)
    gram[256:512, 0:256] = gram[0:256, 256:512].T
    big = gram[...].astype(bf16)
    small = (gram[...] - big.astype(f32)).astype(bf16)
    part[...] = jnp.dot(hid[...], big, preferred_element_type=f32) + jnp.dot(
        hid[...], small, preferred_element_type=f32
    )

    for c in col_copies:
        c.wait_recv()

    u[3, 0:8] = jnp.zeros((8, 2, 8, 128), f32)
    u[3, 88:96] = jnp.zeros((8, 2, 8, 128), f32)
    from_left = (in32 >= 16) & (in32 < 24)
    from_right = (in32 >= 8) & (in32 < 16)
    left_ok = (jnp.zeros((2, 8, 128), jnp.int32) + col) > 0
    right_ok = (jnp.zeros((2, 8, 128), jnp.int32) + col) < 7

    def unpack(g, carry):
        gl = xr[0, g].astype(f32).reshape(2, 8, 128)
        gr = xr[1, g].astype(f32).reshape(2, 8, 128)
        for q in range(4):
            o = u[3, 4 * g + q]
            a = pltpu.roll(gl, (16 - 8 * q) % 128, 2)
            c = pltpu.roll(gr, (8 - 8 * q) % 128, 2)
            o = jnp.where(from_left, jnp.where(left_ok, a, 0.0), o)
            o = jnp.where(from_right, jnp.where(right_ok, c, 0.0), o)
            u[3, 4 * g + q] = o
            k = o[0]
            for b in range(3):
                k = jnp.where(lane[0] // 32 == b, pltpu.roll(o[0], 32 * (b + 1), 1), k)
            cb[2, 4 * g + q] = jnp.where(lane[0] < 96, k, 0.0)
        return carry

    lax.fori_loop(2, GROUPS - 2, unpack, 0)
    clear(3)

    @pl.when(row == 0)
    def _():
        cb[2, 8:16] = jnp.zeros((8, 8, 128), f32)

    @pl.when(row == 7)
    def _():
        cb[2, 80:88] = jnp.zeros((8, 8, 128), f32)

    def shift_conduct(g, carry):
        for q in range(4):
            for side in (0, 2):
                cb[side + 1, 4 * g + q] = pltpu.roll(cb[side, 4 * g + q], 127, 1)
        return carry

    lax.fori_loop(2, GROUPS - 2, shift_conduct, 0)
    first, last = lane == 0, lane == 127

    def run_step(s, with_main):
        blocks = (0, 1, 2, 3) if with_main else (3,)
        count = range(len(blocks))
        ahead_s = s + 1 if with_main else s
        coef = [nl[b] for b in blocks]
        active = [jnp.where(cnt[b] > (s if b < 3 else ahead_s), 1.0, 0.0).astype(f32) for b in blocks]
        begin = (9 + s) // 4

        def kappa(v, i, n, shifted=0):
            return cb[(2 if blocks[n] == 3 else 0) + shifted, i][None] / (1.0 + coef[n] * v * v)

        def ahead(i, vs):
            out = []
            for n, b in enumerate(blocks):
                v = vs[n]
                k = kappa(v, i, n)
                vr = pltpu.roll(v, 127, 2)
                across = (k + kappa(vr, i, n, 1)) * (vr - v)
                if b < 3:
                    across = jnp.where(last, fx[b, s % 2, i], across)
                out.append((k, across))
            return out

        def keep(g, q, made):
            for n, (k, across) in enumerate(made):
                ks[blocks[n], (g % 2) * 4 + q] = k
                ac[blocks[n], (g % 2) * 4 + q] = across

        flows = []
        for q in range(4):
            vs = [u[b, 4 * begin + q] for b in blocks]
            made = ahead(4 * begin + q, vs)
            keep(begin, q, made)
            if q == 0:
                for n, b in enumerate(blocks):
                    before = u[b, 4 * begin - 1]
                    flows.append((made[n][0] + kappa(before, 4 * begin - 1, n)) * (vs[n] - before))

        def group(g, flow):
            flow = list(flow)
            base, now = 4 * g, (g % 2) * 4
            v = [[u[b, base + q] for b in blocks] for q in range(4)]
            k = [[ks[b, now + q] for b in blocks] for q in range(4)]
            a = [[ac[b, now + q] for b in blocks] for q in range(4)]
            v_next = [[u[b, base + 4 + q] for b in blocks] for q in range(4)]
            first_made = None
            for q in range(4):
                made = ahead(base + 4 + q, v_next[q])
                first_made = made if q == 0 else first_made
                for n, b in enumerate(blocks):
                    vn = v[q + 1][n] if q < 3 else v_next[0][n]
                    kn = k[q + 1][n] if q < 3 else first_made[n][0]
                    flow_n = (k[q][n] + kn) * (vn - v[q][n])
                    came = pltpu.roll(a[q][n], 1, 2)
                    if b == 3:
                        f = jnp.where(in32 == 8, pltpu.roll(a[q][n], 113, 2), a[q][n])
                        for to in range(3):
                            fx[to, ahead_s % 2, base + q] = pltpu.roll(f, 120 - 32 * to, 2)
                    else:
                        came = jnp.where(first, fx[b, s % 2, base + q], came)
                    new = v[q][n] + active[n] * ((flow_n - flow[n]) + (a[q][n] - came))
                    u[b, base + q] = new
                    if b < 3:
                        snap[2 * (g % 2) + q // 2, 2 * (g // 2) - 2 + q % 2, s, 16 * b : 16 * b + 16, :] = (
                            new.reshape(16, 128).astype(bf16)
                        )
                    flow[n] = flow_n
                keep(g + 1, q, made)
            return tuple(flow)

        lax.fori_loop(begin, GROUPS - begin, group, tuple(flows))
        for b in blocks:
            clear(b)

    pass_round(0, 0)
    pass_round(0, 1)
    run_step(0, False)

    def one_step(s, carry):
        run_step(s, True)
        for at, hh, kk in ((0, 0, 2), (1, 0, 3), (2, 1, 0), (4, 1, 1), (6, 1, 2)):

            @pl.when(s == at)
            def _():
                pass_round(hh, kk)

        return carry

    lax.fori_loop(0, 8, one_step, 0)

    def give_back(n, carry):
        for q in range(4):
            for b in range(3):
                fs[pl.ds(b * 1024 + 4 * n + q, 16, stride=64), :] = u[b, 4 * n + q + 16].reshape(16, 128)
        return carry

    lax.fori_loop(0, 16, give_back, 0)
    out_copy = pltpu.make_async_copy(fs3, final, loc_sem.at[2])
    out_copy.start()
    pass_round(1, 3)

    def square(n, total):
        x = snap[n // 16, 2 + n % 16].astype(f32).reshape(48, 8, 128)
        return total + jnp.sum(x * x, axis=0)

    squares = lax.fori_loop(0, 64, square, jnp.zeros((8, 128), f32))

    for hh in range(2):
        for kk in range(4):
            fwd_copy(hh, kk).wait_recv()

            lhs = jnp.concatenate([snap[kk, 2 + i].reshape(384, 128) for i in range(16)], axis=1)
            rhs = jnp.concatenate(
                [
                    jnp.concatenate(
                        [
                            dl[kk, i, 128 * hh : 128 * hh + 128, :],
                            dl[kk, i, 256 + 128 * hh : 384 + 128 * hh, :],
                        ],
                        axis=0,
                    )
                    for i in range(16)
                ],
                axis=1,
            )
            got = lax.dot_general(lhs, rhs, nt, preferred_element_type=f32)
            acc[hh] = got if kk == 0 else acc[hh] + got

    total = squares
    for hh in range(2):
        for half in range(2):
            at = slice(256 * half + 128 * hh, 256 * half + 128 * hh + 128)
            a = part[:, at]
            c = acc[hh, :, 128 * half : 128 * half + 128]
            part[:, at] = a - c
            total = total + jnp.sum((hid[:, at].astype(f32) * (a - 2.0 * c)).reshape(48, 8, 128), axis=0)
    loss[...] = total

    out_copy.wait()
    for c in row_copies + edge_copies + col_copies:
        c.wait_send()
    for hh in range(2):
        for kk in range(4):
            for c in dec_copies(hh, kk):
                c.wait_send()
            fwd_copy(hh, kk).wait_send()


def reduce_kernel(part, loss_in, grad, loss_out, r1, q1, r2, q2, l1, l2, l3, g_stage, sem_s, sem_r):
    core, row, col = (lax.axis_index(n) for n in ("run", "row", "col"))
    x, zl = row % 4, row // 4
    y, zh = col // 2, col % 2
    spot = y * 4 + zh * 2 + zl

    def at_x(v):
        return (core, zl * 4 + v, col)

    def at_spot(p):
        return (core, (p % 2) * 4 + x, (p // 4) * 2 + (p // 2) % 2)

    xs = [(x + j) % 4 for j in range(1, 4)]
    spots = [(spot + j) % 16 for j in range(1, 16)]
    sibling = (1 - core, row, col)
    signal_all([at_x(v) for v in xs] + [at_spot(p) for p in spots] + [sibling])
    done = []

    def go(copies):
        for c in copies:
            c.start()
        done.extend(copies)

    first = [
        remote(part.at[pl.ds(pl.multiple_of(96 * v, 8), 96), :], r1.at[j], sem_s.at[j], sem_r.at[j], at_x(v))
        for j, v in enumerate(xs)
    ]
    lfirst = [
        remote(loss_in, l1.at[x], sem_s.at[3 + j], sem_r.at[3 + j], at_x(v)) for j, v in enumerate(xs)
    ]
    go(first + lfirst)
    l1[x] = loss_in[...]
    for c in first + lfirst:
        c.wait_recv()
    total = part[pl.ds(pl.multiple_of(96 * x, 8), 96), :]
    for j in range(3):
        total = total + r1[j]
    for b in range(4):
        q1[b] = total[:, 128 * b : 128 * b + 128]
    l2[spot] = (l1[0] + l1[1]) + (l1[2] + l1[3])

    def tile(ref, p):
        return ref.at[p % 4, pl.ds(pl.multiple_of(24 * (p // 4), 8), 24), :]

    second = [
        remote(tile(q1, p), r2.at[j], sem_s.at[6 + j], sem_r.at[6 + j], at_spot(p)) for j, p in enumerate(spots)
    ]
    lsecond = [
        remote(l2.at[spot], l2.at[spot], sem_s.at[21 + j], sem_r.at[21 + j], at_spot(p))
        for j, p in enumerate(spots)
    ]
    go(second + lsecond)
    for c in second + lsecond:
        c.wait_recv()
    mine = q1[spot % 4, pl.ds(pl.multiple_of(24 * (spot // 4), 8), 24), :]
    for j in range(15):
        mine = mine + r2[j]
    q2[spot % 4, pl.ds(pl.multiple_of(24 * (spot // 4), 8), 24), :] = mine * (1.0 / 768.0)
    lsum = l2[0]
    for p in range(1, 16):
        lsum = lsum + l2[p]
    l3[core] = lsum

    third = [
        remote(tile(q2, spot), tile(q2, spot), sem_s.at[36 + j], sem_r.at[36 + j], at_spot(p))
        for j, p in enumerate(spots)
    ]
    lthird = [remote(l3.at[core], l3.at[core], sem_s.at[51], sem_r.at[51], sibling)]
    go(third + lthird)
    for c in third:
        c.wait_recv()
    for b in range(4):
        g_stage[core, x, :, 128 * b : 128 * b + 128] = q2[b].astype(bf16)

    def block(c, v):
        return g_stage.at[c, v]

    fourth = [
        remote(block(core, x), block(core, x), sem_s.at[52 + j], sem_r.at[52 + j], at_x(v)) for j, v in enumerate(xs)
    ]
    cross = [
        remote(block(core, v), block(core, v), sem_s.at[55 + j], sem_r.at[55 + j], sibling)
        for j, v in enumerate([x] + [(x + 4 - j) % 4 for j in range(1, 4)])
    ]
    go(fourth + cross[:1])
    for j in range(3):
        fourth[j].wait_recv()
        go([cross[1 + j]])
    for c in cross + lthird:
        c.wait_recv()
    grad[...] = g_stage[...].reshape(768, 512)
    loss_out[...] = l3[0] + l3[1]
    for c in done:
        c.wait_send()


def spread(values):
    three = values.reshape(3, 16)
    wide = jnp.broadcast_to(three[:, :, None], (3, 16, 128))
    edge = jnp.concatenate(
        [jnp.broadcast_to(three[b][:, None], (16, 32)) for b in range(3)] + [jnp.zeros((16, 32), values.dtype)],
        axis=1,
    )
    return jnp.concatenate([wide, edge[None]], axis=0).reshape(4, 2, 8, 128)


def per_device(
    init_field, conduct, nonlin, counts, descriptors, time_code, w_in, bias_in, w_out, decoder
):
    core = lax.axis_index("run")
    col = lax.axis_index("col")
    wide = descriptors.astype(f32).reshape(2, 1, 48, 256) + time_code.astype(f32).reshape(1, 8, 1, 256)
    rows_in = wide.astype(bf16).reshape(768, 256)
    pre = jnp.dot(rows_in, w_in, preferred_element_type=f32) + bias_in
    act = jax.nn.gelu(pre).astype(bf16)
    hidden = jnp.dot(act, w_out, preferred_element_type=f32).astype(bf16)
    hid = lax.dynamic_slice_in_dim(hidden, core * 384, 384, 0)

    lanes = jnp.arange(128) % 32
    outside = ((lanes >= 16) & (lanes < 24) & (col == 0)) | ((lanes >= 8) & (lanes < 16) & (col == 7))
    cnt = spread(counts)
    cnt = cnt.at[3].set(jnp.where(outside[None, None, :], 0, cnt[3]))
    vmem = pl.BlockSpec(memory_space=pltpu.VMEM)
    hbm = pl.BlockSpec(memory_space=pl.ANY)
    dma = pltpu.SemaphoreType.DMA
    final, part, loss = pl.pallas_call(
        main_kernel,
        name="solve_and_learn",
        out_shape=(
            jax.ShapeDtypeStruct((48, 64, 128), f32),
            jax.ShapeDtypeStruct((384, 512), f32),
            jax.ShapeDtypeStruct((8, 128), f32),
        ),
        in_specs=[hbm, hbm, vmem, vmem, hbm, vmem],
        out_specs=(hbm, vmem, vmem),
        scratch_shapes=[
            pltpu.VMEM((3072, 128), f32),
            pltpu.VMEM((80, 128), f32),
            pltpu.VMEM((4, ROWS, 2, 8, 128), f32),
            pltpu.VMEM((4, ROWS, 8, 128), f32),
            pltpu.VMEM((2, 8, 3, 16, 128), bf16),
            pltpu.VMEM((2, 8, 3, 16, 128), bf16),
            pltpu.VMEM((2, GROUPS, 16, 128), bf16),
            pltpu.VMEM((2, GROUPS, 16, 128), bf16),
            pltpu.VMEM((3, 2, ROWS, 2, 8, 128), f32),
            pltpu.VMEM((4, 8, 2, 8, 128), f32),
            pltpu.VMEM((4, 8, 2, 8, 128), f32),
            pltpu.VMEM((4, 20, 8, 48, 128), bf16),
            pltpu.VMEM((8, 8, 512, 128), bf16),
            pltpu.VMEM((4, 16, 512, 128), bf16),
            pltpu.VMEM((2, 1024, 1024), bf16),
            pltpu.VMEM((8, 256, 128), f32),
            pltpu.VMEM((512, 512), f32),
            pltpu.VMEM((2, 384, 256), f32),
            dma((3,)), dma((2,)), dma((4,)), dma((4,)), dma((2,)), dma((2,)),
            dma((8, 7)), dma((8, 7)), dma((8,)), dma((8,)), dma((8,)),
        ],
        compiler_params=pltpu.CompilerParams(
            collective_id=0, has_side_effects=True, vmem_limit_bytes=VMEM_ALL - (1 << 16)
        ),
    )(init_field, conduct, spread(nonlin), cnt, decoder.reshape(4096, 1024), hid)

    grad, loss_sum = pl.pallas_call(
        reduce_kernel,
        name="reduce_grad",
        out_shape=(jax.ShapeDtypeStruct((768, 512), bf16), jax.ShapeDtypeStruct((8, 128), f32)),
        in_specs=[vmem, vmem],
        out_specs=(vmem, vmem),
        scratch_shapes=[
            pltpu.VMEM((3, 96, 512), f32),
            pltpu.VMEM((4, 96, 128), f32),
            pltpu.VMEM((15, 24, 128), f32),
            pltpu.VMEM((4, 96, 128), f32),
            pltpu.VMEM((4, 8, 128), f32),
            pltpu.VMEM((16, 8, 128), f32),
            pltpu.VMEM((2, 8, 128), f32),
            pltpu.VMEM((2, 4, 96, 512), bf16),
            dma((60,)), dma((60,)),
        ],
        compiler_params=pltpu.CompilerParams(collective_id=1, has_side_effects=True),
    )(part, loss)

    grad_out = lax.dot_general(act, grad, (((0,), (0,)), ((), ())), preferred_element_type=f32)
    back = lax.dot_general(grad, w_out, (((1,), (1,)), ((), ())), preferred_element_type=f32)
    _, pull = jax.vjp(jax.nn.gelu, pre)
    grad_pre = pull(back)[0]
    grad_in = lax.dot_general(
        rows_in, grad_pre.astype(bf16), (((0,), (0,)), ((), ())), preferred_element_type=f32
    )
    new_w_in = w_in.astype(f32) - RATE * grad_in
    new_bias = bias_in - RATE * jnp.sum(grad_pre, axis=0)
    new_w_out = w_out.astype(f32) - RATE * grad_out
    mean_loss = jnp.sum(loss_sum) / (768 * 512 * 1024)
    return final, new_w_in, new_bias, new_w_out, mean_loss


def solution(mesh):
    in_specs = (
        P("run", "row", "col"), P("row", "col"), P("run"), P("run"), P(), P(), P(), P(), P(),
        P(None, ("row", "col"), None),
    )
    out_specs = (P("run", "row", "col"), P(), P(), P(), P())
    return jax.shard_map(
        per_device, mesh=mesh, in_specs=in_specs, out_specs=out_specs, check_vma=False
    )
```

```python
import jax
import jax.numpy as jnp
from jax import lax
from jax.experimental import pallas as pl
from jax.experimental.pallas import tpu as pltpu
from jax.sharding import PartitionSpec as P

MESH = pl.DeviceIdType.MESH
f32, bf16 = jnp.float32, jnp.bfloat16
STEP, RATE = 0.12, 0.5
ROWS = 96
GROUPS = ROWS // 4
OFFSETS = ((2, 1), (1, 1), (3, 1), (2, 0), (0, 1), (1, 0), (3, 0))
VMEM_ALL = 64 << 20


def signal_all(peers):
    barrier = pltpu.get_barrier_semaphore()
    for peer in peers:
        pl.semaphore_signal(barrier, inc=1, device_id=peer, device_id_type=MESH)
    pl.semaphore_wait(barrier, len(peers))


def remote(src, dst, send, recv, peer):
    return pltpu.make_async_remote_copy(
        src_ref=src, dst_ref=dst, send_sem=send, recv_sem=recv, device_id=peer, device_id_type=MESH
    )


def main_kernel(
    field, conduct, nl, cnt, decoder, hid,
    final, part, loss,
    fs, cd, u, cb, rr, xs, xr, fx, ks, ac, snap, tr, dl, raw, tf, gram, acc,
    loc_sem, raw_sem, row_send, row_recv, col_send, col_recv, dec_send, dec_recv, own_sem, fwd_send, fwd_recv,
):
    core, row, col = (lax.axis_index(n) for n in ("run", "row", "col"))
    y, zh = col // 2, col % 2
    sibling = (1 - core, row, col)
    down, up = (core, (row + 1) % 8, col), (core, (row + 7) % 8, col)
    right, left = (core, row, (col + 1) % 8), (core, row, (col + 7) % 8)
    targets = [((y + dy) % 4) * 2 + (zh + dz) % 2 for dy, dz in OFFSETS]
    signal_all([(core, row, t) for t in targets] + [up, down, sibling])

    fs3 = fs.reshape(48, 64, 128)
    rows_in_field = [field.at[:, pl.ds(56, 8), :], field.at[:, pl.ds(0, 8), :]]
    rows_of_conduct = [conduct.at[pl.ds(56, 8), :], conduct.at[pl.ds(0, 8), :]]
    rr4 = rr.reshape(2, 48, 8, 128)

    def row_copies(way):
        peer = (down, up)[way]
        return [
            remote(rows_in_field[way], rr4.at[way], row_send.at[way], row_recv.at[way], peer),
            remote(
                rows_of_conduct[way], cd.at[pl.ds(72 * way, 8), :], row_send.at[2 + way], row_recv.at[2 + way], peer
            ),
        ]

    may_send = [row < 7, row > 0]
    may_get = [row > 0, row < 7]

    def each_row_copy(allowed, act):
        for way in range(2):

            @pl.when(allowed[way])
            def _():
                for c in row_copies(way):
                    act(c)

    loc_copies = [
        pltpu.make_async_copy(field, fs3, loc_sem.at[0]),
        pltpu.make_async_copy(conduct, cd.at[pl.ds(8, 64), :], loc_sem.at[1]),
    ]

    def raw_copy(part_at, slot):
        start = pl.multiple_of(part_at * 1024, 1024)
        return pltpu.make_async_copy(decoder.at[pl.ds(start, 1024), :], raw.at[slot], raw_sem.at[slot])

    mine, other = 2 * core, 2 * (1 - core)

    def turn(quarter, slot):
        def piece(hb, carry):
            at = pl.multiple_of(hb * 256, 256)
            to = pl.multiple_of(quarter * 128 + hb * 32, 32)
            for t in range(8):
                tf[t] = raw[slot, pl.ds(at, 256), t * 128 : (t + 1) * 128].astype(f32)
            for t in range(8):
                for i in range(8):
                    tr[t, i, pl.ds(to, 32), :] = tf[t, pl.ds(i, 32, stride=8), :].astype(bf16)
            return carry

        lax.fori_loop(0, 4, piece, 0)

    def dec_copies(hh, kk):
        h0 = pl.multiple_of((mine + hh) * 128, 128)
        rnd = hh * 4 + kk
        out = []
        for j, t in enumerate(targets):
            out.append(
                remote(
                    tr.at[t, pl.ds(2 * kk, 2), pl.ds(h0, 128), :],
                    dl.at[kk, pl.ds(2 * col, 2), pl.ds(h0, 128), :],
                    dec_send.at[rnd, j], dec_recv.at[rnd, j], (core, row, t),
                )
            )
        return out

    def own_copy(hh, kk):
        h0 = pl.multiple_of((mine + hh) * 128, 128)
        return pltpu.make_async_copy(
            tr.at[col, pl.ds(2 * kk, 2), pl.ds(h0, 128), :],
            dl.at[kk, pl.ds(2 * col, 2), pl.ds(h0, 128), :],
            own_sem.at[hh * 4 + kk],
        )

    def fwd_copy(hh, kk):
        h0 = pl.multiple_of((mine + hh) * 128, 128)
        block = dl.at[kk, :, pl.ds(h0, 128), :]
        return remote(block, block, fwd_send.at[hh * 4 + kk], fwd_recv.at[hh * 4 + kk], sibling)

    def send_round(hh, kk):
        for c in dec_copies(hh, kk):
            c.start()
        own_copy(hh, kk).start()

    def pass_round(hh, kk):
        for c in dec_copies(hh, kk):
            c.wait_recv()
        own_copy(hh, kk).wait()
        fwd_copy(hh, kk).start()

    each_row_copy(may_send, lambda c: c.start())
    raw_copy(mine, 0).start()
    for c in loc_copies:
        c.start()
    raw_copy(mine + 1, 1).start()
    raw_copy(mine, 0).wait()
    turn(mine, 0)
    raw_copy(other, 0).start()
    send_round(0, 0)

    for c in loc_copies:
        c.wait()
    for b in range(3):
        u[b, 0:8] = jnp.zeros((8, 2, 8, 128), f32)
        u[b, 88:96] = jnp.zeros((8, 2, 8, 128), f32)

    def fill(n, carry):
        for q in range(4):
            i = 4 * n + q
            for b in range(3):
                u[b, i + 16] = fs[pl.ds(b * 1024 + i, 16, stride=64), :].reshape(2, 8, 128)
        return carry

    lax.fori_loop(0, 16, fill, 0)

    send_round(0, 1)
    raw_copy(mine + 1, 1).wait()
    turn(mine + 1, 1)
    raw_copy(other + 1, 1).start()
    each_row_copy(may_get, lambda c: c.wait_recv())

    def unpack_rows(i, carry):
        for b in range(3):
            for way in range(2):
                u[b, i + 8 + 72 * way] = rr[way, pl.ds(b * 128 + i, 16, stride=8), :].reshape(2, 8, 128)
        return carry

    lax.fori_loop(0, 8, unpack_rows, 0)

    def fill_conduct(n, carry):
        for q in range(4):
            i = 4 * n + q
            cb[0, i + 8] = jnp.broadcast_to(cd[pl.ds(i, 1), :] * (0.5 * STEP), (8, 128))
        return carry

    lax.fori_loop(0, 20, fill_conduct, 0)
    for s in range(4):
        cb[s, 0:8] = jnp.zeros((8, 8, 128), f32)
        cb[s, 88:96] = jnp.zeros((8, 8, 128), f32)

    def clear(b):
        @pl.when(row == 0)
        def _():
            u[b, 8:16] = jnp.zeros((8, 2, 8, 128), f32)

        @pl.when(row == 7)
        def _():
            u[b, 80:88] = jnp.zeros((8, 2, 8, 128), f32)

    for b in range(3):
        clear(b)

    @pl.when(row == 0)
    def _():
        cb[0, 8:16] = jnp.zeros((8, 8, 128), f32)

    @pl.when(row == 7)
    def _():
        cb[0, 80:88] = jnp.zeros((8, 8, 128), f32)

    lane = lax.broadcasted_iota(jnp.int32, (2, 8, 128), 2)
    in32 = lane % 32

    def gather_edges(i):
        out = None
        for b in range(4):
            v = u[b, i] if b < 3 else jnp.broadcast_to(cb[0, i][None], (2, 8, 128))
            ends = pltpu.roll(v, (32 * b + 8) % 128, 2)
            starts = pltpu.roll(v, (32 * b + 24) % 128, 2)
            both = jnp.where(in32 < 8, ends, starts)
            out = both if b == 0 else jnp.where(lane // 32 == b, both, out)
        return out

    def pack(g, carry):
        to_right = to_left = None
        for q in range(4):
            o = gather_edges(4 * g + q)
            u[3, 4 * g + q] = o
            r = pltpu.roll(o, 8 * q, 2) if q else o
            l = pltpu.roll(o, (8 * q + 8) % 32 + 96 if q < 3 else 0, 2) if q < 3 else pltpu.roll(o, 0, 2)
            here = in32 // 8 == q
            to_right = r if q == 0 else jnp.where(here, r, to_right)
            to_left = l if q == 0 else jnp.where(here, l, to_left)
        xs[0, g] = to_right.reshape(16, 128).astype(bf16)
        xs[1, g] = to_left.reshape(16, 128).astype(bf16)
        return carry

    lax.fori_loop(2, GROUPS - 2, pack, 0)
    col_copies = [
        remote(xs.at[0], xr.at[0], col_send.at[0], col_recv.at[0], right),
        remote(xs.at[1], xr.at[1], col_send.at[1], col_recv.at[1], left),
    ]
    for c in col_copies:
        c.start()
    for rnd in range(2, 8):
        send_round(rnd // 4, rnd % 4)

    raw_copy(other, 0).wait()
    turn(other, 0)
    raw_copy(other + 1, 1).wait()
    turn(other + 1, 1)

    gram[...] = jnp.zeros((512, 512), f32)
    nt = (((1,), (1,)), ((), ()))

    def add_gram(t, carry):
        x = jnp.concatenate([tr[t, i] for i in range(8)], axis=1)
        gram[0:256] += lax.dot_general(x[0:256], x, nt, preferred_element_type=f32)
        gram[256:512, 256:512] += lax.dot_general(x[256:512], x[256:512], nt, preferred_element_type=f32)
        return carry

    lax.fori_loop(0, 8, add_gram, 0)
    gram[256:512, 0:256] = gram[0:256, 256:512].T
    big = gram[...].astype(bf16)
    small = (gram[...] - big.astype(f32)).astype(bf16)
    product = jnp.dot(hid[...], big, preferred_element_type=f32) + jnp.dot(
        hid[...], small, preferred_element_type=f32
    )
    for t in range(4):
        part[t] = product[:, 128 * t : 128 * t + 128]

    for c in col_copies:
        c.wait_recv()

    u[3, 0:8] = jnp.zeros((8, 2, 8, 128), f32)
    u[3, 88:96] = jnp.zeros((8, 2, 8, 128), f32)
    from_left = (in32 >= 16) & (in32 < 24)
    from_right = (in32 >= 8) & (in32 < 16)
    left_ok = (jnp.zeros((2, 8, 128), jnp.int32) + col) > 0
    right_ok = (jnp.zeros((2, 8, 128), jnp.int32) + col) < 7

    def unpack(g, carry):
        gl = xr[0, g].astype(f32).reshape(2, 8, 128)
        gr = xr[1, g].astype(f32).reshape(2, 8, 128)
        for q in range(4):
            o = u[3, 4 * g + q]
            a = pltpu.roll(gl, (16 - 8 * q) % 128, 2)
            c = pltpu.roll(gr, (8 - 8 * q) % 128, 2)
            o = jnp.where(from_left, jnp.where(left_ok, a, 0.0), o)
            o = jnp.where(from_right, jnp.where(right_ok, c, 0.0), o)
            u[3, 4 * g + q] = o
            k = o[0]
            for b in range(3):
                k = jnp.where(lane[0] // 32 == b, pltpu.roll(o[0], 32 * (b + 1), 1), k)
            cb[2, 4 * g + q] = jnp.where(lane[0] < 96, k, 0.0)
        return carry

    lax.fori_loop(2, GROUPS - 2, unpack, 0)
    clear(3)

    @pl.when(row == 0)
    def _():
        cb[2, 8:16] = jnp.zeros((8, 8, 128), f32)

    @pl.when(row == 7)
    def _():
        cb[2, 80:88] = jnp.zeros((8, 8, 128), f32)

    def shift_conduct(g, carry):
        for q in range(4):
            for side in (0, 2):
                cb[side + 1, 4 * g + q] = pltpu.roll(cb[side, 4 * g + q], 127, 1)
        return carry

    lax.fori_loop(2, GROUPS - 2, shift_conduct, 0)
    first, last = lane == 0, lane == 127

    def run_step(s, with_main):
        blocks = (0, 1, 2, 3) if with_main else (3,)
        count = range(len(blocks))
        ahead_s = s + 1 if with_main else s
        coef = [nl[b] for b in blocks]
        active = [jnp.where(cnt[b] > (s if b < 3 else ahead_s), 1.0, 0.0).astype(f32) for b in blocks]
        begin = (9 + s) // 4

        def kappa(v, i, n, shifted=0):
            return cb[(2 if blocks[n] == 3 else 0) + shifted, i][None] / (1.0 + coef[n] * v * v)

        def ahead(i, vs):
            out = []
            for n, b in enumerate(blocks):
                v = vs[n]
                k = kappa(v, i, n)
                vr = pltpu.roll(v, 127, 2)
                across = (k + kappa(vr, i, n, 1)) * (vr - v)
                if b < 3:
                    across = jnp.where(last, fx[b, s % 2, i], across)
                out.append((k, across))
            return out

        def keep(g, q, made):
            for n, (k, across) in enumerate(made):
                ks[blocks[n], (g % 2) * 4 + q] = k
                ac[blocks[n], (g % 2) * 4 + q] = across

        flows = []
        for q in range(4):
            vs = [u[b, 4 * begin + q] for b in blocks]
            made = ahead(4 * begin + q, vs)
            keep(begin, q, made)
            if q == 0:
                for n, b in enumerate(blocks):
                    before = u[b, 4 * begin - 1]
                    flows.append((made[n][0] + kappa(before, 4 * begin - 1, n)) * (vs[n] - before))

        def group(g, flow):
            flow = list(flow)
            base, now = 4 * g, (g % 2) * 4
            v = [[u[b, base + q] for b in blocks] for q in range(4)]
            k = [[ks[b, now + q] for b in blocks] for q in range(4)]
            a = [[ac[b, now + q] for b in blocks] for q in range(4)]
            v_next = [[u[b, base + 4 + q] for b in blocks] for q in range(4)]
            first_made = None
            for q in range(4):
                made = ahead(base + 4 + q, v_next[q])
                first_made = made if q == 0 else first_made
                for n, b in enumerate(blocks):
                    vn = v[q + 1][n] if q < 3 else v_next[0][n]
                    kn = k[q + 1][n] if q < 3 else first_made[n][0]
                    flow_n = (k[q][n] + kn) * (vn - v[q][n])
                    came = pltpu.roll(a[q][n], 1, 2)
                    if b == 3:
                        f = jnp.where(in32 == 8, pltpu.roll(a[q][n], 113, 2), a[q][n])
                        for to in range(3):
                            fx[to, ahead_s % 2, base + q] = pltpu.roll(f, 120 - 32 * to, 2)
                    else:
                        came = jnp.where(first, fx[b, s % 2, base + q], came)
                    new = v[q][n] + active[n] * ((flow_n - flow[n]) + (a[q][n] - came))
                    u[b, base + q] = new
                    if b < 3:
                        snap[2 * (g % 2) + q // 2, 2 * (g // 2) - 2 + q % 2, s, 16 * b : 16 * b + 16, :] = (
                            new.reshape(16, 128).astype(bf16)
                        )
                    flow[n] = flow_n
                keep(g + 1, q, made)
            return tuple(flow)

        lax.fori_loop(begin, GROUPS - begin, group, tuple(flows))
        for b in blocks:
            clear(b)

    pass_round(0, 0)
    pass_round(0, 1)
    run_step(0, False)

    def one_step(s, carry):
        run_step(s, True)
        for at, hh, kk in ((0, 0, 2), (1, 0, 3), (2, 1, 0), (4, 1, 1), (6, 1, 2)):

            @pl.when(s == at)
            def _():
                pass_round(hh, kk)

        return carry

    lax.fori_loop(0, 8, one_step, 0)

    def give_back(n, carry):
        for q in range(4):
            for b in range(3):
                fs[pl.ds(b * 1024 + 4 * n + q, 16, stride=64), :] = u[b, 4 * n + q + 16].reshape(16, 128)
        return carry

    lax.fori_loop(0, 16, give_back, 0)
    out_copy = pltpu.make_async_copy(fs3, final, loc_sem.at[2])
    out_copy.start()
    pass_round(1, 3)

    def square(n, total):
        x = snap[n // 16, 2 + n % 16].astype(f32).reshape(48, 8, 128)
        return total + jnp.sum(x * x, axis=0)

    squares = lax.fori_loop(0, 64, square, jnp.zeros((8, 128), f32))

    for hh in range(2):
        for kk in range(4):
            fwd_copy(hh, kk).wait_recv()

            lhs = jnp.concatenate([snap[kk, 2 + i].reshape(384, 128) for i in range(16)], axis=1)
            rhs = jnp.concatenate(
                [
                    jnp.concatenate(
                        [
                            dl[kk, i, 128 * hh : 128 * hh + 128, :],
                            dl[kk, i, 256 + 128 * hh : 384 + 128 * hh, :],
                        ],
                        axis=0,
                    )
                    for i in range(16)
                ],
                axis=1,
            )
            got = lax.dot_general(lhs, rhs, nt, preferred_element_type=f32)
            acc[hh] = got if kk == 0 else acc[hh] + got

    total = squares
    for hh in range(2):
        for half in range(2):
            at = slice(256 * half + 128 * hh, 256 * half + 128 * hh + 128)
            a = part[2 * half + hh]
            c = acc[hh, :, 128 * half : 128 * half + 128]
            part[2 * half + hh] = a - c
            total = total + jnp.sum((hid[:, at].astype(f32) * (a - 2.0 * c)).reshape(48, 8, 128), axis=0)
    loss[...] = total

    out_copy.wait()
    each_row_copy(may_send, lambda c: c.wait_send())
    for c in col_copies:
        c.wait_send()
    for hh in range(2):
        for kk in range(4):
            for c in dec_copies(hh, kk):
                c.wait_send()
            fwd_copy(hh, kk).wait_send()


def reduce_kernel(part, loss_in, grad, loss_out, r1, l1, l2, got, send1, recv1, send2, recv2, lsend, lrecv, lsend2, xsend, xrecv):
    core, row, col = (lax.axis_index(n) for n in ("run", "row", "col"))
    x, y, z = row % 4, col // 2, (col % 2) * 2 + row // 4
    sibling = (1 - core, row, col)
    me = row * 8 + col

    def chip(j):
        x1, y1, z1 = (x + j % 4) % 4, (y + j // 4 % 4) % 4, (z + j // 16) % 4
        return (z1 % 2) * 4 + x1, y1 * 2 + z1 // 2

    offsets = list(range(1, 64))
    offsets.sort(key=lambda j: -sum(min(d, 4 - d) for d in (j % 4, j // 4 % 4, j // 16)))
    peers = [(core, *chip(j)) for j in offsets]
    signal_all(peers + [sibling])

    def piece(p):
        return part.at[p // 16, pl.ds(pl.multiple_of(24 * (p % 16), 8), 24), :]

    first = []
    for n, j in enumerate(offsets):
        r, c = chip(j)
        first.append(remote(piece(r * 8 + c), r1.at[n], send1.at[n], recv1.at[n], peers[n]))
    to_zero = remote(loss_in, l1.at[me], lsend, lrecv.at[me], (core, 0, 0))

    @pl.when(me > 0)
    def _():
        to_zero.start()

    for c in first:
        c.start()
    total = part[me // 16, pl.ds(pl.multiple_of(24 * (me % 16), 8), 24), :]
    for n, c in enumerate(first):
        c.wait_recv()
        total = total + r1[n]
    got[core, me] = jnp.concatenate([total * (1.0 / 768.0), jnp.zeros((8, 128), f32)], axis=0).astype(bf16)

    second = [remote(got.at[core, me], got.at[core, me], send2.at[n], recv2.at[n], peers[n]) for n in range(63)]
    for c in second:
        c.start()
    spread_loss = [remote(l2.at[core], l2.at[core], lsend2.at[n], lrecv.at[64], peers[n]) for n in range(63)]

    @pl.when(me == 0)
    def _():
        sums = loss_in[...]
        for p in range(1, 64):
            remote(loss_in, l1.at[p], lsend, lrecv.at[p], (core, 0, 0)).wait_recv()
            sums = sums + l1[p]
        l2[core] = sums
        for c in spread_loss:
            c.start()

    for c in second:
        c.wait_recv()
    cross = remote(got.at[core], got.at[core], xsend.at[0], xrecv.at[0], sibling)
    cross.start()

    @pl.when(me > 0)
    def _():
        spread_loss[0].wait_recv()

    cross_loss = remote(l2.at[core], l2.at[core], xsend.at[1], xrecv.at[1], sibling)
    cross_loss.start()

    def place(own):
        for t in range(4):
            for q in range(8):
                pair = jnp.concatenate(
                    [got[own, 16 * t + 2 * q + i].astype(f32)[0:24] for i in range(2)], axis=0
                ).astype(bf16)
                grad[own, 48 * q : 48 * q + 48, 128 * t : 128 * t + 128] = pair

    place(core)
    cross.wait_recv()
    place(1 - core)
    cross_loss.wait_recv()
    loss_out[...] = l2[0] + l2[1]

    @pl.when(me > 0)
    def _():
        to_zero.wait_send()

    @pl.when(me == 0)
    def _():
        for c in spread_loss:
            c.wait_send()

    for c in first + second + [cross, cross_loss]:
        c.wait_send()


def spread(values):
    three = values.reshape(3, 16)
    wide = jnp.broadcast_to(three[:, :, None], (3, 16, 128))
    edge = jnp.concatenate(
        [jnp.broadcast_to(three[b][:, None], (16, 32)) for b in range(3)] + [jnp.zeros((16, 32), values.dtype)],
        axis=1,
    )
    return jnp.concatenate([wide, edge[None]], axis=0).reshape(4, 2, 8, 128)


def per_device(
    init_field, conduct, nonlin, counts, descriptors, time_code, w_in, bias_in, w_out, decoder
):
    core = lax.axis_index("run")
    col = lax.axis_index("col")
    wide = descriptors.astype(f32).reshape(2, 1, 48, 256) + time_code.astype(f32).reshape(1, 8, 1, 256)
    rows_in = wide.astype(bf16).reshape(768, 256)
    pre = jnp.dot(rows_in, w_in, preferred_element_type=f32) + bias_in
    act = jax.nn.gelu(pre).astype(bf16)
    hidden = jnp.dot(act, w_out, preferred_element_type=f32).astype(bf16)
    hid = lax.dynamic_slice_in_dim(hidden, core * 384, 384, 0)

    lanes = jnp.arange(128) % 32
    outside = ((lanes >= 16) & (lanes < 24) & (col == 0)) | ((lanes >= 8) & (lanes < 16) & (col == 7))
    cnt = spread(counts)
    cnt = cnt.at[3].set(jnp.where(outside[None, None, :], 0, cnt[3]))
    vmem = pl.BlockSpec(memory_space=pltpu.VMEM)
    hbm = pl.BlockSpec(memory_space=pl.ANY)
    dma = pltpu.SemaphoreType.DMA
    final, part, loss = pl.pallas_call(
        main_kernel,
        name="solve_and_learn",
        out_shape=(
            jax.ShapeDtypeStruct((48, 64, 128), f32),
            jax.ShapeDtypeStruct((4, 384, 128), f32),
            jax.ShapeDtypeStruct((8, 128), f32),
        ),
        in_specs=[hbm, hbm, vmem, vmem, hbm, vmem],
        out_specs=(hbm, vmem, vmem),
        scratch_shapes=[
            pltpu.VMEM((3072, 128), f32),
            pltpu.VMEM((80, 128), f32),
            pltpu.VMEM((4, ROWS, 2, 8, 128), f32),
            pltpu.VMEM((4, ROWS, 8, 128), f32),
            pltpu.VMEM((2, 384, 128), f32),
            pltpu.VMEM((2, GROUPS, 16, 128), bf16),
            pltpu.VMEM((2, GROUPS, 16, 128), bf16),
            pltpu.VMEM((3, 2, ROWS, 2, 8, 128), f32),
            pltpu.VMEM((4, 8, 2, 8, 128), f32),
            pltpu.VMEM((4, 8, 2, 8, 128), f32),
            pltpu.VMEM((4, 20, 8, 48, 128), bf16),
            pltpu.VMEM((8, 8, 512, 128), bf16),
            pltpu.VMEM((4, 16, 512, 128), bf16),
            pltpu.VMEM((2, 1024, 1024), bf16),
            pltpu.VMEM((8, 256, 128), f32),
            pltpu.VMEM((512, 512), f32),
            pltpu.VMEM((2, 384, 256), f32),
            dma((3,)), dma((2,)), dma((4,)), dma((4,)), dma((2,)), dma((2,)),
            dma((8, 7)), dma((8, 7)), dma((8,)), dma((8,)), dma((8,)),
        ],
        compiler_params=pltpu.CompilerParams(
            collective_id=0, has_side_effects=True, vmem_limit_bytes=VMEM_ALL - (1 << 16)
        ),
    )(init_field, conduct, spread(nonlin), cnt, decoder.reshape(4096, 1024), hid)

    grad, loss_sum = pl.pallas_call(
        reduce_kernel,
        name="reduce_grad",
        out_shape=(jax.ShapeDtypeStruct((2, 384, 512), bf16), jax.ShapeDtypeStruct((8, 128), f32)),
        in_specs=[vmem, vmem],
        out_specs=(vmem, vmem),
        scratch_shapes=[
            pltpu.VMEM((63, 24, 128), f32),
            pltpu.VMEM((64, 8, 128), f32),
            pltpu.VMEM((2, 8, 128), f32),
            pltpu.VMEM((2, 64, 32, 128), bf16),
            dma((63,)), dma((63,)), dma((63,)), dma((63,)), dma(()), dma((65,)), dma((63,)), dma((2,)), dma((2,)),
        ],
        compiler_params=pltpu.CompilerParams(collective_id=1, has_side_effects=True),
    )(part, loss)
    grad = grad.reshape(768, 512)

    grad_out = lax.dot_general(act, grad, (((0,), (0,)), ((), ())), preferred_element_type=f32)
    back = lax.dot_general(grad, w_out, (((1,), (1,)), ((), ())), preferred_element_type=f32)
    _, pull = jax.vjp(jax.nn.gelu, pre)
    grad_pre = pull(back)[0]
    grad_in = lax.dot_general(
        rows_in, grad_pre.astype(bf16), (((0,), (0,)), ((), ())), preferred_element_type=f32
    )
    new_w_in = w_in.astype(f32) - RATE * grad_in
    new_bias = bias_in - RATE * jnp.sum(grad_pre, axis=0)
    new_w_out = w_out.astype(f32) - RATE * grad_out
    mean_loss = jnp.sum(loss_sum) / (768 * 512 * 1024)
    return final, new_w_in, new_bias, new_w_out, mean_loss


def solution(mesh):
    in_specs = (
        P("run", "row", "col"), P("row", "col"), P("run"), P("run"), P(), P(), P(), P(), P(),
        P(None, ("row", "col"), None),
    )
    out_specs = (P("run", "row", "col"), P(), P(), P(), P())
    return jax.shard_map(
        per_device, mesh=mesh, in_specs=in_specs, out_specs=out_specs, check_vma=False
    )
```

```python
import jax
import jax.numpy as jnp
from jax import lax
from jax.experimental import pallas as pl
from jax.experimental.pallas import tpu as pltpu
from jax.sharding import PartitionSpec as P

MESH = pl.DeviceIdType.MESH
f32, bf16 = jnp.float32, jnp.bfloat16
STEP, RATE = 0.12, 0.5
ROWS = 96
GROUPS = ROWS // 4
OFFSETS = ((2, 1), (1, 1), (3, 1), (2, 0), (0, 1), (1, 0), (3, 0))
VMEM_ALL = 64 << 20


def signal_all(peers):
    barrier = pltpu.get_barrier_semaphore()
    for peer in peers:
        pl.semaphore_signal(barrier, inc=1, device_id=peer, device_id_type=MESH)
    pl.semaphore_wait(barrier, len(peers))


def remote(src, dst, send, recv, peer):
    return pltpu.make_async_remote_copy(
        src_ref=src, dst_ref=dst, send_sem=send, recv_sem=recv, device_id=peer, device_id_type=MESH
    )


def main_kernel(
    field, conduct, nl, cnt, decoder, hid,
    final, part, loss,
    fs, cd, u, cb, rs, rr, xs, xr, fx, ks, ac, snap, tr, dl, raw, tf, gram, acc,
    loc_sem, raw_sem, row_send, row_recv, col_send, col_recv, dec_send, dec_recv, own_sem, fwd_send, fwd_recv,
):
    core, row, col = (lax.axis_index(n) for n in ("run", "row", "col"))
    y, zh = col // 2, col % 2
    sibling = (1 - core, row, col)
    down, up = (core, (row + 1) % 8, col), (core, (row + 7) % 8, col)
    right, left = (core, row, (col + 1) % 8), (core, row, (col + 7) % 8)
    targets = [((y + dy) % 4) * 2 + (zh + dz) % 2 for dy, dz in OFFSETS]
    signal_all([(core, row, t) for t in targets] + [up, down, sibling])

    fs3 = fs.reshape(48, 64, 128)
    rows_of_conduct = [conduct.at[pl.ds(56, 8), :], conduct.at[pl.ds(0, 8), :]]

    def row_copies(way):
        peer = (down, up)[way]
        return [
            remote(rs.at[way], rr.at[way], row_send.at[way], row_recv.at[way], peer),
            remote(
                rows_of_conduct[way], cd.at[pl.ds(72 * way, 8), :], row_send.at[2 + way], row_recv.at[2 + way], peer
            ),
        ]

    may_send = [row < 7, row > 0]
    may_get = [row > 0, row < 7]

    def each_row_copy(allowed, act):
        for way in range(2):

            @pl.when(allowed[way])
            def _():
                for c in row_copies(way):
                    act(c)

    loc_copies = [
        pltpu.make_async_copy(field, fs3, loc_sem.at[0]),
        pltpu.make_async_copy(conduct, cd.at[pl.ds(8, 64), :], loc_sem.at[1]),
    ]

    def raw_copy(part_at, slot):
        start = pl.multiple_of(part_at * 1024, 1024)
        return pltpu.make_async_copy(decoder.at[pl.ds(start, 1024), :], raw.at[slot], raw_sem.at[slot])

    mine, other = 2 * core, 2 * (1 - core)

    def turn(quarter, slot):
        def piece(hb, carry):
            at = pl.multiple_of(hb * 256, 256)
            to = pl.multiple_of(quarter * 128 + hb * 32, 32)
            for t in range(8):
                tf[t] = raw[slot, pl.ds(at, 256), t * 128 : (t + 1) * 128].astype(f32)
            for t in range(8):
                for i in range(8):
                    tr[t, i, pl.ds(to, 32), :] = tf[t, pl.ds(i, 32, stride=8), :].astype(bf16)
            return carry

        lax.fori_loop(0, 4, piece, 0)

    def dec_copies(hh, kk):
        h0 = pl.multiple_of((mine + hh) * 128, 128)
        rnd = hh * 4 + kk
        out = []
        for j, t in enumerate(targets):
            out.append(
                remote(
                    tr.at[t, pl.ds(2 * kk, 2), pl.ds(h0, 128), :],
                    dl.at[kk, pl.ds(2 * col, 2), pl.ds(h0, 128), :],
                    dec_send.at[rnd, j], dec_recv.at[rnd, j], (core, row, t),
                )
            )
        return out

    def own_copy(hh, kk):
        h0 = pl.multiple_of((mine + hh) * 128, 128)
        return pltpu.make_async_copy(
            tr.at[col, pl.ds(2 * kk, 2), pl.ds(h0, 128), :],
            dl.at[kk, pl.ds(2 * col, 2), pl.ds(h0, 128), :],
            own_sem.at[hh * 4 + kk],
        )

    def fwd_copy(hh, kk):
        h0 = pl.multiple_of((mine + hh) * 128, 128)
        block = dl.at[kk, :, pl.ds(h0, 128), :]
        return remote(block, block, fwd_send.at[hh * 4 + kk], fwd_recv.at[hh * 4 + kk], sibling)

    def send_round(hh, kk):
        for c in dec_copies(hh, kk):
            c.start()
        own_copy(hh, kk).start()

    def pass_round(hh, kk):
        for c in dec_copies(hh, kk):
            c.wait_recv()
        own_copy(hh, kk).wait()
        fwd_copy(hh, kk).start()

    for c in loc_copies:
        c.start()
    raw_copy(mine, 0).start()
    raw_copy(mine + 1, 1).start()
    for c in loc_copies:
        c.wait()

    def pack_rows(i, carry):
        for b in range(3):
            for way in range(2):
                rs[way, i, b] = fs[pl.ds(b * 1024 + i + 56 * (1 - way), 16, stride=64), :].astype(bf16)
        return carry

    lax.fori_loop(0, 8, pack_rows, 0)
    each_row_copy(may_send, lambda c: c.start())
    raw_copy(mine, 0).wait()
    turn(mine, 0)
    raw_copy(other, 0).start()
    send_round(0, 0)

    for b in range(3):
        u[b, 0:8] = jnp.zeros((8, 2, 8, 128), f32)
        u[b, 88:96] = jnp.zeros((8, 2, 8, 128), f32)

    def fill(n, carry):
        for q in range(4):
            i = 4 * n + q
            for b in range(3):
                u[b, i + 16] = fs[pl.ds(b * 1024 + i, 16, stride=64), :].reshape(2, 8, 128)
        return carry

    lax.fori_loop(0, 16, fill, 0)

    each_row_copy(may_get, lambda c: c.wait_recv())

    def unpack_rows(i, carry):
        for b in range(3):
            for way in range(2):
                u[b, i + 8 + 72 * way] = rr[way, i, b].astype(f32).reshape(2, 8, 128)
        return carry

    lax.fori_loop(0, 8, unpack_rows, 0)

    def fill_conduct(n, carry):
        for q in range(4):
            i = 4 * n + q
            cb[0, i + 8] = jnp.broadcast_to(cd[pl.ds(i, 1), :] * (0.5 * STEP), (8, 128))
        return carry

    lax.fori_loop(0, 20, fill_conduct, 0)
    for s in range(4):
        cb[s, 0:8] = jnp.zeros((8, 8, 128), f32)
        cb[s, 88:96] = jnp.zeros((8, 8, 128), f32)

    def clear(b):
        @pl.when(row == 0)
        def _():
            u[b, 8:16] = jnp.zeros((8, 2, 8, 128), f32)

        @pl.when(row == 7)
        def _():
            u[b, 80:88] = jnp.zeros((8, 2, 8, 128), f32)

    for b in range(3):
        clear(b)

    @pl.when(row == 0)
    def _():
        cb[0, 8:16] = jnp.zeros((8, 8, 128), f32)

    @pl.when(row == 7)
    def _():
        cb[0, 80:88] = jnp.zeros((8, 8, 128), f32)

    lane = lax.broadcasted_iota(jnp.int32, (2, 8, 128), 2)
    in32 = lane % 32

    def gather_edges(i):
        out = None
        for b in range(4):
            v = u[b, i] if b < 3 else jnp.broadcast_to(cb[0, i][None], (2, 8, 128))
            ends = pltpu.roll(v, (32 * b + 8) % 128, 2)
            starts = pltpu.roll(v, (32 * b + 24) % 128, 2)
            both = jnp.where(in32 < 8, ends, starts)
            out = both if b == 0 else jnp.where(lane // 32 == b, both, out)
        return out

    def pack(g, carry):
        to_right = to_left = None
        for q in range(4):
            o = gather_edges(4 * g + q)
            u[3, 4 * g + q] = o
            r = pltpu.roll(o, 8 * q, 2) if q else o
            l = pltpu.roll(o, (8 * q + 8) % 32 + 96 if q < 3 else 0, 2) if q < 3 else pltpu.roll(o, 0, 2)
            here = in32 // 8 == q
            to_right = r if q == 0 else jnp.where(here, r, to_right)
            to_left = l if q == 0 else jnp.where(here, l, to_left)
        xs[0, g] = to_right.reshape(16, 128).astype(bf16)
        xs[1, g] = to_left.reshape(16, 128).astype(bf16)
        return carry

    lax.fori_loop(2, GROUPS - 2, pack, 0)
    col_copies = [
        remote(xs.at[0, pl.ds(2, 20)], xr.at[0, pl.ds(2, 20)], col_send.at[0], col_recv.at[0], right),
        remote(xs.at[1, pl.ds(2, 20)], xr.at[1, pl.ds(2, 20)], col_send.at[1], col_recv.at[1], left),
    ]
    for c in col_copies:
        c.start()
    raw_copy(mine + 1, 1).wait()
    turn(mine + 1, 1)
    raw_copy(other + 1, 1).start()
    raw_copy(other, 0).wait()
    turn(other, 0)
    for rnd in range(1, 8):
        send_round(rnd // 4, rnd % 4)
    raw_copy(other + 1, 1).wait()
    turn(other + 1, 1)

    gram[...] = jnp.zeros((512, 512), f32)
    nt = (((1,), (1,)), ((), ()))

    def add_gram(t, carry):
        x = jnp.concatenate([tr[t, i] for i in range(8)], axis=1)
        gram[0:256] += lax.dot_general(x[0:256], x, nt, preferred_element_type=f32)
        gram[256:512, 256:512] += lax.dot_general(x[256:512], x[256:512], nt, preferred_element_type=f32)
        return carry

    lax.fori_loop(0, 8, add_gram, 0)
    gram[256:512, 0:256] = gram[0:256, 256:512].T
    big = gram[...].astype(bf16)
    small = (gram[...] - big.astype(f32)).astype(bf16)
    product = jnp.dot(hid[...], big, preferred_element_type=f32) + jnp.dot(
        hid[...], small, preferred_element_type=f32
    )
    for t in range(4):
        part[t] = product[:, 128 * t : 128 * t + 128]

    for c in col_copies:
        c.wait_recv()

    u[3, 0:8] = jnp.zeros((8, 2, 8, 128), f32)
    u[3, 88:96] = jnp.zeros((8, 2, 8, 128), f32)
    from_left = (in32 >= 16) & (in32 < 24)
    from_right = (in32 >= 8) & (in32 < 16)
    left_ok = (jnp.zeros((2, 8, 128), jnp.int32) + col) > 0
    right_ok = (jnp.zeros((2, 8, 128), jnp.int32) + col) < 7

    def unpack(g, carry):
        gl = xr[0, g].astype(f32).reshape(2, 8, 128)
        gr = xr[1, g].astype(f32).reshape(2, 8, 128)
        for q in range(4):
            o = u[3, 4 * g + q]
            a = pltpu.roll(gl, (16 - 8 * q) % 128, 2)
            c = pltpu.roll(gr, (8 - 8 * q) % 128, 2)
            o = jnp.where(from_left, jnp.where(left_ok, a, 0.0), o)
            o = jnp.where(from_right, jnp.where(right_ok, c, 0.0), o)
            u[3, 4 * g + q] = o
            k = o[0]
            for b in range(3):
                k = jnp.where(lane[0] // 32 == b, pltpu.roll(o[0], 32 * (b + 1), 1), k)
            cb[2, 4 * g + q] = jnp.where(lane[0] < 96, k, 0.0)
        return carry

    lax.fori_loop(2, GROUPS - 2, unpack, 0)
    clear(3)

    @pl.when(row == 0)
    def _():
        cb[2, 8:16] = jnp.zeros((8, 8, 128), f32)

    @pl.when(row == 7)
    def _():
        cb[2, 80:88] = jnp.zeros((8, 8, 128), f32)

    def shift_conduct(g, carry):
        for q in range(4):
            for side in (0, 2):
                cb[side + 1, 4 * g + q] = pltpu.roll(cb[side, 4 * g + q], 127, 1)
        return carry

    lax.fori_loop(2, GROUPS - 2, shift_conduct, 0)
    first, last = lane == 0, lane == 127

    def run_step(s, with_main):
        blocks = (0, 1, 2, 3) if with_main else (3,)
        count = range(len(blocks))
        ahead_s = s + 1 if with_main else s
        coef = [nl[b] for b in blocks]
        active = [jnp.where(cnt[b] > (s if b < 3 else ahead_s), 1.0, 0.0).astype(f32) for b in blocks]
        begin = (9 + s) // 4

        def kappa(v, i, n, shifted=0):
            return cb[(2 if blocks[n] == 3 else 0) + shifted, i][None] / (1.0 + coef[n] * v * v)

        def ahead(i, vs):
            out = []
            for n, b in enumerate(blocks):
                v = vs[n]
                k = kappa(v, i, n)
                vr = pltpu.roll(v, 127, 2)
                across = (k + kappa(vr, i, n, 1)) * (vr - v)
                if b < 3:
                    across = jnp.where(last, fx[b, s % 2, i], across)
                out.append((k, across))
            return out

        def keep(g, q, made):
            for n, (k, across) in enumerate(made):
                ks[blocks[n], (g % 2) * 4 + q] = k
                ac[blocks[n], (g % 2) * 4 + q] = across

        flows = []
        for q in range(4):
            vs = [u[b, 4 * begin + q] for b in blocks]
            made = ahead(4 * begin + q, vs)
            keep(begin, q, made)
            if q == 0:
                for n, b in enumerate(blocks):
                    before = u[b, 4 * begin - 1]
                    flows.append((made[n][0] + kappa(before, 4 * begin - 1, n)) * (vs[n] - before))

        def group(g, flow):
            flow = list(flow)
            base, now = 4 * g, (g % 2) * 4
            v = [[u[b, base + q] for b in blocks] for q in range(4)]
            k = [[ks[b, now + q] for b in blocks] for q in range(4)]
            a = [[ac[b, now + q] for b in blocks] for q in range(4)]
            v_next = [[u[b, base + 4 + q] for b in blocks] for q in range(4)]
            first_made = None
            for q in range(4):
                made = ahead(base + 4 + q, v_next[q])
                first_made = made if q == 0 else first_made
                for n, b in enumerate(blocks):
                    vn = v[q + 1][n] if q < 3 else v_next[0][n]
                    kn = k[q + 1][n] if q < 3 else first_made[n][0]
                    flow_n = (k[q][n] + kn) * (vn - v[q][n])
                    came = pltpu.roll(a[q][n], 1, 2)
                    if b == 3:
                        f = jnp.where(in32 == 8, pltpu.roll(a[q][n], 113, 2), a[q][n])
                        for to in range(3):
                            fx[to, ahead_s % 2, base + q] = pltpu.roll(f, 120 - 32 * to, 2)
                    else:
                        came = jnp.where(first, fx[b, s % 2, base + q], came)
                    new = v[q][n] + active[n] * ((flow_n - flow[n]) + (a[q][n] - came))
                    u[b, base + q] = new
                    if b < 3:
                        snap[2 * (g % 2) + q // 2, 2 * (g // 2) - 2 + q % 2, s, 16 * b : 16 * b + 16, :] = (
                            new.reshape(16, 128).astype(bf16)
                        )
                    flow[n] = flow_n
                keep(g + 1, q, made)
            return tuple(flow)

        lax.fori_loop(begin, GROUPS - begin, group, tuple(flows))
        for b in blocks:
            clear(b)

    pass_round(0, 0)
    run_step(0, False)

    def one_step(s, carry):
        run_step(s, True)
        for at, hh, kk in ((0, 0, 1), (1, 0, 2), (3, 0, 3), (4, 1, 0), (5, 1, 1), (6, 1, 2)):

            @pl.when(s == at)
            def _():
                pass_round(hh, kk)

        return carry

    lax.fori_loop(0, 8, one_step, 0)

    pass_round(1, 3)

    def give_back(n, carry):
        for q in range(4):
            for b in range(3):
                fs[pl.ds(b * 1024 + 4 * n + q, 16, stride=64), :] = u[b, 4 * n + q + 16].reshape(16, 128)
        return carry

    lax.fori_loop(0, 16, give_back, 0)
    out_copy = pltpu.make_async_copy(fs3, final, loc_sem.at[2])
    out_copy.start()

    def square(n, total):
        x = snap[n // 16, 2 + n % 16].astype(f32).reshape(48, 8, 128)
        return total + jnp.sum(x * x, axis=0)

    squares = lax.fori_loop(0, 64, square, jnp.zeros((8, 128), f32))

    for hh in range(2):
        for kk in range(4):
            fwd_copy(hh, kk).wait_recv()

            lhs = jnp.concatenate([snap[kk, 2 + i].reshape(384, 128) for i in range(16)], axis=1)
            rhs = jnp.concatenate(
                [
                    jnp.concatenate(
                        [
                            dl[kk, i, 128 * hh : 128 * hh + 128, :],
                            dl[kk, i, 256 + 128 * hh : 384 + 128 * hh, :],
                        ],
                        axis=0,
                    )
                    for i in range(16)
                ],
                axis=1,
            )
            got = lax.dot_general(lhs, rhs, nt, preferred_element_type=f32)
            acc[hh] = got if kk == 0 else acc[hh] + got

    total = squares
    for hh in range(2):
        for half in range(2):
            at = slice(256 * half + 128 * hh, 256 * half + 128 * hh + 128)
            a = part[2 * half + hh]
            c = acc[hh, :, 128 * half : 128 * half + 128]
            part[2 * half + hh] = a - c
            total = total + jnp.sum((hid[:, at].astype(f32) * (a - 2.0 * c)).reshape(48, 8, 128), axis=0)
    loss[...] = total

    out_copy.wait()
    each_row_copy(may_send, lambda c: c.wait_send())
    for c in col_copies:
        c.wait_send()
    for hh in range(2):
        for kk in range(4):
            for c in dec_copies(hh, kk):
                c.wait_send()
            fwd_copy(hh, kk).wait_send()


def reduce_kernel(part, loss_in, grad, loss_out, r1, l1, l2, got, send1, recv1, send2, recv2, lsend, lrecv, lsend2, xsend, xrecv):
    core, row, col = (lax.axis_index(n) for n in ("run", "row", "col"))
    x, y, z = row % 4, col // 2, (col % 2) * 2 + row // 4
    sibling = (1 - core, row, col)
    me = row * 8 + col

    def chip(j):
        x1, y1, z1 = (x + j % 4) % 4, (y + j // 4 % 4) % 4, (z + j // 16) % 4
        return (z1 % 2) * 4 + x1, y1 * 2 + z1 // 2

    offsets = list(range(1, 64))
    offsets.sort(key=lambda j: -sum(min(d, 4 - d) for d in (j % 4, j // 4 % 4, j // 16)))
    peers = [(core, *chip(j)) for j in offsets]
    signal_all(peers + [sibling])

    def piece(p):
        return part.at[p // 16, pl.ds(pl.multiple_of(24 * (p % 16), 8), 24), :]

    first = []
    for n, j in enumerate(offsets):
        r, c = chip(j)
        first.append(remote(piece(r * 8 + c), r1.at[n], send1.at[n], recv1.at[n], peers[n]))
    to_zero = remote(loss_in, l1.at[me], lsend, lrecv.at[me], (core, 0, 0))

    @pl.when(me > 0)
    def _():
        to_zero.start()

    for c in first:
        c.start()
    total = part[me // 16, pl.ds(pl.multiple_of(24 * (me % 16), 8), 24), :]
    for n, c in enumerate(first):
        c.wait_recv()
        total = total + r1[n]
    got[core, me] = jnp.concatenate([total * (1.0 / 768.0), jnp.zeros((8, 128), f32)], axis=0).astype(bf16)

    second = [remote(got.at[core, me], got.at[core, me], send2.at[n], recv2.at[n], peers[n]) for n in range(63)]
    for c in second:
        c.start()
    spread_loss = [remote(l2.at[core], l2.at[core], lsend2.at[n], lrecv.at[64], peers[n]) for n in range(63)]

    @pl.when(me == 0)
    def _():
        sums = loss_in[...]
        for p in range(1, 64):
            remote(loss_in, l1.at[p], lsend, lrecv.at[p], (core, 0, 0)).wait_recv()
            sums = sums + l1[p]
        l2[core] = sums
        for c in spread_loss:
            c.start()

    for c in second:
        c.wait_recv()
    cross = remote(got.at[core], got.at[core], xsend.at[0], xrecv.at[0], sibling)
    cross.start()

    @pl.when(me > 0)
    def _():
        spread_loss[0].wait_recv()

    cross_loss = remote(l2.at[core], l2.at[core], xsend.at[1], xrecv.at[1], sibling)
    cross_loss.start()

    def place(own):
        for t in range(4):
            for q in range(8):
                pair = jnp.concatenate(
                    [got[own, 16 * t + 2 * q + i].astype(f32)[0:24] for i in range(2)], axis=0
                ).astype(bf16)
                grad[own, 48 * q : 48 * q + 48, 128 * t : 128 * t + 128] = pair

    place(core)
    cross.wait_recv()
    place(1 - core)
    cross_loss.wait_recv()
    loss_out[...] = l2[0] + l2[1]

    @pl.when(me > 0)
    def _():
        to_zero.wait_send()

    @pl.when(me == 0)
    def _():
        for c in spread_loss:
            c.wait_send()

    for c in first + second + [cross, cross_loss]:
        c.wait_send()


def spread(values):
    three = values.reshape(3, 16)
    wide = jnp.broadcast_to(three[:, :, None], (3, 16, 128))
    edge = jnp.concatenate(
        [jnp.broadcast_to(three[b][:, None], (16, 32)) for b in range(3)] + [jnp.zeros((16, 32), values.dtype)],
        axis=1,
    )
    return jnp.concatenate([wide, edge[None]], axis=0).reshape(4, 2, 8, 128)


def per_device(
    init_field, conduct, nonlin, counts, descriptors, time_code, w_in, bias_in, w_out, decoder
):
    core = lax.axis_index("run")
    col = lax.axis_index("col")
    wide = descriptors.astype(f32).reshape(2, 1, 48, 256) + time_code.astype(f32).reshape(1, 8, 1, 256)
    rows_in = wide.astype(bf16).reshape(768, 256)
    pre = jnp.dot(rows_in, w_in, preferred_element_type=f32) + bias_in
    act = jax.nn.gelu(pre).astype(bf16)
    hidden = jnp.dot(act, w_out, preferred_element_type=f32).astype(bf16)
    hid = lax.dynamic_slice_in_dim(hidden, core * 384, 384, 0)

    lanes = jnp.arange(128) % 32
    outside = ((lanes >= 16) & (lanes < 24) & (col == 0)) | ((lanes >= 8) & (lanes < 16) & (col == 7))
    cnt = spread(counts)
    cnt = cnt.at[3].set(jnp.where(outside[None, None, :], 0, cnt[3]))
    vmem = pl.BlockSpec(memory_space=pltpu.VMEM)
    hbm = pl.BlockSpec(memory_space=pl.ANY)
    dma = pltpu.SemaphoreType.DMA
    final, part, loss = pl.pallas_call(
        main_kernel,
        name="solve_and_learn",
        out_shape=(
            jax.ShapeDtypeStruct((48, 64, 128), f32),
            jax.ShapeDtypeStruct((4, 384, 128), f32),
            jax.ShapeDtypeStruct((8, 128), f32),
        ),
        in_specs=[hbm, hbm, vmem, vmem, hbm, vmem],
        out_specs=(hbm, vmem, vmem),
        scratch_shapes=[
            pltpu.VMEM((3072, 128), f32),
            pltpu.VMEM((80, 128), f32),
            pltpu.VMEM((4, ROWS, 2, 8, 128), f32),
            pltpu.VMEM((4, ROWS, 8, 128), f32),
            pltpu.VMEM((2, 8, 3, 16, 128), bf16),
            pltpu.VMEM((2, 8, 3, 16, 128), bf16),
            pltpu.VMEM((2, GROUPS, 16, 128), bf16),
            pltpu.VMEM((2, GROUPS, 16, 128), bf16),
            pltpu.VMEM((3, 2, ROWS, 2, 8, 128), f32),
            pltpu.VMEM((4, 8, 2, 8, 128), f32),
            pltpu.VMEM((4, 8, 2, 8, 128), f32),
            pltpu.VMEM((4, 20, 8, 48, 128), bf16),
            pltpu.VMEM((8, 8, 512, 128), bf16),
            pltpu.VMEM((4, 16, 512, 128), bf16),
            pltpu.VMEM((2, 1024, 1024), bf16),
            pltpu.VMEM((8, 256, 128), f32),
            pltpu.VMEM((512, 512), f32),
            pltpu.VMEM((2, 384, 256), f32),
            dma((3,)), dma((2,)), dma((4,)), dma((4,)), dma((2,)), dma((2,)),
            dma((8, 7)), dma((8, 7)), dma((8,)), dma((8,)), dma((8,)),
        ],
        compiler_params=pltpu.CompilerParams(
            collective_id=0, has_side_effects=True, vmem_limit_bytes=VMEM_ALL - (1 << 16)
        ),
    )(init_field, conduct, spread(nonlin), cnt, decoder.reshape(4096, 1024), hid)

    grad, loss_sum = pl.pallas_call(
        reduce_kernel,
        name="reduce_grad",
        out_shape=(jax.ShapeDtypeStruct((2, 384, 512), bf16), jax.ShapeDtypeStruct((8, 128), f32)),
        in_specs=[vmem, vmem],
        out_specs=(vmem, vmem),
        scratch_shapes=[
            pltpu.VMEM((63, 24, 128), f32),
            pltpu.VMEM((64, 8, 128), f32),
            pltpu.VMEM((2, 8, 128), f32),
            pltpu.VMEM((2, 64, 32, 128), bf16),
            dma((63,)), dma((63,)), dma((63,)), dma((63,)), dma(()), dma((65,)), dma((63,)), dma((2,)), dma((2,)),
        ],
        compiler_params=pltpu.CompilerParams(collective_id=1, has_side_effects=True),
    )(part, loss)
    grad = grad.reshape(768, 512)

    grad_out = lax.dot_general(act, grad, (((0,), (0,)), ((), ())), preferred_element_type=f32)
    back = lax.dot_general(grad, w_out, (((1,), (1,)), ((), ())), preferred_element_type=f32)
    _, pull = jax.vjp(jax.nn.gelu, pre)
    grad_pre = pull(back)[0]
    grad_in = lax.dot_general(
        rows_in, grad_pre.astype(bf16), (((0,), (0,)), ((), ())), preferred_element_type=f32
    )
    new_w_in = w_in.astype(f32) - RATE * grad_in
    new_bias = bias_in - RATE * jnp.sum(grad_pre, axis=0)
    new_w_out = w_out.astype(f32) - RATE * grad_out
    mean_loss = jnp.sum(loss_sum) / (768 * 512 * 1024)
    return final, new_w_in, new_bias, new_w_out, mean_loss


def solution(mesh):
    in_specs = (
        P("run", "row", "col"), P("row", "col"), P("run"), P("run"), P(), P(), P(), P(), P(),
        P(None, ("row", "col"), None),
    )
    out_specs = (P("run", "row", "col"), P(), P(), P(), P())
    return jax.shard_map(
        per_device, mesh=mesh, in_specs=in_specs, out_specs=out_specs, check_vma=False
    )
```

```python
import jax
import jax.numpy as jnp
from jax import lax
from jax.experimental import pallas as pl
from jax.experimental.pallas import tpu as pltpu
from jax.sharding import PartitionSpec as P

MESH = pl.DeviceIdType.MESH
f32, bf16 = jnp.float32, jnp.bfloat16
STEP, RATE = 0.12, 0.5
ROWS = 96
GROUPS = ROWS // 4
OFFSETS = ((2, 1), (1, 1), (3, 1), (2, 0), (0, 1), (1, 0), (3, 0))
VMEM_ALL = 64 << 20


def signal_all(peers):
    barrier = pltpu.get_barrier_semaphore()
    for peer in peers:
        pl.semaphore_signal(barrier, inc=1, device_id=peer, device_id_type=MESH)
    pl.semaphore_wait(barrier, len(peers))


def remote(src, dst, send, recv, peer):
    return pltpu.make_async_remote_copy(
        src_ref=src, dst_ref=dst, send_sem=send, recv_sem=recv, device_id=peer, device_id_type=MESH
    )


def main_kernel(
    field, conduct, nonlin, counts, desc, code, w_in, bias, w_out, decoder,
    final, part, loss,
    nl, cnt, hid, fs, cd, u, cb, rs, rr, xs, xr, fx, ks, ac, snap, tr, dl, raw, tf, gram, acc,
    loc_sem, raw_sem, row_send, row_recv, col_send, col_recv, dec_send, dec_recv, own_sem, fwd_send, fwd_recv,
):
    core, row, col = (lax.axis_index(n) for n in ("run", "row", "col"))
    y, zh = col // 2, col % 2
    sibling = (1 - core, row, col)
    down, up = (core, (row + 1) % 8, col), (core, (row + 7) % 8, col)
    right, left = (core, row, (col + 1) % 8), (core, row, (col + 7) % 8)
    targets = [((y + dy) % 4) * 2 + (zh + dz) % 2 for dy, dz in OFFSETS]
    signal_all([(core, row, t) for t in targets] + [up, down, sibling])

    fs3 = fs.reshape(48, 64, 128)
    rows_of_conduct = [conduct.at[pl.ds(56, 8), :], conduct.at[pl.ds(0, 8), :]]

    def row_copies(way):
        peer = (down, up)[way]
        return [
            remote(rs.at[way], rr.at[way], row_send.at[way], row_recv.at[way], peer),
            remote(
                rows_of_conduct[way], cd.at[pl.ds(72 * way, 8), :], row_send.at[2 + way], row_recv.at[2 + way], peer
            ),
        ]

    may_send = [row < 7, row > 0]
    may_get = [row > 0, row < 7]

    def each_row_copy(allowed, act):
        for way in range(2):

            @pl.when(allowed[way])
            def _():
                for c in row_copies(way):
                    act(c)

    loc_copies = [
        pltpu.make_async_copy(field, fs3, loc_sem.at[0]),
        pltpu.make_async_copy(conduct, cd.at[pl.ds(8, 64), :], loc_sem.at[1]),
    ]

    def raw_copy(part_at, slot):
        start = pl.multiple_of(part_at * 1024, 1024)
        return pltpu.make_async_copy(decoder.at[pl.ds(start, 1024), :], raw.at[slot], raw_sem.at[slot])

    mine, other = 2 * core, 2 * (1 - core)

    def turn(quarter, slot):
        def piece(hb, carry):
            at = pl.multiple_of(hb * 256, 256)
            to = pl.multiple_of(quarter * 128 + hb * 32, 32)
            for t in range(8):
                tf[t] = raw[slot, pl.ds(at, 256), t * 128 : (t + 1) * 128].astype(f32)
            for t in range(8):
                for i in range(8):
                    tr[t, i, pl.ds(to, 32), :] = tf[t, pl.ds(i, 32, stride=8), :].astype(bf16)
            return carry

        lax.fori_loop(0, 4, piece, 0)

    def dec_copies(hh, kk):
        h0 = pl.multiple_of((mine + hh) * 128, 128)
        rnd = hh * 4 + kk
        out = []
        for j, t in enumerate(targets):
            out.append(
                remote(
                    tr.at[t, pl.ds(2 * kk, 2), pl.ds(h0, 128), :],
                    dl.at[kk, pl.ds(2 * col, 2), pl.ds(h0, 128), :],
                    dec_send.at[rnd, j], dec_recv.at[rnd, j], (core, row, t),
                )
            )
        return out

    def own_copy(hh, kk):
        h0 = pl.multiple_of((mine + hh) * 128, 128)
        return pltpu.make_async_copy(
            tr.at[col, pl.ds(2 * kk, 2), pl.ds(h0, 128), :],
            dl.at[kk, pl.ds(2 * col, 2), pl.ds(h0, 128), :],
            own_sem.at[hh * 4 + kk],
        )

    def fwd_copy(hh, kk):
        h0 = pl.multiple_of((mine + hh) * 128, 128)
        block = dl.at[kk, :, pl.ds(h0, 128), :]
        return remote(block, block, fwd_send.at[hh * 4 + kk], fwd_recv.at[hh * 4 + kk], sibling)

    def send_round(hh, kk):
        for c in dec_copies(hh, kk):
            c.start()
        own_copy(hh, kk).start()

    def pass_round(hh, kk):
        for c in dec_copies(hh, kk):
            c.wait_recv()
        own_copy(hh, kk).wait()
        fwd_copy(hh, kk).start()

    for c in loc_copies:
        c.start()
    raw_copy(mine, 0).start()
    raw_copy(mine + 1, 1).start()
    for c in loc_copies:
        c.wait()

    def pack_rows(i, carry):
        for b in range(3):
            for way in range(2):
                rs[way, i, b] = fs[pl.ds(b * 1024 + i + 56 * (1 - way), 16, stride=64), :].astype(bf16)
        return carry

    lax.fori_loop(0, 8, pack_rows, 0)
    each_row_copy(may_send, lambda c: c.start())
    raw_copy(mine, 0).wait()
    turn(mine, 0)
    raw_copy(other, 0).start()
    send_round(0, 0)

    for b in range(3):
        u[b, 0:8] = jnp.zeros((8, 2, 8, 128), f32)
        u[b, 88:96] = jnp.zeros((8, 2, 8, 128), f32)

    def fill(n, carry):
        for q in range(4):
            i = 4 * n + q
            for b in range(3):
                u[b, i + 16] = fs[pl.ds(b * 1024 + i, 16, stride=64), :].reshape(2, 8, 128)
        return carry

    lax.fori_loop(0, 16, fill, 0)

    each_row_copy(may_get, lambda c: c.wait_recv())

    def unpack_rows(i, carry):
        for b in range(3):
            for way in range(2):
                u[b, i + 8 + 72 * way] = rr[way, i, b].astype(f32).reshape(2, 8, 128)
        return carry

    lax.fori_loop(0, 8, unpack_rows, 0)

    def fill_conduct(n, carry):
        for q in range(4):
            i = 4 * n + q
            cb[0, i + 8] = jnp.broadcast_to(cd[pl.ds(i, 1), :] * (0.5 * STEP), (8, 128))
        return carry

    lax.fori_loop(0, 20, fill_conduct, 0)
    for s in range(4):
        cb[s, 0:8] = jnp.zeros((8, 8, 128), f32)
        cb[s, 88:96] = jnp.zeros((8, 8, 128), f32)

    def clear(b):
        @pl.when(row == 0)
        def _():
            u[b, 8:16] = jnp.zeros((8, 2, 8, 128), f32)

        @pl.when(row == 7)
        def _():
            u[b, 80:88] = jnp.zeros((8, 2, 8, 128), f32)

    for b in range(3):
        clear(b)

    @pl.when(row == 0)
    def _():
        cb[0, 8:16] = jnp.zeros((8, 8, 128), f32)

    @pl.when(row == 7)
    def _():
        cb[0, 80:88] = jnp.zeros((8, 8, 128), f32)

    lane = lax.broadcasted_iota(jnp.int32, (2, 8, 128), 2)
    in32 = lane % 32

    def gather_edges(i):
        out = None
        for b in range(4):
            v = u[b, i] if b < 3 else jnp.broadcast_to(cb[0, i][None], (2, 8, 128))
            ends = pltpu.roll(v, (32 * b + 8) % 128, 2)
            starts = pltpu.roll(v, (32 * b + 24) % 128, 2)
            both = jnp.where(in32 < 8, ends, starts)
            out = both if b == 0 else jnp.where(lane // 32 == b, both, out)
        return out

    def pack(g, carry):
        to_right = to_left = None
        for q in range(4):
            o = gather_edges(4 * g + q)
            u[3, 4 * g + q] = o
            r = pltpu.roll(o, 8 * q, 2) if q else o
            l = pltpu.roll(o, (8 * q + 8) % 32 + 96 if q < 3 else 0, 2) if q < 3 else pltpu.roll(o, 0, 2)
            here = in32 // 8 == q
            to_right = r if q == 0 else jnp.where(here, r, to_right)
            to_left = l if q == 0 else jnp.where(here, l, to_left)
        xs[0, g] = to_right.reshape(16, 128).astype(bf16)
        xs[1, g] = to_left.reshape(16, 128).astype(bf16)
        return carry

    lax.fori_loop(2, GROUPS - 2, pack, 0)
    col_copies = [
        remote(xs.at[0, pl.ds(2, 20)], xr.at[0, pl.ds(2, 20)], col_send.at[0], col_recv.at[0], right),
        remote(xs.at[1, pl.ds(2, 20)], xr.at[1, pl.ds(2, 20)], col_send.at[1], col_recv.at[1], left),
    ]
    for c in col_copies:
        c.start()
    raw_copy(mine + 1, 1).wait()
    turn(mine + 1, 1)
    raw_copy(other + 1, 1).start()
    raw_copy(other, 0).wait()
    turn(other, 0)
    for rnd in range(1, 8):
        send_round(rnd // 4, rnd % 4)
    raw_copy(other + 1, 1).wait()
    turn(other + 1, 1)

    wide = desc[pl.ds(pl.multiple_of(core * 48, 16), 48), :].astype(f32)
    for s in range(8):
        rows_s = (wide + code[s : s + 1, :].astype(f32)).astype(bf16)
        act_s = jax.nn.gelu(jnp.dot(rows_s, w_in[...], preferred_element_type=f32) + bias[...]).astype(bf16)
        hid[48 * s : 48 * s + 48, :] = jnp.dot(act_s, w_out[...], preferred_element_type=f32).astype(bf16)

    gram[...] = jnp.zeros((512, 512), f32)
    nt = (((1,), (1,)), ((), ()))

    def add_gram(t, carry):
        x = jnp.concatenate([tr[t, i] for i in range(8)], axis=1)
        gram[0:256] += lax.dot_general(x[0:256], x, nt, preferred_element_type=f32)
        gram[256:512, 256:512] += lax.dot_general(x[256:512], x[256:512], nt, preferred_element_type=f32)
        return carry

    lax.fori_loop(0, 8, add_gram, 0)
    gram[256:512, 0:256] = gram[0:256, 256:512].T
    big = gram[...].astype(bf16)
    small = (gram[...] - big.astype(f32)).astype(bf16)
    product = jnp.dot(hid[...], big, preferred_element_type=f32) + jnp.dot(
        hid[...], small, preferred_element_type=f32
    )
    for t in range(4):
        part[t] = product[:, 128 * t : 128 * t + 128]

    for c in col_copies:
        c.wait_recv()

    def of_runs(ref, b):
        return jnp.broadcast_to(ref[16 * b : 16 * b + 16, :], (16, 128)).reshape(2, 8, 128)

    def lanes_of_runs(ref):
        out = jnp.zeros((2, 8, 128), ref.dtype)
        for b in range(3):
            out = jnp.where(lane // 32 == b, of_runs(ref, b), out)
        return out

    for b in range(3):
        nl[b] = of_runs(nonlin, b)
        cnt[b] = of_runs(counts, b)
    nl[3] = lanes_of_runs(nonlin)

    u[3, 0:8] = jnp.zeros((8, 2, 8, 128), f32)
    u[3, 88:96] = jnp.zeros((8, 2, 8, 128), f32)
    from_left = (in32 >= 16) & (in32 < 24)
    from_right = (in32 >= 8) & (in32 < 16)
    left_ok = (jnp.zeros((2, 8, 128), jnp.int32) + col) > 0
    right_ok = (jnp.zeros((2, 8, 128), jnp.int32) + col) < 7

    taken = jnp.where(from_left & jnp.logical_not(left_ok), 0, lanes_of_runs(counts))
    cnt[3] = jnp.where(from_right & jnp.logical_not(right_ok), 0, taken)

    def unpack(g, carry):
        gl = xr[0, g].astype(f32).reshape(2, 8, 128)
        gr = xr[1, g].astype(f32).reshape(2, 8, 128)
        for q in range(4):
            o = u[3, 4 * g + q]
            a = pltpu.roll(gl, (16 - 8 * q) % 128, 2)
            c = pltpu.roll(gr, (8 - 8 * q) % 128, 2)
            o = jnp.where(from_left, jnp.where(left_ok, a, 0.0), o)
            o = jnp.where(from_right, jnp.where(right_ok, c, 0.0), o)
            u[3, 4 * g + q] = o
            k = o[0]
            for b in range(3):
                k = jnp.where(lane[0] // 32 == b, pltpu.roll(o[0], 32 * (b + 1), 1), k)
            cb[2, 4 * g + q] = jnp.where(lane[0] < 96, k, 0.0)
        return carry

    lax.fori_loop(2, GROUPS - 2, unpack, 0)
    clear(3)

    @pl.when(row == 0)
    def _():
        cb[2, 8:16] = jnp.zeros((8, 8, 128), f32)

    @pl.when(row == 7)
    def _():
        cb[2, 80:88] = jnp.zeros((8, 8, 128), f32)

    def shift_conduct(g, carry):
        for q in range(4):
            for side in (0, 2):
                cb[side + 1, 4 * g + q] = pltpu.roll(cb[side, 4 * g + q], 127, 1)
        return carry

    lax.fori_loop(2, GROUPS - 2, shift_conduct, 0)
    first, last = lane == 0, lane == 127

    def run_step(s, with_main):
        blocks = (0, 1, 2, 3) if with_main else (3,)
        count = range(len(blocks))
        ahead_s = s + 1 if with_main else s
        coef = [nl[b] for b in blocks]
        active = [jnp.where(cnt[b] > (s if b < 3 else ahead_s), 1.0, 0.0).astype(f32) for b in blocks]
        begin = (9 + s) // 4

        def kappa(v, i, n, shifted=0):
            return cb[(2 if blocks[n] == 3 else 0) + shifted, i][None] / (1.0 + coef[n] * v * v)

        def ahead(i, vs):
            out = []
            for n, b in enumerate(blocks):
                v = vs[n]
                k = kappa(v, i, n)
                vr = pltpu.roll(v, 127, 2)
                across = (k + kappa(vr, i, n, 1)) * (vr - v)
                if b < 3:
                    across = jnp.where(last, fx[b, s % 2, i], across)
                out.append((k, across))
            return out

        def keep(g, q, made):
            for n, (k, across) in enumerate(made):
                ks[blocks[n], (g % 2) * 4 + q] = k
                ac[blocks[n], (g % 2) * 4 + q] = across

        flows = []
        for q in range(4):
            vs = [u[b, 4 * begin + q] for b in blocks]
            made = ahead(4 * begin + q, vs)
            keep(begin, q, made)
            if q == 0:
                for n, b in enumerate(blocks):
                    before = u[b, 4 * begin - 1]
                    flows.append((made[n][0] + kappa(before, 4 * begin - 1, n)) * (vs[n] - before))

        def group(g, flow):
            flow = list(flow)
            base, now = 4 * g, (g % 2) * 4
            v = [[u[b, base + q] for b in blocks] for q in range(4)]
            k = [[ks[b, now + q] for b in blocks] for q in range(4)]
            a = [[ac[b, now + q] for b in blocks] for q in range(4)]
            v_next = [[u[b, base + 4 + q] for b in blocks] for q in range(4)]
            first_made = None
            for q in range(4):
                made = ahead(base + 4 + q, v_next[q])
                first_made = made if q == 0 else first_made
                for n, b in enumerate(blocks):
                    vn = v[q + 1][n] if q < 3 else v_next[0][n]
                    kn = k[q + 1][n] if q < 3 else first_made[n][0]
                    flow_n = (k[q][n] + kn) * (vn - v[q][n])
                    came = pltpu.roll(a[q][n], 1, 2)
                    if b == 3:
                        f = jnp.where(in32 == 8, pltpu.roll(a[q][n], 113, 2), a[q][n])
                        for to in range(3):
                            fx[to, ahead_s % 2, base + q] = pltpu.roll(f, 120 - 32 * to, 2)
                    else:
                        came = jnp.where(first, fx[b, s % 2, base + q], came)
                    new = v[q][n] + active[n] * ((flow_n - flow[n]) + (a[q][n] - came))
                    u[b, base + q] = new
                    if b < 3:
                        snap[2 * (g % 2) + q // 2, 2 * (g // 2) - 2 + q % 2, s, 16 * b : 16 * b + 16, :] = (
                            new.reshape(16, 128).astype(bf16)
                        )
                    flow[n] = flow_n
                keep(g + 1, q, made)
            return tuple(flow)

        lax.fori_loop(begin, GROUPS - begin, group, tuple(flows))
        for b in blocks:
            clear(b)

    pass_round(0, 0)
    run_step(0, False)

    def one_step(s, carry):
        run_step(s, True)
        for at, hh, kk in ((0, 0, 1), (1, 0, 2), (3, 0, 3), (4, 1, 0), (5, 1, 1), (6, 1, 2)):

            @pl.when(s == at)
            def _():
                pass_round(hh, kk)

        return carry

    lax.fori_loop(0, 8, one_step, 0)

    pass_round(1, 3)

    def give_back(n, carry):
        for q in range(4):
            for b in range(3):
                fs[pl.ds(b * 1024 + 4 * n + q, 16, stride=64), :] = u[b, 4 * n + q + 16].reshape(16, 128)
        return carry

    lax.fori_loop(0, 16, give_back, 0)
    out_copy = pltpu.make_async_copy(fs3, final, loc_sem.at[2])
    out_copy.start()

    def square(n, total):
        x = snap[n // 16, 2 + n % 16].astype(f32).reshape(48, 8, 128)
        return total + jnp.sum(x * x, axis=0)

    squares = lax.fori_loop(0, 64, square, jnp.zeros((8, 128), f32))

    for hh in range(2):
        for kk in range(4):
            fwd_copy(hh, kk).wait_recv()

            lhs = jnp.concatenate([snap[kk, 2 + i].reshape(384, 128) for i in range(16)], axis=1)
            rhs = jnp.concatenate(
                [
                    jnp.concatenate(
                        [
                            dl[kk, i, 128 * hh : 128 * hh + 128, :],
                            dl[kk, i, 256 + 128 * hh : 384 + 128 * hh, :],
                        ],
                        axis=0,
                    )
                    for i in range(16)
                ],
                axis=1,
            )
            got = lax.dot_general(lhs, rhs, nt, preferred_element_type=f32)
            acc[hh] = got if kk == 0 else acc[hh] + got

    total = squares
    for hh in range(2):
        for half in range(2):
            at = slice(256 * half + 128 * hh, 256 * half + 128 * hh + 128)
            a = part[2 * half + hh]
            c = acc[hh, :, 128 * half : 128 * half + 128]
            part[2 * half + hh] = a - c
            total = total + jnp.sum((hid[:, at].astype(f32) * (a - 2.0 * c)).reshape(48, 8, 128), axis=0)
    loss[...] = total

    out_copy.wait()
    each_row_copy(may_send, lambda c: c.wait_send())
    for c in col_copies:
        c.wait_send()
    for hh in range(2):
        for kk in range(4):
            for c in dec_copies(hh, kk):
                c.wait_send()
            fwd_copy(hh, kk).wait_send()


def reduce_kernel(
    part, loss_in, desc, code, w_in, bias, w_out,
    new_in, new_bias, new_out, loss_out,
    rows, act, slope, grad, back, r1, l1, l2, got, send1, recv1, send2, recv2, lsend, lrecv, lsend2, xsend, xrecv,
):
    core, row, col = (lax.axis_index(n) for n in ("run", "row", "col"))
    x, y, z = row % 4, col // 2, (col % 2) * 2 + row // 4
    sibling = (1 - core, row, col)
    me = row * 8 + col

    def chip(j):
        x1, y1, z1 = (x + j % 4) % 4, (y + j // 4 % 4) % 4, (z + j // 16) % 4
        return (z1 % 2) * 4 + x1, y1 * 2 + z1 // 2

    offsets = list(range(1, 64))
    offsets.sort(key=lambda j: -sum(min(d, 4 - d) for d in (j % 4, j // 4 % 4, j // 16)))
    peers = [(core, *chip(j)) for j in offsets]
    signal_all(peers + [sibling])

    def piece(p):
        return part.at[p // 16, pl.ds(pl.multiple_of(24 * (p % 16), 8), 24), :]

    first = []
    for n, j in enumerate(offsets):
        r, c = chip(j)
        first.append(remote(piece(r * 8 + c), r1.at[n], send1.at[n], recv1.at[n], peers[n]))
    to_zero = remote(loss_in, l1.at[me], lsend, lrecv.at[me], (core, 0, 0))

    @pl.when(me > 0)
    def _():
        to_zero.start()

    for c in first:
        c.start()

    def trunk(n, carry):
        at = pl.multiple_of(48 * n, 48)
        half = pl.multiple_of(48 * (n // 8), 48)
        rows_n = (desc[pl.ds(half, 48), :].astype(f32) + code[n % 8]).astype(bf16)
        pre = jnp.dot(rows_n, w_in[...], preferred_element_type=f32) + bias[...]
        value, pull = jax.vjp(jax.nn.gelu, pre)
        rows[pl.ds(at, 48), :] = rows_n
        act[pl.ds(at, 48), :] = value.astype(bf16)
        slope[pl.ds(at, 48), :] = pull(jnp.ones_like(pre))[0]
        return carry

    lax.fori_loop(0, 16, trunk, 0)
    total = part[me // 16, pl.ds(pl.multiple_of(24 * (me % 16), 8), 24), :]
    for n, c in enumerate(first):
        c.wait_recv()
        total = total + r1[n]
    got[core, me] = jnp.concatenate([total * (1.0 / 768.0), jnp.zeros((8, 128), f32)], axis=0).astype(bf16)

    second = [remote(got.at[core, me], got.at[core, me], send2.at[n], recv2.at[n], peers[n]) for n in range(63)]
    for c in second:
        c.start()
    spread_loss = [remote(l2.at[core], l2.at[core], lsend2.at[n], lrecv.at[64], peers[n]) for n in range(63)]

    @pl.when(me == 0)
    def _():
        sums = loss_in[...]
        for p in range(1, 64):
            remote(loss_in, l1.at[p], lsend, lrecv.at[p], (core, 0, 0)).wait_recv()
            sums = sums + l1[p]
        l2[core] = sums
        for c in spread_loss:
            c.start()

    for c in second:
        c.wait_recv()
    cross = remote(got.at[core], got.at[core], xsend.at[0], xrecv.at[0], sibling)
    cross.start()

    @pl.when(me > 0)
    def _():
        spread_loss[0].wait_recv()

    cross_loss = remote(l2.at[core], l2.at[core], xsend.at[1], xrecv.at[1], sibling)
    cross_loss.start()

    def place(own):
        for t in range(4):
            for q in range(8):
                pair = jnp.concatenate(
                    [got[own, 16 * t + 2 * q + i].astype(f32)[0:24] for i in range(2)], axis=0
                ).astype(bf16)
                grad[pl.ds(pl.multiple_of(384 * own + 48 * q, 48), 48), 128 * t : 128 * t + 128] = pair

    place(core)
    cross.wait_recv()
    place(1 - core)
    tn = (((0,), (0,)), ((), ()))
    new_out[...] = w_out[...].astype(f32) - RATE * lax.dot_general(
        act[...], grad[...], tn, preferred_element_type=f32
    )
    back[...] = (
        lax.dot_general(grad[...], w_out[...], (((1,), (1,)), ((), ())), preferred_element_type=f32) * slope[...]
    )
    new_bias[...] = bias[...] - RATE * jnp.sum(back[...], axis=0, keepdims=True)
    new_in[...] = w_in[...].astype(f32) - RATE * lax.dot_general(
        rows[...], back[...].astype(bf16), tn, preferred_element_type=f32
    )
    cross_loss.wait_recv()
    loss_out[...] = l2[0] + l2[1]

    @pl.when(me > 0)
    def _():
        to_zero.wait_send()

    @pl.when(me == 0)
    def _():
        for c in spread_loss:
            c.wait_send()

    for c in first + second + [cross, cross_loss]:
        c.wait_send()


def per_device(
    init_field, conduct, nonlin, counts, descriptors, time_code, w_in, bias_in, w_out, decoder
):
    bias_row = bias_in.reshape(1, 512)
    vmem = pl.BlockSpec(memory_space=pltpu.VMEM)
    hbm = pl.BlockSpec(memory_space=pl.ANY)
    dma = pltpu.SemaphoreType.DMA
    final, part, loss = pl.pallas_call(
        main_kernel,
        name="solve_and_learn",
        out_shape=(
            jax.ShapeDtypeStruct((48, 64, 128), f32),
            jax.ShapeDtypeStruct((4, 384, 128), f32),
            jax.ShapeDtypeStruct((8, 128), f32),
        ),
        in_specs=[hbm, hbm, vmem, vmem, vmem, vmem, vmem, vmem, vmem, hbm],
        out_specs=(hbm, vmem, vmem),
        scratch_shapes=[
            pltpu.VMEM((4, 2, 8, 128), f32),
            pltpu.VMEM((4, 2, 8, 128), jnp.int32),
            pltpu.VMEM((384, 512), bf16),
            pltpu.VMEM((3072, 128), f32),
            pltpu.VMEM((80, 128), f32),
            pltpu.VMEM((4, ROWS, 2, 8, 128), f32),
            pltpu.VMEM((4, ROWS, 8, 128), f32),
            pltpu.VMEM((2, 8, 3, 16, 128), bf16),
            pltpu.VMEM((2, 8, 3, 16, 128), bf16),
            pltpu.VMEM((2, GROUPS, 16, 128), bf16),
            pltpu.VMEM((2, GROUPS, 16, 128), bf16),
            pltpu.VMEM((3, 2, ROWS, 2, 8, 128), f32),
            pltpu.VMEM((4, 8, 2, 8, 128), f32),
            pltpu.VMEM((4, 8, 2, 8, 128), f32),
            pltpu.VMEM((4, 20, 8, 48, 128), bf16),
            pltpu.VMEM((8, 8, 512, 128), bf16),
            pltpu.VMEM((4, 16, 512, 128), bf16),
            pltpu.VMEM((2, 1024, 1024), bf16),
            pltpu.VMEM((8, 256, 128), f32),
            pltpu.VMEM((512, 512), f32),
            pltpu.VMEM((2, 384, 256), f32),
            dma((3,)), dma((2,)), dma((4,)), dma((4,)), dma((2,)), dma((2,)),
            dma((8, 7)), dma((8, 7)), dma((8,)), dma((8,)), dma((8,)),
        ],
        compiler_params=pltpu.CompilerParams(
            collective_id=0, has_side_effects=True, vmem_limit_bytes=VMEM_ALL - (1 << 16)
        ),
    )(
        init_field, conduct, nonlin.reshape(48, 1), counts.reshape(48, 1),
        descriptors, time_code, w_in, bias_row, w_out, decoder.reshape(4096, 1024),
    )

    new_w_in, new_bias, new_w_out, loss_sum = pl.pallas_call(
        reduce_kernel,
        name="reduce_grad",
        out_shape=(
            jax.ShapeDtypeStruct((256, 512), f32),
            jax.ShapeDtypeStruct((1, 512), f32),
            jax.ShapeDtypeStruct((512, 512), f32),
            jax.ShapeDtypeStruct((8, 128), f32),
        ),
        in_specs=[vmem] * 7,
        out_specs=(vmem,) * 4,
        scratch_shapes=[
            pltpu.VMEM((768, 256), bf16),
            pltpu.VMEM((768, 512), bf16),
            pltpu.VMEM((768, 512), f32),
            pltpu.VMEM((768, 512), bf16),
            pltpu.VMEM((768, 512), f32),
            pltpu.VMEM((63, 24, 128), f32),
            pltpu.VMEM((64, 8, 128), f32),
            pltpu.VMEM((2, 8, 128), f32),
            pltpu.VMEM((2, 64, 32, 128), bf16),
            dma((63,)), dma((63,)), dma((63,)), dma((63,)), dma(()), dma((65,)), dma((63,)), dma((2,)), dma((2,)),
        ],
        compiler_params=pltpu.CompilerParams(collective_id=1, has_side_effects=True),
    )(part, loss, descriptors, time_code.astype(f32).reshape(8, 1, 256), w_in, bias_row, w_out)
    mean_loss = jnp.sum(loss_sum) / (768 * 512 * 1024)
    return final, new_w_in, new_bias.reshape(512), new_w_out, mean_loss


def solution(mesh):
    in_specs = (
        P("run", "row", "col"), P("row", "col"), P("run"), P("run"), P(), P(), P(), P(), P(),
        P(None, ("row", "col"), None),
    )
    out_specs = (P("run", "row", "col"), P(), P(), P(), P())
    return jax.shard_map(
        per_device, mesh=mesh, in_specs=in_specs, out_specs=out_specs, check_vma=False
    )
```

```python
import jax
import jax.numpy as jnp
from jax import lax
from jax.experimental import pallas as pl
from jax.experimental.pallas import tpu as pltpu
from jax.sharding import PartitionSpec as P

MESH = pl.DeviceIdType.MESH
f32, bf16 = jnp.float32, jnp.bfloat16
STEP, RATE = 0.12, 0.5
ROWS = 96
GROUPS = ROWS // 4
OFFSETS = ((2, 1), (1, 1), (3, 1), (2, 0), (0, 1), (1, 0), (3, 0))
VMEM_ALL = 64 << 20


def signal_all(peers):
    barrier = pltpu.get_barrier_semaphore()
    for peer in peers:
        pl.semaphore_signal(barrier, inc=1, device_id=peer, device_id_type=MESH)
    pl.semaphore_wait(barrier, len(peers))


def remote(src, dst, send, recv, peer):
    return pltpu.make_async_remote_copy(
        src_ref=src, dst_ref=dst, send_sem=send, recv_sem=recv, device_id=peer, device_id_type=MESH
    )


def main_kernel(
    field, conduct, nonlin, counts, desc, code, w_in, bias, w_out, decoder,
    final, part, loss,
    nl, cnt, hid, fs, cd, u, cb, rs, rr, xs, xr, fx, ks, ac, snap, tr, dl, raw, tf, gram, acc,
    loc_sem, raw_sem, row_send, row_recv, col_send, col_recv, dec_send, dec_recv, own_sem, fwd_send, fwd_recv,
):
    core, row, col = (lax.axis_index(n) for n in ("run", "row", "col"))
    y, zh = col // 2, col % 2
    sibling = (1 - core, row, col)
    down, up = (core, (row + 1) % 8, col), (core, (row + 7) % 8, col)
    right, left = (core, row, (col + 1) % 8), (core, row, (col + 7) % 8)
    targets = [((y + dy) % 4) * 2 + (zh + dz) % 2 for dy, dz in OFFSETS]
    signal_all([(core, q // 8, q % 8) for q in [(row * 8 + col + j) % 64 for j in range(1, 64)]] + [sibling])

    fs3 = fs.reshape(48, 64, 128)
    rows_of_conduct = [conduct.at[pl.ds(56, 8), :], conduct.at[pl.ds(0, 8), :]]

    def row_copies(way):
        peer = (down, up)[way]
        return [
            remote(rs.at[way], rr.at[way], row_send.at[way], row_recv.at[way], peer),
            remote(
                rows_of_conduct[way], cd.at[pl.ds(72 * way, 8), :], row_send.at[2 + way], row_recv.at[2 + way], peer
            ),
        ]

    may_send = [row < 7, row > 0]
    may_get = [row > 0, row < 7]

    def each_row_copy(allowed, act):
        for way in range(2):

            @pl.when(allowed[way])
            def _():
                for c in row_copies(way):
                    act(c)

    loc_copies = [
        pltpu.make_async_copy(field, fs3, loc_sem.at[0]),
        pltpu.make_async_copy(conduct, cd.at[pl.ds(8, 64), :], loc_sem.at[1]),
    ]

    def raw_copy(part_at, slot):
        start = pl.multiple_of(part_at * 1024, 1024)
        return pltpu.make_async_copy(decoder.at[pl.ds(start, 1024), :], raw.at[slot], raw_sem.at[slot])

    mine, other = 2 * core, 2 * (1 - core)

    def turn(quarter, slot):
        def piece(hb, carry):
            at = pl.multiple_of(hb * 256, 256)
            to = pl.multiple_of(quarter * 128 + hb * 32, 32)
            for t in range(8):
                tf[t] = raw[slot, pl.ds(at, 256), t * 128 : (t + 1) * 128].astype(f32)
            for t in range(8):
                for i in range(8):
                    tr[t, i, pl.ds(to, 32), :] = tf[t, pl.ds(i, 32, stride=8), :].astype(bf16)
            return carry

        lax.fori_loop(0, 4, piece, 0)

    def dec_copies(hh, kk):
        h0 = pl.multiple_of((mine + hh) * 128, 128)
        rnd = hh * 4 + kk
        out = []
        for j, t in enumerate(targets):
            out.append(
                remote(
                    tr.at[t, pl.ds(2 * kk, 2), pl.ds(h0, 128), :],
                    dl.at[kk, pl.ds(2 * col, 2), pl.ds(h0, 128), :],
                    dec_send.at[rnd, j], dec_recv.at[rnd, j], (core, row, t),
                )
            )
        return out

    def own_copy(hh, kk):
        h0 = pl.multiple_of((mine + hh) * 128, 128)
        return pltpu.make_async_copy(
            tr.at[col, pl.ds(2 * kk, 2), pl.ds(h0, 128), :],
            dl.at[kk, pl.ds(2 * col, 2), pl.ds(h0, 128), :],
            own_sem.at[hh * 4 + kk],
        )

    def fwd_copy(hh, kk):
        h0 = pl.multiple_of((mine + hh) * 128, 128)
        block = dl.at[kk, :, pl.ds(h0, 128), :]
        return remote(block, block, fwd_send.at[hh * 4 + kk], fwd_recv.at[hh * 4 + kk], sibling)

    def send_round(hh, kk):
        for c in dec_copies(hh, kk):
            c.start()
        own_copy(hh, kk).start()

    def pass_round(hh, kk):
        for c in dec_copies(hh, kk):
            c.wait_recv()
        own_copy(hh, kk).wait()
        fwd_copy(hh, kk).start()

    for c in loc_copies:
        c.start()
    raw_copy(mine, 0).start()
    raw_copy(mine + 1, 1).start()
    for c in loc_copies:
        c.wait()

    def pack_rows(i, carry):
        for b in range(3):
            for way in range(2):
                rs[way, i, b] = fs[pl.ds(b * 1024 + i + 56 * (1 - way), 16, stride=64), :].astype(bf16)
        return carry

    lax.fori_loop(0, 8, pack_rows, 0)
    each_row_copy(may_send, lambda c: c.start())
    raw_copy(mine, 0).wait()
    turn(mine, 0)
    raw_copy(other, 0).start()
    send_round(0, 0)

    for b in range(3):
        u[b, 0:8] = jnp.zeros((8, 2, 8, 128), f32)
        u[b, 88:96] = jnp.zeros((8, 2, 8, 128), f32)

    def fill(n, carry):
        for q in range(4):
            i = 4 * n + q
            for b in range(3):
                u[b, i + 16] = fs[pl.ds(b * 1024 + i, 16, stride=64), :].reshape(2, 8, 128)
        return carry

    lax.fori_loop(0, 16, fill, 0)

    each_row_copy(may_get, lambda c: c.wait_recv())

    def unpack_rows(i, carry):
        for b in range(3):
            for way in range(2):
                u[b, i + 8 + 72 * way] = rr[way, i, b].astype(f32).reshape(2, 8, 128)
        return carry

    lax.fori_loop(0, 8, unpack_rows, 0)

    def fill_conduct(n, carry):
        for q in range(4):
            i = 4 * n + q
            cb[0, i + 8] = jnp.broadcast_to(cd[pl.ds(i, 1), :] * (0.5 * STEP), (8, 128))
        return carry

    lax.fori_loop(0, 20, fill_conduct, 0)
    for s in range(4):
        cb[s, 0:8] = jnp.zeros((8, 8, 128), f32)
        cb[s, 88:96] = jnp.zeros((8, 8, 128), f32)

    def clear(b):
        @pl.when(row == 0)
        def _():
            u[b, 8:16] = jnp.zeros((8, 2, 8, 128), f32)

        @pl.when(row == 7)
        def _():
            u[b, 80:88] = jnp.zeros((8, 2, 8, 128), f32)

    for b in range(3):
        clear(b)

    @pl.when(row == 0)
    def _():
        cb[0, 8:16] = jnp.zeros((8, 8, 128), f32)

    @pl.when(row == 7)
    def _():
        cb[0, 80:88] = jnp.zeros((8, 8, 128), f32)

    lane = lax.broadcasted_iota(jnp.int32, (2, 8, 128), 2)
    in32 = lane % 32

    def gather_edges(i):
        out = None
        for b in range(4):
            v = u[b, i] if b < 3 else jnp.broadcast_to(cb[0, i][None], (2, 8, 128))
            ends = pltpu.roll(v, (32 * b + 8) % 128, 2)
            starts = pltpu.roll(v, (32 * b + 24) % 128, 2)
            both = jnp.where(in32 < 8, ends, starts)
            out = both if b == 0 else jnp.where(lane // 32 == b, both, out)
        return out

    def pack(g, carry):
        to_right = to_left = None
        for q in range(4):
            o = gather_edges(4 * g + q)
            u[3, 4 * g + q] = o
            r = pltpu.roll(o, 8 * q, 2) if q else o
            l = pltpu.roll(o, (8 * q + 8) % 32 + 96 if q < 3 else 0, 2) if q < 3 else pltpu.roll(o, 0, 2)
            here = in32 // 8 == q
            to_right = r if q == 0 else jnp.where(here, r, to_right)
            to_left = l if q == 0 else jnp.where(here, l, to_left)
        xs[0, g] = to_right.reshape(16, 128).astype(bf16)
        xs[1, g] = to_left.reshape(16, 128).astype(bf16)
        return carry

    lax.fori_loop(2, GROUPS - 2, pack, 0)
    col_copies = [
        remote(xs.at[0, pl.ds(2, 20)], xr.at[0, pl.ds(2, 20)], col_send.at[0], col_recv.at[0], right),
        remote(xs.at[1, pl.ds(2, 20)], xr.at[1, pl.ds(2, 20)], col_send.at[1], col_recv.at[1], left),
    ]
    for c in col_copies:
        c.start()
    raw_copy(mine + 1, 1).wait()
    turn(mine + 1, 1)
    raw_copy(other + 1, 1).start()
    raw_copy(other, 0).wait()
    turn(other, 0)
    for rnd in range(1, 8):
        send_round(rnd // 4, rnd % 4)
    raw_copy(other + 1, 1).wait()
    turn(other + 1, 1)

    wide = desc[pl.ds(pl.multiple_of(core * 48, 16), 48), :].astype(f32)
    for s in range(8):
        rows_s = (wide + code[s : s + 1, :].astype(f32)).astype(bf16)
        act_s = jax.nn.gelu(jnp.dot(rows_s, w_in[...], preferred_element_type=f32) + bias[...]).astype(bf16)
        hid[48 * s : 48 * s + 48, :] = jnp.dot(act_s, w_out[...], preferred_element_type=f32).astype(bf16)

    gram[...] = jnp.zeros((512, 512), f32)
    nt = (((1,), (1,)), ((), ()))

    def add_gram(t, carry):
        x = jnp.concatenate([tr[t, i] for i in range(8)], axis=1)
        gram[0:256] += lax.dot_general(x[0:256], x, nt, preferred_element_type=f32)
        gram[256:512, 256:512] += lax.dot_general(x[256:512], x[256:512], nt, preferred_element_type=f32)
        return carry

    lax.fori_loop(0, 8, add_gram, 0)
    gram[256:512, 0:256] = gram[0:256, 256:512].T
    big = gram[...].astype(bf16)
    small = (gram[...] - big.astype(f32)).astype(bf16)
    product = jnp.dot(hid[...], big, preferred_element_type=f32) + jnp.dot(
        hid[...], small, preferred_element_type=f32
    )
    for t in range(4):
        part[t] = product[:, 128 * t : 128 * t + 128]

    for c in col_copies:
        c.wait_recv()

    place_of = lax.broadcasted_iota(jnp.int32, (2, 8, 128), 0) * 8 + lax.broadcasted_iota(jnp.int32, (2, 8, 128), 1)

    def of_runs(ref, b):
        out = jnp.zeros((2, 8, 128), f32)
        for i in range(16):
            out = jnp.where(place_of == i, ref[16 * b + i].astype(f32), out)
        return out

    def lanes_of_runs(made):
        out = jnp.zeros((2, 8, 128), f32)
        for b in range(3):
            out = jnp.where(lane // 32 == b, made[b], out)
        return out

    for b in range(3):
        nl[b] = of_runs(nonlin, b)
        cnt[b] = of_runs(counts, b)
    nl[3] = lanes_of_runs(nl)

    u[3, 0:8] = jnp.zeros((8, 2, 8, 128), f32)
    u[3, 88:96] = jnp.zeros((8, 2, 8, 128), f32)
    from_left = (in32 >= 16) & (in32 < 24)
    from_right = (in32 >= 8) & (in32 < 16)
    left_ok = (jnp.zeros((2, 8, 128), jnp.int32) + col) > 0
    right_ok = (jnp.zeros((2, 8, 128), jnp.int32) + col) < 7

    taken = jnp.where(from_left & jnp.logical_not(left_ok), 0.0, lanes_of_runs(cnt))
    cnt[3] = jnp.where(from_right & jnp.logical_not(right_ok), 0.0, taken)

    def unpack(g, carry):
        gl = xr[0, g].astype(f32).reshape(2, 8, 128)
        gr = xr[1, g].astype(f32).reshape(2, 8, 128)
        for q in range(4):
            o = u[3, 4 * g + q]
            a = pltpu.roll(gl, (16 - 8 * q) % 128, 2)
            c = pltpu.roll(gr, (8 - 8 * q) % 128, 2)
            o = jnp.where(from_left, jnp.where(left_ok, a, 0.0), o)
            o = jnp.where(from_right, jnp.where(right_ok, c, 0.0), o)
            u[3, 4 * g + q] = o
            k = o[0]
            for b in range(3):
                k = jnp.where(lane[0] // 32 == b, pltpu.roll(o[0], 32 * (b + 1), 1), k)
            cb[2, 4 * g + q] = jnp.where(lane[0] < 96, k, 0.0)
        return carry

    lax.fori_loop(2, GROUPS - 2, unpack, 0)
    clear(3)

    @pl.when(row == 0)
    def _():
        cb[2, 8:16] = jnp.zeros((8, 8, 128), f32)

    @pl.when(row == 7)
    def _():
        cb[2, 80:88] = jnp.zeros((8, 8, 128), f32)

    def shift_conduct(g, carry):
        for q in range(4):
            for side in (0, 2):
                cb[side + 1, 4 * g + q] = pltpu.roll(cb[side, 4 * g + q], 127, 1)
        return carry

    lax.fori_loop(2, GROUPS - 2, shift_conduct, 0)
    first, last = lane == 0, lane == 127

    def run_step(s, with_main):
        blocks = (0, 1, 2, 3) if with_main else (3,)
        count = range(len(blocks))
        ahead_s = s + 1 if with_main else s
        coef = [nl[b] for b in blocks]
        active = [jnp.where(cnt[b] > (s if b < 3 else ahead_s).astype(f32), 1.0, 0.0) for b in blocks]
        begin = (9 + s) // 4

        def kappa(v, i, n, shifted=0):
            return cb[(2 if blocks[n] == 3 else 0) + shifted, i][None] / (1.0 + coef[n] * v * v)

        def ahead(i, vs):
            out = []
            for n, b in enumerate(blocks):
                v = vs[n]
                k = kappa(v, i, n)
                vr = pltpu.roll(v, 127, 2)
                across = (k + kappa(vr, i, n, 1)) * (vr - v)
                if b < 3:
                    across = jnp.where(last, fx[b, s % 2, i], across)
                out.append((k, across))
            return out

        def keep(g, q, made):
            for n, (k, across) in enumerate(made):
                ks[blocks[n], (g % 2) * 4 + q] = k
                ac[blocks[n], (g % 2) * 4 + q] = across

        flows = []
        for q in range(4):
            vs = [u[b, 4 * begin + q] for b in blocks]
            made = ahead(4 * begin + q, vs)
            keep(begin, q, made)
            if q == 0:
                for n, b in enumerate(blocks):
                    before = u[b, 4 * begin - 1]
                    flows.append((made[n][0] + kappa(before, 4 * begin - 1, n)) * (vs[n] - before))

        def group(g, flow):
            flow = list(flow)
            base, now = 4 * g, (g % 2) * 4
            v = [[u[b, base + q] for b in blocks] for q in range(4)]
            k = [[ks[b, now + q] for b in blocks] for q in range(4)]
            a = [[ac[b, now + q] for b in blocks] for q in range(4)]
            v_next = [[u[b, base + 4 + q] for b in blocks] for q in range(4)]
            first_made = None
            for q in range(4):
                made = ahead(base + 4 + q, v_next[q])
                first_made = made if q == 0 else first_made
                for n, b in enumerate(blocks):
                    vn = v[q + 1][n] if q < 3 else v_next[0][n]
                    kn = k[q + 1][n] if q < 3 else first_made[n][0]
                    flow_n = (k[q][n] + kn) * (vn - v[q][n])
                    came = pltpu.roll(a[q][n], 1, 2)
                    if b == 3:
                        f = jnp.where(in32 == 8, pltpu.roll(a[q][n], 113, 2), a[q][n])
                        for to in range(3):
                            fx[to, ahead_s % 2, base + q] = pltpu.roll(f, 120 - 32 * to, 2)
                    else:
                        came = jnp.where(first, fx[b, s % 2, base + q], came)
                    new = v[q][n] + active[n] * ((flow_n - flow[n]) + (a[q][n] - came))
                    u[b, base + q] = new
                    if b < 3:
                        snap[2 * (g % 2) + q // 2, 2 * (g // 2) - 2 + q % 2, s, 16 * b : 16 * b + 16, :] = (
                            new.reshape(16, 128).astype(bf16)
                        )
                    flow[n] = flow_n
                keep(g + 1, q, made)
            return tuple(flow)

        lax.fori_loop(begin, GROUPS - begin, group, tuple(flows))
        for b in blocks:
            clear(b)

    pass_round(0, 0)
    run_step(jnp.int32(0), False)

    def one_step(s, carry):
        run_step(s, True)
        for at, hh, kk in ((0, 0, 1), (1, 0, 2), (3, 0, 3), (4, 1, 0), (5, 1, 1), (6, 1, 2)):

            @pl.when(s == at)
            def _():
                pass_round(hh, kk)

        return carry

    lax.fori_loop(0, 8, one_step, 0)

    pass_round(1, 3)

    def give_back(n, carry):
        for q in range(4):
            for b in range(3):
                fs[pl.ds(b * 1024 + 4 * n + q, 16, stride=64), :] = u[b, 4 * n + q + 16].reshape(16, 128)
        return carry

    lax.fori_loop(0, 16, give_back, 0)
    out_copy = pltpu.make_async_copy(fs3, final, loc_sem.at[2])
    out_copy.start()

    def square(n, total):
        x = snap[n // 16, 2 + n % 16].astype(f32).reshape(48, 8, 128)
        return total + jnp.sum(x * x, axis=0)

    squares = lax.fori_loop(0, 64, square, jnp.zeros((8, 128), f32))

    for hh in range(2):
        for kk in range(4):
            fwd_copy(hh, kk).wait_recv()

            lhs = jnp.concatenate([snap[kk, 2 + i].reshape(384, 128) for i in range(16)], axis=1)
            rhs = jnp.concatenate(
                [
                    jnp.concatenate(
                        [
                            dl[kk, i, 128 * hh : 128 * hh + 128, :],
                            dl[kk, i, 256 + 128 * hh : 384 + 128 * hh, :],
                        ],
                        axis=0,
                    )
                    for i in range(16)
                ],
                axis=1,
            )
            got = lax.dot_general(lhs, rhs, nt, preferred_element_type=f32)
            acc[hh] = got if kk == 0 else acc[hh] + got

    total = squares
    for hh in range(2):
        for half in range(2):
            at = slice(256 * half + 128 * hh, 256 * half + 128 * hh + 128)
            a = part[2 * half + hh]
            c = acc[hh, :, 128 * half : 128 * half + 128]
            part[2 * half + hh] = a - c
            total = total + jnp.sum((hid[:, at].astype(f32) * (a - 2.0 * c)).reshape(48, 8, 128), axis=0)
    loss[...] = total

    out_copy.wait()
    each_row_copy(may_send, lambda c: c.wait_send())
    for c in col_copies:
        c.wait_send()
    for hh in range(2):
        for kk in range(4):
            for c in dec_copies(hh, kk):
                c.wait_send()
            fwd_copy(hh, kk).wait_send()


def reduce_kernel(
    part, loss_in, desc, code, w_in, bias, w_out,
    new_in, new_bias, new_out, loss_out,
    code_wide, rows, act, slope, grad, back, r1, l1, l2, got, send1, recv1, send2, recv2, lsend, lrecv, lsend2, xsend, xrecv,
):
    core, row, col = (lax.axis_index(n) for n in ("run", "row", "col"))
    x, y, z = row % 4, col // 2, (col % 2) * 2 + row // 4
    sibling = (1 - core, row, col)
    me = row * 8 + col

    def chip(j):
        x1, y1, z1 = (x + j % 4) % 4, (y + j // 4 % 4) % 4, (z + j // 16) % 4
        return (z1 % 2) * 4 + x1, y1 * 2 + z1 // 2

    offsets = list(range(1, 64))
    offsets.sort(key=lambda j: -sum(min(d, 4 - d) for d in (j % 4, j // 4 % 4, j // 16)))
    peers = [(core, *chip(j)) for j in offsets]

    def piece(p):
        return part.at[p // 16, pl.ds(pl.multiple_of(24 * (p % 16), 8), 24), :]

    first = []
    for n, j in enumerate(offsets):
        r, c = chip(j)
        first.append(remote(piece(r * 8 + c), r1.at[n], send1.at[n], recv1.at[n], peers[n]))
    to_zero = remote(loss_in, l1.at[me], lsend, lrecv.at[me], (core, 0, 0))

    @pl.when(me > 0)
    def _():
        to_zero.start()

    for c in first:
        c.start()

    code_wide[...] = code[...].astype(f32)

    def trunk(n, carry):
        at = pl.multiple_of(48 * n, 48)
        half = pl.multiple_of(48 * (n // 8), 48)
        rows_n = (desc[pl.ds(half, 48), :].astype(f32) + code_wide[pl.ds(n % 8, 1), :]).astype(bf16)
        pre = jnp.dot(rows_n, w_in[...], preferred_element_type=f32) + bias[...]
        value, pull = jax.vjp(jax.nn.gelu, pre)
        rows[pl.ds(at, 48), :] = rows_n
        act[pl.ds(at, 48), :] = value.astype(bf16)
        slope[pl.ds(at, 48), :] = pull(jnp.ones_like(pre))[0]
        return carry

    lax.fori_loop(0, 16, trunk, 0)
    total = part[me // 16, pl.ds(pl.multiple_of(24 * (me % 16), 8), 24), :]
    for n, c in enumerate(first):
        c.wait_recv()
        total = total + r1[n]
    got[core, me] = jnp.concatenate([total * (1.0 / 768.0), jnp.zeros((8, 128), f32)], axis=0).astype(bf16)

    second = [remote(got.at[core, me], got.at[core, me], send2.at[n], recv2.at[n], peers[n]) for n in range(63)]
    for c in second:
        c.start()
    spread_loss = [remote(l2.at[core], l2.at[core], lsend2.at[n], lrecv.at[64], peers[n]) for n in range(63)]

    @pl.when(me == 0)
    def _():
        sums = loss_in[...]
        for p in range(1, 64):
            remote(loss_in, l1.at[p], lsend, lrecv.at[p], (core, 0, 0)).wait_recv()
            sums = sums + l1[p]
        l2[core] = sums
        for c in spread_loss:
            c.start()

    for c in second:
        c.wait_recv()
    cross = remote(got.at[core], got.at[core], xsend.at[0], xrecv.at[0], sibling)
    cross.start()

    @pl.when(me > 0)
    def _():
        spread_loss[0].wait_recv()

    cross_loss = remote(l2.at[core], l2.at[core], xsend.at[1], xrecv.at[1], sibling)
    cross_loss.start()

    def place(own):
        for t in range(4):
            for q in range(8):
                pair = jnp.concatenate(
                    [got[own, 16 * t + 2 * q + i].astype(f32)[0:24] for i in range(2)], axis=0
                ).astype(bf16)
                grad[pl.ds(pl.multiple_of(384 * own + 48 * q, 48), 48), 128 * t : 128 * t + 128] = pair

    place(core)
    cross.wait_recv()
    place(1 - core)
    tn = (((0,), (0,)), ((), ()))
    new_out[...] = w_out[...].astype(f32) - RATE * lax.dot_general(
        act[...], grad[...], tn, preferred_element_type=f32
    )
    back[...] = (
        lax.dot_general(grad[...], w_out[...], (((1,), (1,)), ((), ())), preferred_element_type=f32) * slope[...]
    )
    new_bias[...] = bias[...] - RATE * jnp.sum(back[...], axis=0, keepdims=True)
    new_in[...] = w_in[...].astype(f32) - RATE * lax.dot_general(
        rows[...], back[...].astype(bf16), tn, preferred_element_type=f32
    )
    cross_loss.wait_recv()
    loss_out[...] = jnp.sum(l2[0] + l2[1], keepdims=True) * (1.0 / (768 * 512 * 1024))

    @pl.when(me > 0)
    def _():
        to_zero.wait_send()

    @pl.when(me == 0)
    def _():
        for c in spread_loss:
            c.wait_send()

    for c in first + second + [cross, cross_loss]:
        c.wait_send()


def per_device(
    init_field, conduct, nonlin, counts, descriptors, time_code, w_in, bias_in, w_out, decoder
):
    bias_row = bias_in.reshape(1, 512)
    vmem = pl.BlockSpec(memory_space=pltpu.VMEM)
    hbm = pl.BlockSpec(memory_space=pl.ANY)
    dma = pltpu.SemaphoreType.DMA
    first = [
        pltpu.VMEM((4, 2, 8, 128), f32),
        pltpu.VMEM((4, 2, 8, 128), f32),
        pltpu.VMEM((384, 512), bf16),
        pltpu.VMEM((3072, 128), f32),
        pltpu.VMEM((80, 128), f32),
        pltpu.VMEM((4, ROWS, 2, 8, 128), f32),
        pltpu.VMEM((4, ROWS, 8, 128), f32),
        pltpu.VMEM((2, 8, 3, 16, 128), bf16),
        pltpu.VMEM((2, 8, 3, 16, 128), bf16),
        pltpu.VMEM((2, GROUPS, 16, 128), bf16),
        pltpu.VMEM((2, GROUPS, 16, 128), bf16),
        pltpu.VMEM((3, 2, ROWS, 2, 8, 128), f32),
        pltpu.VMEM((4, 8, 2, 8, 128), f32),
        pltpu.VMEM((4, 8, 2, 8, 128), f32),
        pltpu.VMEM((4, 20, 8, 48, 128), bf16),
        pltpu.VMEM((8, 8, 512, 128), bf16),
        pltpu.VMEM((4, 16, 512, 128), bf16),
        pltpu.VMEM((2, 1024, 1024), bf16),
        pltpu.VMEM((8, 256, 128), f32),
        pltpu.VMEM((512, 512), f32),
        pltpu.VMEM((2, 384, 256), f32),
        dma((3,)), dma((2,)), dma((4,)), dma((4,)), dma((2,)), dma((2,)),
        dma((8, 7)), dma((8, 7)), dma((8,)), dma((8,)), dma((8,)),
    ]
    second = [
        pltpu.VMEM((8, 256), f32),
        pltpu.VMEM((768, 256), bf16),
        pltpu.VMEM((768, 512), bf16),
        pltpu.VMEM((768, 512), f32),
        pltpu.VMEM((768, 512), bf16),
        pltpu.VMEM((768, 512), f32),
        pltpu.VMEM((63, 24, 128), f32),
        pltpu.VMEM((64, 8, 128), f32),
        pltpu.VMEM((2, 8, 128), f32),
        pltpu.VMEM((2, 64, 32, 128), bf16),
        dma((63,)), dma((63,)), dma((63,)), dma((63,)), dma(()), dma((65,)), dma((63,)), dma((2,)), dma((2,)),
    ]
    part_and_loss = [pltpu.VMEM((4, 384, 128), f32), pltpu.VMEM((8, 128), f32)]

    def whole_kernel(field, cond, nonlin, counts, desc, code, w_in, bias, w_out, dec, final, new_in, new_bias, new_out, total, part, loss, *rest):
        main_kernel(field, cond, nonlin, counts, desc, code, w_in, bias, w_out, dec, final, part, loss, *rest[: len(first)])
        reduce_kernel(
            part, loss, desc, code, w_in, bias, w_out, new_in, new_bias, new_out, total, *rest[len(first) :]
        )

    final, new_w_in, new_bias, new_w_out, loss_sum = pl.pallas_call(
        whole_kernel,
        name="solve_and_learn",
        out_shape=(
            jax.ShapeDtypeStruct((48, 64, 128), f32),
            jax.ShapeDtypeStruct((256, 512), f32),
            jax.ShapeDtypeStruct((1, 512), f32),
            jax.ShapeDtypeStruct((512, 512), f32),
            jax.ShapeDtypeStruct((1, 1), f32),
        ),
        in_specs=[hbm, hbm] + [pl.BlockSpec(memory_space=pltpu.SMEM)] * 2 + [vmem] * 5 + [hbm],
        out_specs=(hbm, vmem, vmem, vmem, vmem),
        scratch_shapes=part_and_loss + first + second,
        compiler_params=pltpu.CompilerParams(
            collective_id=0, has_side_effects=True, vmem_limit_bytes=VMEM_ALL - (1 << 16)
        ),
    )(
        init_field, conduct, nonlin, counts,
        descriptors, time_code, w_in, bias_row, w_out, decoder.reshape(4096, 1024),
    )
    mean_loss = loss_sum.reshape(())
    return final, new_w_in, new_bias.reshape(512), new_w_out, mean_loss


def solution(mesh):
    in_specs = (
        P("run", "row", "col"), P("row", "col"), P("run"), P("run"), P(), P(), P(), P(), P(),
        P(None, ("row", "col"), None),
    )
    out_specs = (P("run", "row", "col"), P(), P(), P(), P())
    return jax.shard_map(
        per_device, mesh=mesh, in_specs=in_specs, out_specs=out_specs, check_vma=False
    )
```

```python
import jax
import jax.numpy as jnp
from jax import lax
from jax.experimental import pallas as pl
from jax.experimental.pallas import tpu as pltpu
from jax.sharding import PartitionSpec as P

MESH = pl.DeviceIdType.MESH
f32, bf16 = jnp.float32, jnp.bfloat16
STEP, RATE = 0.12, 0.5
ROWS = 96
GROUPS = ROWS // 4
OFFSETS = ((2, 1), (1, 1), (3, 1), (2, 0), (0, 1), (1, 0), (3, 0))
VMEM_ALL = 64 << 20


def signal_all(peers):
    barrier = pltpu.get_barrier_semaphore()
    for peer in peers:
        pl.semaphore_signal(barrier, inc=1, device_id=peer, device_id_type=MESH)
    pl.semaphore_wait(barrier, len(peers))


def remote(src, dst, send, recv, peer):
    return pltpu.make_async_remote_copy(
        src_ref=src, dst_ref=dst, send_sem=send, recv_sem=recv, device_id=peer, device_id_type=MESH
    )


def main_kernel(
    on_half, field, conduct, nonlin, counts, desc, code, w_in, bias, w_out, decoder,
    final, part, loss,
    nl, cnt, hid, fs, cd, u, cb, rs, rr, xs, xr, fx, ks, ac, snap, tr, dl, raw, tf, gram, acc,
    loc_sem, raw_sem, row_send, row_recv, col_send, col_recv, dec_send, dec_recv, own_sem, fwd_send, fwd_recv,
):
    core, row, col = (lax.axis_index(n) for n in ("run", "row", "col"))
    y, zh = col // 2, col % 2
    sibling = (1 - core, row, col)
    down, up = (core, (row + 1) % 8, col), (core, (row + 7) % 8, col)
    right, left = (core, row, (col + 1) % 8), (core, row, (col + 7) % 8)
    targets = [((y + dy) % 4) * 2 + (zh + dz) % 2 for dy, dz in OFFSETS]
    signal_all([(core, q // 8, q % 8) for q in [(row * 8 + col + j) % 64 for j in range(1, 64)]] + [sibling])

    fs3 = fs.reshape(48, 64, 128)
    rows_of_conduct = [conduct.at[pl.ds(56, 8), :], conduct.at[pl.ds(0, 8), :]]

    def row_copies(way):
        peer = (down, up)[way]
        return [
            remote(rs.at[way], rr.at[way], row_send.at[way], row_recv.at[way], peer),
            remote(
                rows_of_conduct[way], cd.at[pl.ds(72 * way, 8), :], row_send.at[2 + way], row_recv.at[2 + way], peer
            ),
        ]

    may_send = [row < 7, row > 0]
    may_get = [row > 0, row < 7]

    def each_row_copy(allowed, act):
        for way in range(2):

            @pl.when(allowed[way])
            def _():
                for c in row_copies(way):
                    act(c)

    loc_copies = [
        pltpu.make_async_copy(field, fs3, loc_sem.at[0]),
        pltpu.make_async_copy(conduct, cd.at[pl.ds(8, 64), :], loc_sem.at[1]),
    ]

    def raw_copy(part_at, slot):
        start = pl.multiple_of(part_at * 1024, 1024)
        return pltpu.make_async_copy(decoder.at[pl.ds(start, 1024), :], raw.at[slot], raw_sem.at[slot])

    mine, other = 2 * core, 2 * (1 - core)

    def turn(quarter, slot):
        def piece(hb, carry):
            at = pl.multiple_of(hb * 256, 256)
            to = pl.multiple_of(quarter * 128 + hb * 32, 32)
            for t in range(8):
                tf[t] = raw[slot, pl.ds(at, 256), t * 128 : (t + 1) * 128].astype(f32)
            for t in range(8):
                for i in range(8):
                    tr[t, i, pl.ds(to, 32), :] = tf[t, pl.ds(i, 32, stride=8), :].astype(bf16)
            return carry

        lax.fori_loop(0, 4, piece, 0)

    def dec_copies(hh, kk):
        h0 = pl.multiple_of((mine + hh) * 128, 128)
        rnd = hh * 4 + kk
        out = []
        for j, t in enumerate(targets):
            out.append(
                remote(
                    tr.at[t, pl.ds(2 * kk, 2), pl.ds(h0, 128), :],
                    dl.at[kk, pl.ds(2 * col, 2), pl.ds(h0, 128), :],
                    dec_send.at[rnd, j], dec_recv.at[rnd, j], (core, row, t),
                )
            )
        return out

    def own_copy(hh, kk):
        h0 = pl.multiple_of((mine + hh) * 128, 128)
        return pltpu.make_async_copy(
            tr.at[col, pl.ds(2 * kk, 2), pl.ds(h0, 128), :],
            dl.at[kk, pl.ds(2 * col, 2), pl.ds(h0, 128), :],
            own_sem.at[hh * 4 + kk],
        )

    def fwd_copy(hh, kk):
        h0 = pl.multiple_of((mine + hh) * 128, 128)
        block = dl.at[kk, :, pl.ds(h0, 128), :]
        return remote(block, block, fwd_send.at[hh * 4 + kk], fwd_recv.at[hh * 4 + kk], sibling)

    def send_round(hh, kk):
        for c in dec_copies(hh, kk):
            c.start()
        own_copy(hh, kk).start()

    def pass_round(hh, kk):
        for c in dec_copies(hh, kk):
            c.wait_recv()
        own_copy(hh, kk).wait()
        fwd_copy(hh, kk).start()

    for c in loc_copies:
        c.start()
    raw_copy(mine, 0).start()
    raw_copy(mine + 1, 1).start()
    for c in loc_copies:
        c.wait()

    def pack_rows(i, carry):
        for b in range(3):
            for way in range(2):
                rs[way, i, b] = fs[pl.ds(b * 1024 + i + 56 * (1 - way), 16, stride=64), :].astype(bf16)
        return carry

    lax.fori_loop(0, 8, pack_rows, 0)
    each_row_copy(may_send, lambda c: c.start())
    raw_copy(mine, 0).wait()
    turn(mine, 0)
    raw_copy(other, 0).start()
    send_round(0, 0)

    for b in range(3):
        u[b, 0:8] = jnp.zeros((8, 2, 8, 128), f32)
        u[b, 88:96] = jnp.zeros((8, 2, 8, 128), f32)

    def fill(n, carry):
        for q in range(4):
            i = 4 * n + q
            for b in range(3):
                u[b, i + 16] = fs[pl.ds(b * 1024 + i, 16, stride=64), :].reshape(2, 8, 128)
        return carry

    lax.fori_loop(0, 16, fill, 0)

    each_row_copy(may_get, lambda c: c.wait_recv())

    def unpack_rows(i, carry):
        for b in range(3):
            for way in range(2):
                u[b, i + 8 + 72 * way] = rr[way, i, b].astype(f32).reshape(2, 8, 128)
        return carry

    lax.fori_loop(0, 8, unpack_rows, 0)

    def fill_conduct(n, carry):
        for q in range(4):
            i = 4 * n + q
            cb[0, i + 8] = jnp.broadcast_to(cd[pl.ds(i, 1), :] * (0.5 * STEP), (8, 128))
        return carry

    lax.fori_loop(0, 20, fill_conduct, 0)
    for s in range(4):
        cb[s, 0:8] = jnp.zeros((8, 8, 128), f32)
        cb[s, 88:96] = jnp.zeros((8, 8, 128), f32)

    def clear(b):
        @pl.when(row == 0)
        def _():
            u[b, 8:16] = jnp.zeros((8, 2, 8, 128), f32)

        @pl.when(row == 7)
        def _():
            u[b, 80:88] = jnp.zeros((8, 2, 8, 128), f32)

    for b in range(3):
        clear(b)

    @pl.when(row == 0)
    def _():
        cb[0, 8:16] = jnp.zeros((8, 8, 128), f32)

    @pl.when(row == 7)
    def _():
        cb[0, 80:88] = jnp.zeros((8, 8, 128), f32)

    lane = lax.broadcasted_iota(jnp.int32, (2, 8, 128), 2)
    in32 = lane % 32

    def gather_edges(i):
        out = None
        for b in range(4):
            v = u[b, i] if b < 3 else jnp.broadcast_to(cb[0, i][None], (2, 8, 128))
            ends = pltpu.roll(v, (32 * b + 8) % 128, 2)
            starts = pltpu.roll(v, (32 * b + 24) % 128, 2)
            both = jnp.where(in32 < 8, ends, starts)
            out = both if b == 0 else jnp.where(lane // 32 == b, both, out)
        return out

    def pack(g, carry):
        to_right = to_left = None
        for q in range(4):
            o = gather_edges(4 * g + q)
            u[3, 4 * g + q] = o
            r = pltpu.roll(o, 8 * q, 2) if q else o
            l = pltpu.roll(o, (8 * q + 8) % 32 + 96 if q < 3 else 0, 2) if q < 3 else pltpu.roll(o, 0, 2)
            here = in32 // 8 == q
            to_right = r if q == 0 else jnp.where(here, r, to_right)
            to_left = l if q == 0 else jnp.where(here, l, to_left)
        xs[0, g] = to_right.reshape(16, 128).astype(bf16)
        xs[1, g] = to_left.reshape(16, 128).astype(bf16)
        return carry

    lax.fori_loop(2, GROUPS - 2, pack, 0)
    col_copies = [
        remote(xs.at[0, pl.ds(2, 20)], xr.at[0, pl.ds(2, 20)], col_send.at[0], col_recv.at[0], right),
        remote(xs.at[1, pl.ds(2, 20)], xr.at[1, pl.ds(2, 20)], col_send.at[1], col_recv.at[1], left),
    ]
    for c in col_copies:
        c.start()
    raw_copy(mine + 1, 1).wait()
    turn(mine + 1, 1)
    raw_copy(other + 1, 1).start()
    raw_copy(other, 0).wait()
    turn(other, 0)
    for rnd in range(1, 8):
        send_round(rnd // 4, rnd % 4)
    raw_copy(other + 1, 1).wait()
    turn(other + 1, 1)

    wide = desc[pl.ds(pl.multiple_of(core * 48, 16), 48), :].astype(f32)
    for s in range(8):
        rows_s = (wide + code[s : s + 1, :].astype(f32)).astype(bf16)
        act_s = jax.nn.gelu(jnp.dot(rows_s, w_in[...], preferred_element_type=f32) + bias[...]).astype(bf16)
        hid[48 * s : 48 * s + 48, :] = jnp.dot(act_s, w_out[...], preferred_element_type=f32).astype(bf16)

    gram[...] = jnp.zeros((512, 512), f32)
    nt = (((1,), (1,)), ((), ()))

    def add_gram(t, carry):
        x = jnp.concatenate([tr[t, i] for i in range(8)], axis=1)
        gram[0:256] += lax.dot_general(x[0:256], x, nt, preferred_element_type=f32)
        gram[256:512, 256:512] += lax.dot_general(x[256:512], x[256:512], nt, preferred_element_type=f32)
        return carry

    lax.fori_loop(0, 8, add_gram, 0)
    gram[256:512, 0:256] = gram[0:256, 256:512].T
    big = gram[...].astype(bf16)
    small = (gram[...] - big.astype(f32)).astype(bf16)
    product = jnp.dot(hid[...], big, preferred_element_type=f32) + jnp.dot(
        hid[...], small, preferred_element_type=f32
    )
    for t in range(4):
        part[t] = product[:, 128 * t : 128 * t + 128]

    for c in col_copies:
        c.wait_recv()

    place_of = lax.broadcasted_iota(jnp.int32, (2, 8, 128), 0) * 8 + lax.broadcasted_iota(jnp.int32, (2, 8, 128), 1)

    def of_runs(ref, b):
        out = jnp.zeros((2, 8, 128), f32)
        for i in range(16):
            out = jnp.where(place_of == i, ref[16 * b + i].astype(f32), out)
        return out

    def lanes_of_runs(made):
        out = jnp.zeros((2, 8, 128), f32)
        for b in range(3):
            out = jnp.where(lane // 32 == b, made[b], out)
        return out

    for b in range(3):
        nl[b] = of_runs(nonlin, b)
        cnt[b] = of_runs(counts, b)
    nl[3] = lanes_of_runs(nl)

    u[3, 0:8] = jnp.zeros((8, 2, 8, 128), f32)
    u[3, 88:96] = jnp.zeros((8, 2, 8, 128), f32)
    from_left = (in32 >= 16) & (in32 < 24)
    from_right = (in32 >= 8) & (in32 < 16)
    left_ok = (jnp.zeros((2, 8, 128), jnp.int32) + col) > 0
    right_ok = (jnp.zeros((2, 8, 128), jnp.int32) + col) < 7

    taken = jnp.where(from_left & jnp.logical_not(left_ok), 0.0, lanes_of_runs(cnt))
    cnt[3] = jnp.where(from_right & jnp.logical_not(right_ok), 0.0, taken)

    def unpack(g, carry):
        gl = xr[0, g].astype(f32).reshape(2, 8, 128)
        gr = xr[1, g].astype(f32).reshape(2, 8, 128)
        for q in range(4):
            o = u[3, 4 * g + q]
            a = pltpu.roll(gl, (16 - 8 * q) % 128, 2)
            c = pltpu.roll(gr, (8 - 8 * q) % 128, 2)
            o = jnp.where(from_left, jnp.where(left_ok, a, 0.0), o)
            o = jnp.where(from_right, jnp.where(right_ok, c, 0.0), o)
            u[3, 4 * g + q] = o
            k = o[0]
            for b in range(3):
                k = jnp.where(lane[0] // 32 == b, pltpu.roll(o[0], 32 * (b + 1), 1), k)
            cb[2, 4 * g + q] = jnp.where(lane[0] < 96, k, 0.0)
        return carry

    lax.fori_loop(2, GROUPS - 2, unpack, 0)
    clear(3)

    @pl.when(row == 0)
    def _():
        cb[2, 8:16] = jnp.zeros((8, 8, 128), f32)

    @pl.when(row == 7)
    def _():
        cb[2, 80:88] = jnp.zeros((8, 8, 128), f32)

    def shift_conduct(g, carry):
        for q in range(4):
            for side in (0, 2):
                cb[side + 1, 4 * g + q] = pltpu.roll(cb[side, 4 * g + q], 127, 1)
        return carry

    lax.fori_loop(2, GROUPS - 2, shift_conduct, 0)
    first, last = lane == 0, lane == 127

    def run_step(s, with_main):
        blocks = (0, 1, 2, 3) if with_main else (3,)
        count = range(len(blocks))
        ahead_s = s + 1 if with_main else s
        coef = [nl[b] for b in blocks]
        active = [jnp.where(cnt[b] > (s if b < 3 else ahead_s).astype(f32), 1.0, 0.0) for b in blocks]
        begin = (9 + s) // 4

        def kappa(v, i, n, shifted=0):
            return cb[(2 if blocks[n] == 3 else 0) + shifted, i][None] / (1.0 + coef[n] * v * v)

        def ahead(i, vs):
            out = []
            for n, b in enumerate(blocks):
                v = vs[n]
                k = kappa(v, i, n)
                vr = pltpu.roll(v, 127, 2)
                across = (k + kappa(vr, i, n, 1)) * (vr - v)
                if b < 3:
                    across = jnp.where(last, fx[b, s % 2, i], across)
                out.append((k, across))
            return out

        def keep(g, q, made):
            for n, (k, across) in enumerate(made):
                ks[blocks[n], (g % 2) * 4 + q] = k
                ac[blocks[n], (g % 2) * 4 + q] = across

        flows = []
        for q in range(4):
            vs = [u[b, 4 * begin + q] for b in blocks]
            made = ahead(4 * begin + q, vs)
            keep(begin, q, made)
            if q == 0:
                for n, b in enumerate(blocks):
                    before = u[b, 4 * begin - 1]
                    flows.append((made[n][0] + kappa(before, 4 * begin - 1, n)) * (vs[n] - before))

        def group(g, flow):
            flow = list(flow)
            base, now = 4 * g, (g % 2) * 4
            v = [[u[b, base + q] for b in blocks] for q in range(4)]
            k = [[ks[b, now + q] for b in blocks] for q in range(4)]
            a = [[ac[b, now + q] for b in blocks] for q in range(4)]
            v_next = [[u[b, base + 4 + q] for b in blocks] for q in range(4)]
            first_made = None
            for q in range(4):
                made = ahead(base + 4 + q, v_next[q])
                first_made = made if q == 0 else first_made
                for n, b in enumerate(blocks):
                    vn = v[q + 1][n] if q < 3 else v_next[0][n]
                    kn = k[q + 1][n] if q < 3 else first_made[n][0]
                    flow_n = (k[q][n] + kn) * (vn - v[q][n])
                    came = pltpu.roll(a[q][n], 1, 2)
                    if b == 3:
                        f = jnp.where(in32 == 8, pltpu.roll(a[q][n], 113, 2), a[q][n])
                        for to in range(3):
                            fx[to, ahead_s % 2, base + q] = pltpu.roll(f, 120 - 32 * to, 2)
                    else:
                        came = jnp.where(first, fx[b, s % 2, base + q], came)
                    new = v[q][n] + active[n] * ((flow_n - flow[n]) + (a[q][n] - came))
                    u[b, base + q] = new
                    if b < 3:
                        snap[2 * (g % 2) + q // 2, 2 * (g // 2) - 2 + q % 2, s, 16 * b : 16 * b + 16, :] = (
                            new.reshape(16, 128).astype(bf16)
                        )
                    flow[n] = flow_n
                keep(g + 1, q, made)
            return tuple(flow)

        lax.fori_loop(begin, GROUPS - begin, group, tuple(flows))
        for b in blocks:
            clear(b)

    pass_round(0, 0)
    run_step(jnp.int32(0), False)

    def one_step(s, carry):
        run_step(s, True)
        for at, hh, kk in ((0, 0, 1), (1, 0, 2), (3, 0, 3), (4, 1, 0), (5, 1, 1), (6, 1, 2)):

            @pl.when(s == at)
            def _():
                pass_round(hh, kk)

        return carry

    lax.fori_loop(0, 8, one_step, 0)

    pass_round(1, 3)

    def give_back(n, carry):
        for q in range(4):
            for b in range(3):
                fs[pl.ds(b * 1024 + 4 * n + q, 16, stride=64), :] = u[b, 4 * n + q + 16].reshape(16, 128)
        return carry

    lax.fori_loop(0, 16, give_back, 0)
    out_copy = pltpu.make_async_copy(fs3, final, loc_sem.at[2])
    out_copy.start()

    def square(n, total):
        x = snap[n // 16, 2 + n % 16].astype(f32).reshape(48, 8, 128)
        return total + jnp.sum(x * x, axis=0)

    squares = lax.fori_loop(0, 64, square, jnp.zeros((8, 128), f32))

    total = squares
    for hh in range(2):
        for kk in range(4):
            fwd_copy(hh, kk).wait_recv()

            lhs = jnp.concatenate([snap[kk, 2 + i].reshape(384, 128) for i in range(16)], axis=1)
            rhs = jnp.concatenate(
                [
                    jnp.concatenate(
                        [
                            dl[kk, i, 128 * hh : 128 * hh + 128, :],
                            dl[kk, i, 256 + 128 * hh : 384 + 128 * hh, :],
                        ],
                        axis=0,
                    )
                    for i in range(16)
                ],
                axis=1,
            )
            got = lax.dot_general(lhs, rhs, nt, preferred_element_type=f32)
            acc[hh] = got if kk == 0 else acc[hh] + got

        for half in range(2):
            at = slice(256 * half + 128 * hh, 256 * half + 128 * hh + 128)
            a = part[2 * half + hh]
            c = acc[hh, :, 128 * half : 128 * half + 128]
            part[2 * half + hh] = a - c
            total = total + jnp.sum((hid[:, at].astype(f32) * (a - 2.0 * c)).reshape(48, 8, 128), axis=0)
        on_half(hh)

    loss[...] = total

    out_copy.wait()
    each_row_copy(may_send, lambda c: c.wait_send())
    for c in col_copies:
        c.wait_send()
    for hh in range(2):
        for kk in range(4):
            for c in dec_copies(hh, kk):
                c.wait_send()
            fwd_copy(hh, kk).wait_send()


def piece_copies(part, r1, send1, recv1):
    core, row, col = (lax.axis_index(n) for n in ("run", "row", "col"))
    x, y, z = row % 4, col // 2, (col % 2) * 2 + row // 4

    def chip(j):
        x1, y1, z1 = (x + j % 4) % 4, (y + j // 4 % 4) % 4, (z + j // 16) % 4
        return (z1 % 2) * 4 + x1, y1 * 2 + z1 // 2

    offsets = list(range(1, 64))
    offsets.sort(key=lambda j: -sum(min(d, 4 - d) for d in (j % 4, j // 4 % 4, j // 16)))
    peers = [(core, *chip(j)) for j in offsets]

    def piece(p):
        return part.at[p // 16, pl.ds(pl.multiple_of(24 * (p % 16), 8), 24), :]

    first, halves = [], []
    for n, j in enumerate(offsets):
        r, c = chip(j)
        halves.append((r * 8 + c) // 16 % 2)
        first.append(remote(piece(r * 8 + c), r1.at[n], send1.at[n], recv1.at[n], peers[n]))
    return first, peers, halves


def reduce_kernel(
    pieces, part, loss_in, desc, code, w_in, bias, w_out,
    new_in, new_bias, new_out, loss_out,
    code_wide, rows, act, slope, grad, back, r1, l1, l2, got, send1, recv1, send2, recv2, lsend, lrecv, lsend2, xsend, xrecv,
):
    core, row, col = (lax.axis_index(n) for n in ("run", "row", "col"))
    x, y, z = row % 4, col // 2, (col % 2) * 2 + row // 4
    sibling = (1 - core, row, col)
    me = row * 8 + col

    first, peers = pieces

    to_zero = remote(loss_in, l1.at[me], lsend, lrecv.at[me], (core, 0, 0))

    @pl.when(me > 0)
    def _():
        to_zero.start()


    code_wide[...] = code[...].astype(f32)

    def trunk(n, carry):
        at = pl.multiple_of(48 * n, 48)
        half = pl.multiple_of(48 * (n // 8), 48)
        rows_n = (desc[pl.ds(half, 48), :].astype(f32) + code_wide[pl.ds(n % 8, 1), :]).astype(bf16)
        pre = jnp.dot(rows_n, w_in[...], preferred_element_type=f32) + bias[...]
        value, pull = jax.vjp(jax.nn.gelu, pre)
        rows[pl.ds(at, 48), :] = rows_n
        act[pl.ds(at, 48), :] = value.astype(bf16)
        slope[pl.ds(at, 48), :] = pull(jnp.ones_like(pre))[0]
        return carry

    lax.fori_loop(0, 16, trunk, 0)
    total = part[me // 16, pl.ds(pl.multiple_of(24 * (me % 16), 8), 24), :]
    for n, c in enumerate(first):
        c.wait_recv()
        total = total + r1[n]
    got[core, me] = jnp.concatenate([total * (1.0 / 768.0), jnp.zeros((8, 128), f32)], axis=0).astype(bf16)

    second = [remote(got.at[core, me], got.at[core, me], send2.at[n], recv2.at[n], peers[n]) for n in range(63)]
    for c in second:
        c.start()
    spread_loss = [remote(l2.at[core], l2.at[core], lsend2.at[n], lrecv.at[64], peers[n]) for n in range(63)]

    @pl.when(me == 0)
    def _():
        sums = loss_in[...]
        for p in range(1, 64):
            remote(loss_in, l1.at[p], lsend, lrecv.at[p], (core, 0, 0)).wait_recv()
            sums = sums + l1[p]
        l2[core] = sums
        for c in spread_loss:
            c.start()

    for c in second:
        c.wait_recv()
    cross = remote(got.at[core], got.at[core], xsend.at[0], xrecv.at[0], sibling)
    cross.start()

    @pl.when(me > 0)
    def _():
        spread_loss[0].wait_recv()

    cross_loss = remote(l2.at[core], l2.at[core], xsend.at[1], xrecv.at[1], sibling)
    cross_loss.start()

    def place(own):
        for t in range(4):
            for q in range(8):
                pair = jnp.concatenate(
                    [got[own, 16 * t + 2 * q + i].astype(f32)[0:24] for i in range(2)], axis=0
                ).astype(bf16)
                grad[pl.ds(pl.multiple_of(384 * own + 48 * q, 48), 48), 128 * t : 128 * t + 128] = pair

    tn = (((0,), (0,)), ((), ()))

    def gradients(own):
        at = pl.ds(pl.multiple_of(384 * own, 384), 384)
        g = grad[at, :]
        to_out = lax.dot_general(act[at, :], g, tn, preferred_element_type=f32)
        to_pre = (
            lax.dot_general(g, w_out[...], (((1,), (1,)), ((), ())), preferred_element_type=f32) * slope[at, :]
        )
        to_in = lax.dot_general(rows[at, :], to_pre.astype(bf16), tn, preferred_element_type=f32)
        return to_in, jnp.sum(to_pre, axis=0, keepdims=True), to_out

    place(core)
    new_in[...], new_bias[...], new_out[...] = gradients(core)
    cross.wait_recv()
    place(1 - core)
    to_in, to_bias, to_out = gradients(1 - core)
    new_out[...] = w_out[...].astype(f32) - RATE * (new_out[...] + to_out)
    new_bias[...] = bias[...] - RATE * (new_bias[...] + to_bias)
    new_in[...] = w_in[...].astype(f32) - RATE * (new_in[...] + to_in)
    cross_loss.wait_recv()
    loss_out[...] = jnp.sum(l2[0] + l2[1], keepdims=True) * (1.0 / (768 * 512 * 1024))

    @pl.when(me > 0)
    def _():
        to_zero.wait_send()

    @pl.when(me == 0)
    def _():
        for c in spread_loss:
            c.wait_send()

    for c in first + second + [cross, cross_loss]:
        c.wait_send()


def per_device(
    init_field, conduct, nonlin, counts, descriptors, time_code, w_in, bias_in, w_out, decoder
):
    bias_row = bias_in.reshape(1, 512)
    vmem = pl.BlockSpec(memory_space=pltpu.VMEM)
    hbm = pl.BlockSpec(memory_space=pl.ANY)
    dma = pltpu.SemaphoreType.DMA
    first = [
        pltpu.VMEM((4, 2, 8, 128), f32),
        pltpu.VMEM((4, 2, 8, 128), f32),
        pltpu.VMEM((384, 512), bf16),
        pltpu.VMEM((3072, 128), f32),
        pltpu.VMEM((80, 128), f32),
        pltpu.VMEM((4, ROWS, 2, 8, 128), f32),
        pltpu.VMEM((4, ROWS, 8, 128), f32),
        pltpu.VMEM((2, 8, 3, 16, 128), bf16),
        pltpu.VMEM((2, 8, 3, 16, 128), bf16),
        pltpu.VMEM((2, GROUPS, 16, 128), bf16),
        pltpu.VMEM((2, GROUPS, 16, 128), bf16),
        pltpu.VMEM((3, 2, ROWS, 2, 8, 128), f32),
        pltpu.VMEM((4, 8, 2, 8, 128), f32),
        pltpu.VMEM((4, 8, 2, 8, 128), f32),
        pltpu.VMEM((4, 20, 8, 48, 128), bf16),
        pltpu.VMEM((8, 8, 512, 128), bf16),
        pltpu.VMEM((4, 16, 512, 128), bf16),
        pltpu.VMEM((2, 1024, 1024), bf16),
        pltpu.VMEM((8, 256, 128), f32),
        pltpu.VMEM((512, 512), f32),
        pltpu.VMEM((2, 384, 256), f32),
        dma((3,)), dma((2,)), dma((4,)), dma((4,)), dma((2,)), dma((2,)),
        dma((8, 7)), dma((8, 7)), dma((8,)), dma((8,)), dma((8,)),
    ]
    second = [
        pltpu.VMEM((8, 256), f32),
        pltpu.VMEM((768, 256), bf16),
        pltpu.VMEM((768, 512), bf16),
        pltpu.VMEM((768, 512), f32),
        pltpu.VMEM((768, 512), bf16),
        pltpu.VMEM((768, 512), f32),
        pltpu.VMEM((63, 24, 128), f32),
        pltpu.VMEM((64, 8, 128), f32),
        pltpu.VMEM((2, 8, 128), f32),
        pltpu.VMEM((2, 64, 32, 128), bf16),
        dma((63,)), dma((63,)), dma((63,)), dma((63,)), dma(()), dma((65,)), dma((63,)), dma((2,)), dma((2,)),
    ]
    part_and_loss = [pltpu.VMEM((4, 384, 128), f32), pltpu.VMEM((8, 128), f32)]

    def whole_kernel(field, cond, nonlin, counts, desc, code, w_in, bias, w_out, dec, final, new_in, new_bias, new_out, total, part, loss, *rest):
        later = rest[len(first) :]
        copies, peers, halves = piece_copies(part, later[6], later[10], later[11])

        def on_half(hh):
            for c, half in zip(copies, halves):

                @pl.when(half == hh)
                def _():
                    c.start()

        main_kernel(on_half, field, cond, nonlin, counts, desc, code, w_in, bias, w_out, dec, final, part, loss, *rest[: len(first)])
        reduce_kernel(
            (copies, peers), part, loss, desc, code, w_in, bias, w_out, new_in, new_bias, new_out, total, *later
        )

    final, new_w_in, new_bias, new_w_out, loss_sum = pl.pallas_call(
        whole_kernel,
        name="solve_and_learn",
        out_shape=(
            jax.ShapeDtypeStruct((48, 64, 128), f32),
            jax.ShapeDtypeStruct((256, 512), f32),
            jax.ShapeDtypeStruct((1, 512), f32),
            jax.ShapeDtypeStruct((512, 512), f32),
            jax.ShapeDtypeStruct((1, 1), f32),
        ),
        in_specs=[hbm, hbm] + [pl.BlockSpec(memory_space=pltpu.SMEM)] * 2 + [vmem] * 5 + [hbm],
        out_specs=(hbm, vmem, vmem, vmem, vmem),
        scratch_shapes=part_and_loss + first + second,
        compiler_params=pltpu.CompilerParams(
            collective_id=0, has_side_effects=True, vmem_limit_bytes=VMEM_ALL - (1 << 16)
        ),
    )(
        init_field, conduct, nonlin, counts,
        descriptors, time_code, w_in, bias_row, w_out, decoder.reshape(4096, 1024),
    )
    mean_loss = loss_sum.reshape(())
    return final, new_w_in, new_bias.reshape(512), new_w_out, mean_loss


def solution(mesh):
    in_specs = (
        P("run", "row", "col"), P("row", "col"), P("run"), P("run"), P(), P(), P(), P(), P(),
        P(None, ("row", "col"), None),
    )
    out_specs = (P("run", "row", "col"), P(), P(), P(), P())
    return jax.shard_map(
        per_device, mesh=mesh, in_specs=in_specs, out_specs=out_specs, check_vma=False
    )
```

```python
import jax
import jax.numpy as jnp
from jax import lax
from jax.experimental import pallas as pl
from jax.experimental.pallas import tpu as pltpu
from jax.sharding import PartitionSpec as P

MESH = pl.DeviceIdType.MESH
f32, bf16 = jnp.float32, jnp.bfloat16
STEP, RATE = 0.12, 0.5
ROWS = 96
GROUPS = ROWS // 4
OFFSETS = ((2, 1), (1, 1), (3, 1), (2, 0), (0, 1), (1, 0), (3, 0))
VMEM_ALL = 64 << 20


def signal_all(peers):
    barrier = pltpu.get_barrier_semaphore()
    for peer in peers:
        pl.semaphore_signal(barrier, inc=1, device_id=peer, device_id_type=MESH)
    pl.semaphore_wait(barrier, len(peers))


def remote(src, dst, send, recv, peer):
    return pltpu.make_async_remote_copy(
        src_ref=src, dst_ref=dst, send_sem=send, recv_sem=recv, device_id=peer, device_id_type=MESH
    )


def main_kernel(
    field, conduct, nonlin, counts, desc, code, w_in, bias, w_out, decoder,
    final, part, loss,
    nl, cnt, hid, fs, cd, u, cb, rs, rr, xs, xr, fx, ks, ac, snap, tr, dl, raw, tf, gram, acc,
    loc_sem, raw_sem, row_send, row_recv, col_send, col_recv, dec_send, dec_recv, own_sem, fwd_send, fwd_recv,
):
    core, row, col = (lax.axis_index(n) for n in ("run", "row", "col"))
    y, zh = col // 2, col % 2
    sibling = (1 - core, row, col)
    down, up = (core, (row + 1) % 8, col), (core, (row + 7) % 8, col)
    right, left = (core, row, (col + 1) % 8), (core, row, (col + 7) % 8)
    targets = [((y + dy) % 4) * 2 + (zh + dz) % 2 for dy, dz in OFFSETS]
    signal_all([(core, q // 8, q % 8) for q in [(row * 8 + col + j) % 64 for j in range(1, 64)]] + [sibling])

    fs3 = fs.reshape(48, 64, 128)
    rows_of_conduct = [conduct.at[pl.ds(56, 8), :], conduct.at[pl.ds(0, 8), :]]

    def row_copies(way):
        peer = (down, up)[way]
        return [
            remote(rs.at[way], rr.at[way], row_send.at[way], row_recv.at[way], peer),
            remote(
                rows_of_conduct[way], cd.at[pl.ds(72 * way, 8), :], row_send.at[2 + way], row_recv.at[2 + way], peer
            ),
        ]

    may_send = [row < 7, row > 0]
    may_get = [row > 0, row < 7]

    def each_row_copy(allowed, act):
        for way in range(2):

            @pl.when(allowed[way])
            def _():
                for c in row_copies(way):
                    act(c)

    loc_copies = [
        pltpu.make_async_copy(field, fs3, loc_sem.at[0]),
        pltpu.make_async_copy(conduct, cd.at[pl.ds(8, 64), :], loc_sem.at[1]),
    ]

    def raw_copy(part_at, slot):
        start = pl.multiple_of(part_at * 1024, 1024)
        return pltpu.make_async_copy(decoder.at[pl.ds(start, 1024), :], raw.at[slot], raw_sem.at[slot])

    mine, other = 2 * core, 2 * (1 - core)

    def turn(quarter, slot):
        def piece(hb, carry):
            at = pl.multiple_of(hb * 256, 256)
            to = pl.multiple_of(quarter * 128 + hb * 32, 32)
            for t in range(8):
                tf[t] = raw[slot, pl.ds(at, 256), t * 128 : (t + 1) * 128].astype(f32)
            for t in range(8):
                for i in range(8):
                    tr[t, i, pl.ds(to, 32), :] = tf[t, pl.ds(i, 32, stride=8), :].astype(bf16)
            return carry

        lax.fori_loop(0, 4, piece, 0)

    def dec_copies(hh, kk):
        h0 = pl.multiple_of((mine + hh) * 128, 128)
        rnd = hh * 4 + kk
        out = []
        for j, t in enumerate(targets):
            out.append(
                remote(
                    tr.at[t, pl.ds(2 * kk, 2), pl.ds(h0, 128), :],
                    dl.at[kk, pl.ds(2 * col, 2), pl.ds(h0, 128), :],
                    dec_send.at[rnd, j], dec_recv.at[rnd, j], (core, row, t),
                )
            )
        return out

    def own_copy(hh, kk):
        h0 = pl.multiple_of((mine + hh) * 128, 128)
        return pltpu.make_async_copy(
            tr.at[col, pl.ds(2 * kk, 2), pl.ds(h0, 128), :],
            dl.at[kk, pl.ds(2 * col, 2), pl.ds(h0, 128), :],
            own_sem.at[hh * 4 + kk],
        )

    def fwd_copy(hh, kk):
        h0 = pl.multiple_of((mine + hh) * 128, 128)
        block = dl.at[kk, :, pl.ds(h0, 128), :]
        return remote(block, block, fwd_send.at[hh * 4 + kk], fwd_recv.at[hh * 4 + kk], sibling)

    def send_round(hh, kk):
        for c in dec_copies(hh, kk):
            c.start()
        own_copy(hh, kk).start()

    def pass_round(hh, kk):
        for c in dec_copies(hh, kk):
            c.wait_recv()
        own_copy(hh, kk).wait()
        fwd_copy(hh, kk).start()

    for c in loc_copies:
        c.start()
    raw_copy(mine, 0).start()
    raw_copy(mine + 1, 1).start()
    for c in loc_copies:
        c.wait()

    def pack_rows(i, carry):
        for b in range(3):
            for way in range(2):
                rs[way, i, b] = fs[pl.ds(b * 1024 + i + 56 * (1 - way), 16, stride=64), :].astype(bf16)
        return carry

    lax.fori_loop(0, 8, pack_rows, 0)
    each_row_copy(may_send, lambda c: c.start())
    raw_copy(mine, 0).wait()
    turn(mine, 0)
    raw_copy(other, 0).start()
    send_round(0, 0)

    for b in range(3):
        u[b, 0:8] = jnp.zeros((8, 2, 8, 128), f32)
        u[b, 88:96] = jnp.zeros((8, 2, 8, 128), f32)

    def fill(n, carry):
        for q in range(4):
            i = 4 * n + q
            for b in range(3):
                u[b, i + 16] = fs[pl.ds(b * 1024 + i, 16, stride=64), :].reshape(2, 8, 128)
        return carry

    lax.fori_loop(0, 16, fill, 0)

    each_row_copy(may_get, lambda c: c.wait_recv())

    def unpack_rows(i, carry):
        for b in range(3):
            for way in range(2):
                u[b, i + 8 + 72 * way] = rr[way, i, b].astype(f32).reshape(2, 8, 128)
        return carry

    lax.fori_loop(0, 8, unpack_rows, 0)

    def fill_conduct(n, carry):
        for q in range(4):
            i = 4 * n + q
            cb[0, i + 8] = jnp.broadcast_to(cd[pl.ds(i, 1), :] * (0.5 * STEP), (8, 128))
        return carry

    lax.fori_loop(0, 20, fill_conduct, 0)
    for s in range(4):
        cb[s, 0:8] = jnp.zeros((8, 8, 128), f32)
        cb[s, 88:96] = jnp.zeros((8, 8, 128), f32)

    def clear(b):
        @pl.when(row == 0)
        def _():
            u[b, 8:16] = jnp.zeros((8, 2, 8, 128), f32)

        @pl.when(row == 7)
        def _():
            u[b, 80:88] = jnp.zeros((8, 2, 8, 128), f32)

    for b in range(3):
        clear(b)

    @pl.when(row == 0)
    def _():
        cb[0, 8:16] = jnp.zeros((8, 8, 128), f32)

    @pl.when(row == 7)
    def _():
        cb[0, 80:88] = jnp.zeros((8, 8, 128), f32)

    lane = lax.broadcasted_iota(jnp.int32, (2, 8, 128), 2)
    in32 = lane % 32

    def gather_edges(i):
        out = None
        for b in range(4):
            v = u[b, i] if b < 3 else jnp.broadcast_to(cb[0, i][None], (2, 8, 128))
            ends = pltpu.roll(v, (32 * b + 8) % 128, 2)
            starts = pltpu.roll(v, (32 * b + 24) % 128, 2)
            both = jnp.where(in32 < 8, ends, starts)
            out = both if b == 0 else jnp.where(lane // 32 == b, both, out)
        return out

    def pack(g, carry):
        to_right = to_left = None
        for q in range(4):
            o = gather_edges(4 * g + q)
            u[3, 4 * g + q] = o
            r = pltpu.roll(o, 8 * q, 2) if q else o
            l = pltpu.roll(o, (8 * q + 8) % 32 + 96 if q < 3 else 0, 2) if q < 3 else pltpu.roll(o, 0, 2)
            here = in32 // 8 == q
            to_right = r if q == 0 else jnp.where(here, r, to_right)
            to_left = l if q == 0 else jnp.where(here, l, to_left)
        xs[0, g] = to_right.reshape(16, 128).astype(bf16)
        xs[1, g] = to_left.reshape(16, 128).astype(bf16)
        return carry

    lax.fori_loop(2, GROUPS - 2, pack, 0)
    col_copies = [
        remote(xs.at[0, pl.ds(2, 20)], xr.at[0, pl.ds(2, 20)], col_send.at[0], col_recv.at[0], right),
        remote(xs.at[1, pl.ds(2, 20)], xr.at[1, pl.ds(2, 20)], col_send.at[1], col_recv.at[1], left),
    ]
    for c in col_copies:
        c.start()
    raw_copy(mine + 1, 1).wait()
    turn(mine + 1, 1)
    raw_copy(other + 1, 1).start()
    for rnd in range(1, 8):
        send_round(rnd // 4, rnd % 4)
    raw_copy(other, 0).wait()
    turn(other, 0)
    raw_copy(other + 1, 1).wait()
    turn(other + 1, 1)

    wide = desc[pl.ds(pl.multiple_of(core * 48, 16), 48), :].astype(f32)
    for s in range(8):
        rows_s = (wide + code[s : s + 1, :].astype(f32)).astype(bf16)
        act_s = jax.nn.gelu(jnp.dot(rows_s, w_in[...], preferred_element_type=f32) + bias[...]).astype(bf16)
        hid[48 * s : 48 * s + 48, :] = jnp.dot(act_s, w_out[...], preferred_element_type=f32).astype(bf16)

    gram[...] = jnp.zeros((512, 512), f32)
    nt = (((1,), (1,)), ((), ()))

    def add_gram(t, carry):
        x = jnp.concatenate([tr[t, i] for i in range(8)], axis=1)
        gram[0:256] += lax.dot_general(x[0:256], x, nt, preferred_element_type=f32)
        gram[256:512, 256:512] += lax.dot_general(x[256:512], x[256:512], nt, preferred_element_type=f32)
        return carry

    lax.fori_loop(0, 8, add_gram, 0)
    gram[256:512, 0:256] = gram[0:256, 256:512].T
    big = gram[...].astype(bf16)
    small = (gram[...] - big.astype(f32)).astype(bf16)
    product = jnp.dot(hid[...], big, preferred_element_type=f32) + jnp.dot(
        hid[...], small, preferred_element_type=f32
    )
    for t in range(4):
        part[t] = product[:, 128 * t : 128 * t + 128]

    for c in col_copies:
        c.wait_recv()

    place_of = lax.broadcasted_iota(jnp.int32, (2, 8, 128), 0) * 8 + lax.broadcasted_iota(jnp.int32, (2, 8, 128), 1)

    def of_runs(ref, b):
        out = jnp.zeros((2, 8, 128), f32)
        for i in range(16):
            out = jnp.where(place_of == i, ref[16 * b + i].astype(f32), out)
        return out

    def lanes_of_runs(made):
        out = jnp.zeros((2, 8, 128), f32)
        for b in range(3):
            out = jnp.where(lane // 32 == b, made[b], out)
        return out

    for b in range(3):
        nl[b] = of_runs(nonlin, b)
        cnt[b] = of_runs(counts, b)
    nl[3] = lanes_of_runs(nl)

    u[3, 0:8] = jnp.zeros((8, 2, 8, 128), f32)
    u[3, 88:96] = jnp.zeros((8, 2, 8, 128), f32)
    from_left = (in32 >= 16) & (in32 < 24)
    from_right = (in32 >= 8) & (in32 < 16)
    left_ok = (jnp.zeros((2, 8, 128), jnp.int32) + col) > 0
    right_ok = (jnp.zeros((2, 8, 128), jnp.int32) + col) < 7

    taken = jnp.where(from_left & jnp.logical_not(left_ok), 0.0, lanes_of_runs(cnt))
    cnt[3] = jnp.where(from_right & jnp.logical_not(right_ok), 0.0, taken)

    def unpack(g, carry):
        gl = xr[0, g].astype(f32).reshape(2, 8, 128)
        gr = xr[1, g].astype(f32).reshape(2, 8, 128)
        for q in range(4):
            o = u[3, 4 * g + q]
            a = pltpu.roll(gl, (16 - 8 * q) % 128, 2)
            c = pltpu.roll(gr, (8 - 8 * q) % 128, 2)
            o = jnp.where(from_left, jnp.where(left_ok, a, 0.0), o)
            o = jnp.where(from_right, jnp.where(right_ok, c, 0.0), o)
            u[3, 4 * g + q] = o
            k = o[0]
            for b in range(3):
                k = jnp.where(lane[0] // 32 == b, pltpu.roll(o[0], 32 * (b + 1), 1), k)
            cb[2, 4 * g + q] = jnp.where(lane[0] < 96, k, 0.0)
        return carry

    lax.fori_loop(2, GROUPS - 2, unpack, 0)
    clear(3)

    @pl.when(row == 0)
    def _():
        cb[2, 8:16] = jnp.zeros((8, 8, 128), f32)

    @pl.when(row == 7)
    def _():
        cb[2, 80:88] = jnp.zeros((8, 8, 128), f32)

    def shift_conduct(g, carry):
        for q in range(4):
            for side in (0, 2):
                cb[side + 1, 4 * g + q] = pltpu.roll(cb[side, 4 * g + q], 127, 1)
        return carry

    lax.fori_loop(2, GROUPS - 2, shift_conduct, 0)
    first, last = lane == 0, lane == 127

    def run_step(s, with_main):
        blocks = (0, 1, 2, 3) if with_main else (3,)
        count = range(len(blocks))
        ahead_s = s + 1 if with_main else s
        coef = [nl[b] for b in blocks]
        active = [jnp.where(cnt[b] > (s if b < 3 else ahead_s).astype(f32), 1.0, 0.0) for b in blocks]
        begin = (9 + s) // 4

        def kappa(v, i, n, shifted=0):
            return cb[(2 if blocks[n] == 3 else 0) + shifted, i][None] / (1.0 + coef[n] * v * v)

        def ahead(i, vs):
            out = []
            for n, b in enumerate(blocks):
                v = vs[n]
                k = kappa(v, i, n)
                vr = pltpu.roll(v, 127, 2)
                across = (k + kappa(vr, i, n, 1)) * (vr - v)
                if b < 3:
                    across = jnp.where(last, fx[b, s % 2, i], across)
                out.append((k, across))
            return out

        def keep(g, q, made):
            for n, (k, across) in enumerate(made):
                ks[blocks[n], (g % 2) * 4 + q] = k
                ac[blocks[n], (g % 2) * 4 + q] = across

        flows = []
        for q in range(4):
            vs = [u[b, 4 * begin + q] for b in blocks]
            made = ahead(4 * begin + q, vs)
            keep(begin, q, made)
            if q == 0:
                for n, b in enumerate(blocks):
                    before = u[b, 4 * begin - 1]
                    flows.append((made[n][0] + kappa(before, 4 * begin - 1, n)) * (vs[n] - before))

        def group(g, flow):
            flow = list(flow)
            base, now = 4 * g, (g % 2) * 4
            v = [[u[b, base + q] for b in blocks] for q in range(4)]
            k = [[ks[b, now + q] for b in blocks] for q in range(4)]
            a = [[ac[b, now + q] for b in blocks] for q in range(4)]
            v_next = [[u[b, base + 4 + q] for b in blocks] for q in range(4)]
            first_made = None
            for q in range(4):
                made = ahead(base + 4 + q, v_next[q])
                first_made = made if q == 0 else first_made
                for n, b in enumerate(blocks):
                    vn = v[q + 1][n] if q < 3 else v_next[0][n]
                    kn = k[q + 1][n] if q < 3 else first_made[n][0]
                    flow_n = (k[q][n] + kn) * (vn - v[q][n])
                    came = pltpu.roll(a[q][n], 1, 2)
                    if b == 3:
                        f = jnp.where(in32 == 8, pltpu.roll(a[q][n], 113, 2), a[q][n])
                        for to in range(3):
                            fx[to, ahead_s % 2, base + q] = pltpu.roll(f, 120 - 32 * to, 2)
                    else:
                        came = jnp.where(first, fx[b, s % 2, base + q], came)
                    new = v[q][n] + active[n] * ((flow_n - flow[n]) + (a[q][n] - came))
                    u[b, base + q] = new
                    if b < 3:
                        snap[2 * (g % 2) + q // 2, 2 * (g // 2) - 2 + q % 2, s, 16 * b : 16 * b + 16, :] = (
                            new.reshape(16, 128).astype(bf16)
                        )
                    flow[n] = flow_n
                keep(g + 1, q, made)
            return tuple(flow)

        lax.fori_loop(begin, GROUPS - begin, group, tuple(flows))
        for b in blocks:
            clear(b)

    pass_round(0, 0)
    run_step(jnp.int32(0), False)

    def one_step(s, carry):
        run_step(s, True)
        for at, hh, kk in ((0, 0, 1), (1, 0, 2), (3, 0, 3), (4, 1, 0), (5, 1, 1), (6, 1, 2)):

            @pl.when(s == at)
            def _():
                pass_round(hh, kk)

        return carry

    lax.fori_loop(0, 8, one_step, 0)

    pass_round(1, 3)

    def give_back(n, carry):
        for q in range(4):
            for b in range(3):
                fs[pl.ds(b * 1024 + 4 * n + q, 16, stride=64), :] = u[b, 4 * n + q + 16].reshape(16, 128)
        return carry

    lax.fori_loop(0, 16, give_back, 0)
    out_copy = pltpu.make_async_copy(fs3, final, loc_sem.at[2])
    out_copy.start()

    def square(n, total):
        x = snap[n // 16, 2 + n % 16].astype(f32).reshape(48, 8, 128)
        return total + jnp.sum(x * x, axis=0)

    squares = lax.fori_loop(0, 64, square, jnp.zeros((8, 128), f32))

    for hh in range(2):
        for kk in range(4):
            fwd_copy(hh, kk).wait_recv()

            lhs = jnp.concatenate([snap[kk, 2 + i].reshape(384, 128) for i in range(16)], axis=1)
            rhs = jnp.concatenate(
                [
                    jnp.concatenate(
                        [
                            dl[kk, i, 128 * hh : 128 * hh + 128, :],
                            dl[kk, i, 256 + 128 * hh : 384 + 128 * hh, :],
                        ],
                        axis=0,
                    )
                    for i in range(16)
                ],
                axis=1,
            )
            got = lax.dot_general(lhs, rhs, nt, preferred_element_type=f32)
            acc[hh] = got if kk == 0 else acc[hh] + got

    total = squares
    for hh in range(2):
        for half in range(2):
            at = slice(256 * half + 128 * hh, 256 * half + 128 * hh + 128)
            a = part[2 * half + hh]
            c = acc[hh, :, 128 * half : 128 * half + 128]
            part[2 * half + hh] = a - c
            total = total + jnp.sum((hid[:, at].astype(f32) * (a - 2.0 * c)).reshape(48, 8, 128), axis=0)
    loss[...] = total

    out_copy.wait()
    each_row_copy(may_send, lambda c: c.wait_send())
    for c in col_copies:
        c.wait_send()
    for hh in range(2):
        for kk in range(4):
            for c in dec_copies(hh, kk):
                c.wait_send()
            fwd_copy(hh, kk).wait_send()


def reduce_kernel(
    part, loss_in, desc, code, w_in, bias, w_out,
    new_in, new_bias, new_out, loss_out,
    code_wide, rows, act, slope, grad, back, r1, l1, l2, got, send1, recv1, send2, recv2, lsend, lrecv, lsend2, xsend, xrecv,
):
    core, row, col = (lax.axis_index(n) for n in ("run", "row", "col"))
    x, y, z = row % 4, col // 2, (col % 2) * 2 + row // 4
    sibling = (1 - core, row, col)
    me = row * 8 + col

    def chip(j):
        x1, y1, z1 = (x + j % 4) % 4, (y + j // 4 % 4) % 4, (z + j // 16) % 4
        return (z1 % 2) * 4 + x1, y1 * 2 + z1 // 2

    offsets = list(range(1, 64))
    offsets.sort(key=lambda j: -sum(min(d, 4 - d) for d in (j % 4, j // 4 % 4, j // 16)))
    peers = [(core, *chip(j)) for j in offsets]

    def piece(p):
        return part.at[p // 16, pl.ds(pl.multiple_of(24 * (p % 16), 8), 24), :]

    first = []
    for n, j in enumerate(offsets):
        r, c = chip(j)
        first.append(remote(piece(r * 8 + c), r1.at[n], send1.at[n], recv1.at[n], peers[n]))
    to_zero = remote(loss_in, l1.at[me], lsend, lrecv.at[me], (core, 0, 0))

    @pl.when(me > 0)
    def _():
        to_zero.start()

    for c in first:
        c.start()

    code_wide[...] = code[...].astype(f32)

    def trunk(n, carry):
        at = pl.multiple_of(48 * n, 48)
        half = pl.multiple_of(48 * (n // 8), 48)
        rows_n = (desc[pl.ds(half, 48), :].astype(f32) + code_wide[pl.ds(n % 8, 1), :]).astype(bf16)
        pre = jnp.dot(rows_n, w_in[...], preferred_element_type=f32) + bias[...]
        value, pull = jax.vjp(jax.nn.gelu, pre)
        rows[pl.ds(at, 48), :] = rows_n
        act[pl.ds(at, 48), :] = value.astype(bf16)
        slope[pl.ds(at, 48), :] = pull(jnp.ones_like(pre))[0]
        return carry

    lax.fori_loop(0, 16, trunk, 0)
    total = part[me // 16, pl.ds(pl.multiple_of(24 * (me % 16), 8), 24), :]
    for n, c in enumerate(first):
        c.wait_recv()
        total = total + r1[n]
    got[core, me] = jnp.concatenate([total * (1.0 / 768.0), jnp.zeros((8, 128), f32)], axis=0).astype(bf16)

    second = [remote(got.at[core, me], got.at[core, me], send2.at[n], recv2.at[n], peers[n]) for n in range(63)]
    for c in second:
        c.start()
    spread_loss = [remote(l2.at[core], l2.at[core], lsend2.at[n], lrecv.at[64], peers[n]) for n in range(63)]

    @pl.when(me == 0)
    def _():
        sums = loss_in[...]
        for p in range(1, 64):
            remote(loss_in, l1.at[p], lsend, lrecv.at[p], (core, 0, 0)).wait_recv()
            sums = sums + l1[p]
        l2[core] = sums
        for c in spread_loss:
            c.start()

    for c in second:
        c.wait_recv()
    cross = remote(got.at[core], got.at[core], xsend.at[0], xrecv.at[0], sibling)
    cross.start()

    @pl.when(me > 0)
    def _():
        spread_loss[0].wait_recv()

    cross_loss = remote(l2.at[core], l2.at[core], xsend.at[1], xrecv.at[1], sibling)
    cross_loss.start()

    def place(own):
        for t in range(4):
            for q in range(8):
                pair = jnp.concatenate(
                    [got[own, 16 * t + 2 * q + i].astype(f32)[0:24] for i in range(2)], axis=0
                ).astype(bf16)
                grad[pl.ds(pl.multiple_of(384 * own + 48 * q, 48), 48), 128 * t : 128 * t + 128] = pair

    place(core)
    cross.wait_recv()
    place(1 - core)
    tn = (((0,), (0,)), ((), ()))
    new_out[...] = w_out[...].astype(f32) - RATE * lax.dot_general(
        act[...], grad[...], tn, preferred_element_type=f32
    )
    back[...] = (
        lax.dot_general(grad[...], w_out[...], (((1,), (1,)), ((), ())), preferred_element_type=f32) * slope[...]
    )
    new_bias[...] = bias[...] - RATE * jnp.sum(back[...], axis=0, keepdims=True)
    new_in[...] = w_in[...].astype(f32) - RATE * lax.dot_general(
        rows[...], back[...].astype(bf16), tn, preferred_element_type=f32
    )
    cross_loss.wait_recv()
    loss_out[...] = jnp.sum(l2[0] + l2[1], keepdims=True) * (1.0 / (768 * 512 * 1024))

    @pl.when(me > 0)
    def _():
        to_zero.wait_send()

    @pl.when(me == 0)
    def _():
        for c in spread_loss:
            c.wait_send()

    for c in first + second + [cross, cross_loss]:
        c.wait_send()


def per_device(
    init_field, conduct, nonlin, counts, descriptors, time_code, w_in, bias_in, w_out, decoder
):
    bias_row = bias_in.reshape(1, 512)
    vmem = pl.BlockSpec(memory_space=pltpu.VMEM)
    hbm = pl.BlockSpec(memory_space=pl.ANY)
    dma = pltpu.SemaphoreType.DMA
    first = [
        pltpu.VMEM((4, 2, 8, 128), f32),
        pltpu.VMEM((4, 2, 8, 128), f32),
        pltpu.VMEM((384, 512), bf16),
        pltpu.VMEM((3072, 128), f32),
        pltpu.VMEM((80, 128), f32),
        pltpu.VMEM((4, ROWS, 2, 8, 128), f32),
        pltpu.VMEM((4, ROWS, 8, 128), f32),
        pltpu.VMEM((2, 8, 3, 16, 128), bf16),
        pltpu.VMEM((2, 8, 3, 16, 128), bf16),
        pltpu.VMEM((2, GROUPS, 16, 128), bf16),
        pltpu.VMEM((2, GROUPS, 16, 128), bf16),
        pltpu.VMEM((3, 2, ROWS, 2, 8, 128), f32),
        pltpu.VMEM((4, 8, 2, 8, 128), f32),
        pltpu.VMEM((4, 8, 2, 8, 128), f32),
        pltpu.VMEM((4, 20, 8, 48, 128), bf16),
        pltpu.VMEM((8, 8, 512, 128), bf16),
        pltpu.VMEM((4, 16, 512, 128), bf16),
        pltpu.VMEM((2, 1024, 1024), bf16),
        pltpu.VMEM((8, 256, 128), f32),
        pltpu.VMEM((512, 512), f32),
        pltpu.VMEM((2, 384, 256), f32),
        dma((3,)), dma((2,)), dma((4,)), dma((4,)), dma((2,)), dma((2,)),
        dma((8, 7)), dma((8, 7)), dma((8,)), dma((8,)), dma((8,)),
    ]
    second = [
        pltpu.VMEM((8, 256), f32),
        pltpu.VMEM((768, 256), bf16),
        pltpu.VMEM((768, 512), bf16),
        pltpu.VMEM((768, 512), f32),
        pltpu.VMEM((768, 512), bf16),
        pltpu.VMEM((768, 512), f32),
        pltpu.VMEM((63, 24, 128), f32),
        pltpu.VMEM((64, 8, 128), f32),
        pltpu.VMEM((2, 8, 128), f32),
        pltpu.VMEM((2, 64, 32, 128), bf16),
        dma((63,)), dma((63,)), dma((63,)), dma((63,)), dma(()), dma((65,)), dma((63,)), dma((2,)), dma((2,)),
    ]
    part_and_loss = [pltpu.VMEM((4, 384, 128), f32), pltpu.VMEM((8, 128), f32)]

    def whole_kernel(field, cond, nonlin, counts, desc, code, w_in, bias, w_out, dec, final, new_in, new_bias, new_out, total, part, loss, *rest):
        main_kernel(field, cond, nonlin, counts, desc, code, w_in, bias, w_out, dec, final, part, loss, *rest[: len(first)])
        reduce_kernel(
            part, loss, desc, code, w_in, bias, w_out, new_in, new_bias, new_out, total, *rest[len(first) :]
        )

    final, new_w_in, new_bias, new_w_out, loss_sum = pl.pallas_call(
        whole_kernel,
        name="solve_and_learn",
        out_shape=(
            jax.ShapeDtypeStruct((48, 64, 128), f32),
            jax.ShapeDtypeStruct((256, 512), f32),
            jax.ShapeDtypeStruct((1, 512), f32),
            jax.ShapeDtypeStruct((512, 512), f32),
            jax.ShapeDtypeStruct((1, 1), f32),
        ),
        in_specs=[hbm, hbm] + [pl.BlockSpec(memory_space=pltpu.SMEM)] * 2 + [vmem] * 5 + [hbm],
        out_specs=(hbm, vmem, vmem, vmem, vmem),
        scratch_shapes=part_and_loss + first + second,
        compiler_params=pltpu.CompilerParams(
            collective_id=0, has_side_effects=True, vmem_limit_bytes=VMEM_ALL - (1 << 16)
        ),
    )(
        init_field, conduct, nonlin, counts,
        descriptors, time_code, w_in, bias_row, w_out, decoder.reshape(4096, 1024),
    )
    mean_loss = loss_sum.reshape(())
    return final, new_w_in, new_bias.reshape(512), new_w_out, mean_loss


def solution(mesh):
    in_specs = (
        P("run", "row", "col"), P("row", "col"), P("run"), P("run"), P(), P(), P(), P(), P(),
        P(None, ("row", "col"), None),
    )
    out_specs = (P("run", "row", "col"), P(), P(), P(), P())
    return jax.shard_map(
        per_device, mesh=mesh, in_specs=in_specs, out_specs=out_specs, check_vma=False
    )
```
